32 devices in a mesh: rep: 8 (over y, x, core), shard: 4 (over z).
Axes of the slice: x: 2, y: 2, z: 4, core: 2. Of those that a mesh axis runs over, the one named last changes fastest.
Arguments:
- tokens: bfloat16 [32, 512, 512], P(('rep', 'shard')), may hold values from -6 to 6
- segments: int32 [32, 512], P(('rep', 'shard')), may hold values from 0 to 7, never falling along the last dimension, each value on 1 to 256 neighbouring positions
- choices: int32 [32, 512, 2], P(('rep', 'shard')), may hold values from 0 to 7, all different within a row
- priority: int32 [32, 512], P(('rep', 'shard')), may hold values from 0 to 511, each once within a row
- cotangent: bfloat16 [32, 512, 512], P(('rep', 'shard')), may hold values from -6 to 6
- qkv_weights: bfloat16 [3, 512, 512], P(None, 'shard'), may hold values from -0.25 to 0.25
- out_weight: bfloat16 [512, 512], P('shard'), may hold values from -1.5 to 1.5
- router_weight: bfloat16 [512, 8], P('shard'), may hold values from -0.1875 to 0.1875
- gains: bfloat16 [2, 512], P(None, 'shard'), may hold values from 0.25 to 1.75
- w_in: bfloat16 [8, 512, 2048], P('shard'), may hold values from -0.25 to 0.25
- w_out: bfloat16 [8, 512, 2048], P('shard'), may hold values from -1 to 1
Outputs:
- result: bfloat16 [32, 512, 512], P(('rep', 'shard'))
- grad_tokens: bfloat16 [32, 512, 512], P(('rep', 'shard'))
- grad_qkv: float32 [3, 512, 512], P(None, 'shard')
- grad_out_weight: float32 [512, 512], P('shard')
- grad_router: float32 [512, 8], P('shard')
- grad_gains: float32 [2, 512], P(None, 'shard')
- grad_w_in: float32 [8, 512, 2048], P('shard')
- grad_w_out: float32 [8, 512, 2048], P('shard')
The draws below stay inside these ranges and needn't reach their ends.
All inputs are finite; a program needn't handle non-finite values.
Results may differ from the reference program's by a relative error of at most 0.019.
Values may be sent and summed in bfloat16 or wider, within the bound.
No kernel may reach another device: no remote copies, remote signals or barrier semaphores. Data moves between devices by JAX's collectives and lax.ppermute only.
A program may use at most 256 MiB of HBM per device.

```python
import math
import jax
import jax.numpy as jnp
import numpy as np
from jax import lax

D = 512
HEADS = 8
HEAD_DIM = 64
FF = 2048
EXPERTS = 8
TOK_DEV = 512
CAPACITY = 135
GROUPS = 32


def shard_levels(stream_key, dims, cuts, low, high):
    loudness, own = 1.0, jax.random.fold_in(stream_key, 6)
    for position, shards_of in cuts:
        steps = jnp.exp(jax.random.uniform(jax.random.fold_in(own, position), (shards_of,), jnp.float32, low / len(cuts), high / len(cuts)))
        loudness = loudness * jnp.repeat(steps, dims[position] // shards_of).reshape([-1 if axis == position else 1 for axis in range(len(dims))])
    return loudness


def picks_of(own_key, rows, count, top, lift):
    sequence = jax.random.permutation(jax.random.fold_in(own_key, 1), count)
    boost = sequence
    for power in range(3):
        boost = boost * boost // count
    boost = boost * lift // count
    lots = jax.random.randint(jax.random.fold_in(own_key, 2), (rows, count), 0, 4096) + boost
    holders = jax.random.permutation(jax.random.fold_in(own_key, 3), rows)[jnp.arange(count) % rows]
    lots = jnp.where(jnp.arange(rows)[:, None] == holders[None, :], 1 << 14, lots)
    merit = lots * count + jnp.arange(count)
    return lax.top_k(merit.astype(jnp.int32), top)[1].astype(jnp.int32)


def split_up(amount, total, limit, lean):
    weights = [(1 << 20) // math.isqrt(standing ** lean) + 1 for standing in range(2, amount + 1)]
    spare, given = total - limit - (amount - 1), [1] * (amount - 1)
    while spare > 0:
        candidates = [i for i in range(amount - 1) if given[i] < limit]
        whole, remaining = sum([weights[i] for i in candidates]), spare
        for i in candidates:
            more = min(limit - given[i], max(1, remaining * weights[i] // whole), spare)
            given[i] = given[i] + more
            spare = spare - more
    return np.array([limit] + given)


def uneven_parts(stream_key, number_of, total, most, slope):
    if number_of == 2:
        one = jax.random.randint(stream_key, (), max(1, total - most), min(most, total - 1) + 1)
        return jnp.stack([one, total - one])
    sizes = jnp.asarray(split_up(number_of, total, most, slope), jnp.int32)
    twos = (number_of - 1) // 2
    donor, taker = sizes[1:1 + 2 * twos:2], sizes[2:2 + 2 * twos:2]
    slack = jnp.minimum(donor - 1, most - taker)
    moved = jax.random.randint(jax.random.fold_in(stream_key, 1), (twos,), 0, 1 << 20) % (slack + 1)
    sizes = sizes.at[1:1 + 2 * twos:2].set(donor - moved).at[2:2 + 2 * twos:2].set(taker + moved)
    return sizes[jax.random.permutation(jax.random.fold_in(stream_key, 2), number_of)]


def normal_values(rng, dims, spread, most, cuts=(), kind=jnp.bfloat16):
    array = spread * jax.random.normal(rng, dims, jnp.float32)
    if cuts:
        array = array * shard_levels(rng, dims, cuts, -0.22, 0.18)
    return jnp.clip(array, -most, most).astype(kind)


def setup_inputs(seed: int = 0) -> dict:
    key_of = jax.random.split(jax.random.key(seed), 12)
    return {
        "tokens": normal_values(key_of[0], (GROUPS, TOK_DEV, D), 1.0, 6.0, ((0, 32),)),
        "segments": jax.vmap(lambda own: jnp.searchsorted(jnp.cumsum(uneven_parts(own, 8, TOK_DEV, TOK_DEV // 2, 2)), jnp.arange(TOK_DEV), side="right"))(jax.random.split(key_of[1], GROUPS)).reshape((GROUPS, TOK_DEV)).astype(jnp.int32),
        "choices": picks_of(key_of[2], GROUPS * TOK_DEV, EXPERTS, 2, 2048).reshape((GROUPS, TOK_DEV, 2)),
        "priority": jax.vmap(lambda own: jax.random.permutation(own, TOK_DEV))(jax.random.split(key_of[3], GROUPS)).reshape((GROUPS, TOK_DEV)).astype(jnp.int32),
        "cotangent": normal_values(key_of[4], (GROUPS, TOK_DEV, D), 1.0, 6.0, ((0, 32),)),
        "qkv_weights": normal_values(key_of[5], (3, D, D), D ** -0.5, 0.25, ((1, 4),)),
        "out_weight": normal_values(key_of[6], (D, D), 0.265, 1.5, ((0, 4),)),
        "router_weight": normal_values(key_of[7], (D, EXPERTS), 0.03, 0.1875, ((0, 4),)),
        "gains": jnp.clip(1.0 + 0.15 * jax.random.normal(key_of[8], (2, D), jnp.float32), 0.25, 1.75).astype(jnp.bfloat16),
        "w_in": normal_values(key_of[9], (EXPERTS, D, FF), D ** -0.5, 0.25, ((0, 4),)),
        "w_out": normal_values(key_of[10], (EXPERTS, D, FF), 0.17, 1.0, ((0, 4),)),
    }


@jax.custom_vjp
def low(v):
    return lax.optimization_barrier(v.astype(jnp.bfloat16)).astype(jnp.float32)

@jax.custom_vjp
def low_back(v):
    return v

def low_keep(v):
    return (low(v), None)

def low_pass(kept, grad):
    return (grad,)

def back_keep(v):
    return (v, None)

def back_low(kept, grad):
    return (low(grad),)
low.defvjp(low_keep, low_pass)
low_back.defvjp(back_keep, back_low)
exact_mode = lax.Precision.HIGHEST

def gelu_tanh(values):
    return jax.nn.gelu(values, approximate=True)

def layer_norm(values, gain_row):
    row_mean = lax.optimization_barrier(jnp.mean(values, axis=-1, keepdims=True))
    centered = values - row_mean
    row_var = lax.optimization_barrier(jnp.mean(centered * centered, axis=-1, keepdims=True))
    return centered * lax.rsqrt(row_var + 1e-06) * gain_row

def route_slots(choice_row, priority_row):
    count_tok = choice_row.shape[0]
    expert_ids = jnp.arange(EXPERTS, dtype=jnp.int32)
    onehot = (choice_row[:, :, None] == expert_ids).astype(jnp.int32)
    order_key = (jnp.arange(2, dtype=jnp.int32)[None, :] * count_tok + priority_row[:, None]).astype(jnp.int32)
    ordered = jnp.zeros((2 * count_tok, EXPERTS), jnp.int32).at[order_key.reshape(-1)].set(onehot.reshape(2 * count_tok, EXPERTS))
    earlier = (jnp.cumsum(ordered, axis=0, dtype=jnp.int32) - ordered).astype(jnp.int32)
    slot_pos = lax.optimization_barrier(jnp.sum(earlier[order_key] * onehot, axis=-1, dtype=jnp.int32)).astype(jnp.int32)
    valid_pair = slot_pos < CAPACITY
    flat_index = jnp.where(valid_pair, choice_row * CAPACITY + slot_pos, EXPERTS * CAPACITY).astype(jnp.int32)
    return (flat_index, valid_pair)

def group_forward(param_set, inputs, seg_row, flat_index, valid_pair, choice_row):
    qkv_full, out_full, router_full, gain_full, win_full, wout_full = param_set
    count_tok, model_width = inputs.shape
    norm_one = low(layer_norm(inputs, gain_full[0]))
    projected = low_back(low(jnp.einsum('td,sde->ste', norm_one, qkv_full, precision=exact_mode)))
    split_heads = projected.reshape(3, count_tok, HEADS, HEAD_DIM)
    scores = jnp.einsum('qhc,khc->hqk', split_heads[0], split_heads[1], precision=exact_mode) * HEAD_DIM ** (-0.5)
    scores = low_back(scores)
    same_doc = (seg_row[:, None] == seg_row[None, :])[None]
    scores = jnp.where(same_doc, scores, -1e+30)
    row_top = lax.optimization_barrier(jnp.max(scores, axis=-1, keepdims=True))
    exp_terms = jnp.exp(scores - row_top)
    attn_weights = low(exp_terms / lax.optimization_barrier(jnp.sum(exp_terms, axis=-1, keepdims=True)))
    mixed_rows = jnp.einsum('hqk,khc->qhc', attn_weights, split_heads[2], precision=exact_mode).reshape(count_tok, model_width)
    mixed_rows = low_back(low(mixed_rows))
    branch = low_back(jnp.dot(mixed_rows, out_full, precision=exact_mode))
    resid_sum = inputs + branch
    norm_two = low(layer_norm(resid_sum, gain_full[1]))
    logits = low_back(jnp.dot(norm_two, router_full, precision=exact_mode))
    gate_probs = jax.nn.softmax(logits, axis=-1)
    pair_rows = jnp.broadcast_to(norm_two[:, None, :], (count_tok, 2, model_width)).reshape(2 * count_tok, model_width)
    slot_in = jnp.zeros((EXPERTS * CAPACITY, model_width), jnp.float32).at[flat_index.reshape(-1)].set(pair_rows, mode='drop')
    slot_in = low_back(slot_in).reshape(EXPERTS, CAPACITY, model_width)
    pre_act = low_back(jnp.einsum('ecd,edf->ecf', slot_in, win_full, precision=exact_mode))
    hidden = low(gelu_tanh(pre_act))
    expert_out = low_back(low(jnp.einsum('ecf,edf->ecd', hidden, wout_full, precision=exact_mode)))
    expert_out = expert_out.reshape(EXPERTS * CAPACITY, model_width)
    picked = jnp.take(expert_out, flat_index, axis=0, mode='fill', fill_value=0.0)
    gate_pair = jnp.take_along_axis(gate_probs, choice_row, axis=-1) * valid_pair.astype(jnp.float32)
    return resid_sum + lax.optimization_barrier(jnp.sum(gate_pair[:, :, None] * picked, axis=1))

def reference(tokens, segments, choices, priority, cotangent, qkv_weights, out_weight, router_weight, gains, w_in, w_out):
    flat_index, valid_pair = jax.vmap(route_slots)(choices, priority)
    param_set = tuple((weight.astype(jnp.float32) for weight in (qkv_weights, out_weight, router_weight, gains, w_in, w_out)))

    def forward(param_arg, inputs):

        def one_group(group_items):
            return jax.checkpoint(group_forward)(param_arg, group_items[0], group_items[1], group_items[2], group_items[3], group_items[4])
        return lax.map(one_group, (inputs, segments, flat_index, valid_pair, choices))
    result, pullback = jax.vjp(forward, param_set, tokens.astype(jnp.float32))
    grad_params, grad_inputs = pullback(cotangent.astype(jnp.float32))
    return (result.astype(jnp.bfloat16), grad_inputs.astype(jnp.bfloat16), grad_params[0], grad_params[1], grad_params[2], grad_params[3], grad_params[4], grad_params[5])
```

```python
import jax
import jax.numpy as jnp
from jax import lax
from jax.experimental import pallas as pl
from jax.experimental.pallas import tpu as pltpu
from jax.sharding import PartitionSpec as P

HEADS = 8
HEAD_DIM = 64
EXPERTS = 8
CAPACITY = 135
ROWS = 144
SLOTS = 136
EPS = 1e-06
F32 = jnp.float32
BF = jnp.bfloat16
AXES = ("rep", "shard")
FF_BLOCKS = 2
FF_STEP = 512
GELU_A = 0.7978845608028654
GELU_B = 0.044715


def dot_nn(a, b):
    return lax.dot_general(a, b, (((1,), (0,)), ((), ())), preferred_element_type=F32)


def dot_nt(a, b):
    return lax.dot_general(a, b, (((1,), (1,)), ((), ())), preferred_element_type=F32)


def dot_tn(a, b):
    return lax.dot_general(a, b, (((0,), (0,)), ((), ())), preferred_element_type=F32)


def iota(shape, dim):
    return lax.broadcasted_iota(jnp.int32, shape, dim)


def unit_of(values):
    mean = jnp.mean(values, axis=-1, keepdims=True)
    centered = values - mean
    inv = lax.rsqrt(jnp.mean(centered * centered, axis=-1, keepdims=True) + EPS)
    return centered * inv, inv


def split3(values):
    high = values.astype(BF)
    rest = values - high.astype(F32)
    mid = rest.astype(BF)
    low = (rest - mid.astype(F32)).astype(BF)
    return high, mid, low


def piece_rows(values):
    high, mid, low = split3(values)
    shape = (8, values.shape[1])
    row = iota(shape, 0)
    parts = [jnp.broadcast_to(part.astype(F32), shape) for part in (high, mid, low)]
    return jnp.where(
        row == 0, parts[0], jnp.where(row == 1, parts[1], jnp.where(row == 2, parts[2], 0.0))
    )


def vmem(n):
    return [pl.BlockSpec(memory_space=pltpu.VMEM)] * n


def params(mib):
    return pltpu.CompilerParams(vmem_limit_bytes=mib << 20)


def route_body(choice_ref, prio_row_ref, prio_col_ref, cot_ref, index_ref, sent_ref):
    count = cot_ref.shape[-2]
    choice = choice_ref[...]
    experts = iota((EXPERTS, count), 0)
    first = (choice[0:1, :] == experts).astype(F32)
    second = (choice[1:2, :] == experts).astype(F32)
    earlier = jnp.where(prio_col_ref[...] < prio_row_ref[...], 1.0, 0.0).astype(BF)
    slot0 = jnp.sum(first * dot_nn(first.astype(BF), earlier), axis=0, keepdims=True)
    behind = dot_nn(second.astype(BF), earlier) + jnp.sum(first, axis=1, keepdims=True)
    slot1 = jnp.sum(second * behind, axis=0, keepdims=True)
    slot = jnp.concatenate([slot0, slot1], axis=0).astype(jnp.int32)
    index = jnp.where(slot < CAPACITY, choice * ROWS + slot, -1)
    index_ref[...] = index
    cot = cot_ref[0]
    for e in range(EXPERTS):
        row = iota((ROWS, count), 0) + e * ROWS
        pick = (row == index[0:1, :]) | (row == index[1:2, :])
        sent_ref[e] = dot_nn(jnp.where(pick, 1.0, 0.0).astype(BF), cot).astype(BF)


def route(choice_t, prio_row, prio_col, cot):
    _, count, width = cot.shape
    return pl.pallas_call(
        route_body,
        out_shape=(
            jax.ShapeDtypeStruct((2, count), jnp.int32),
            jax.ShapeDtypeStruct((EXPERTS, ROWS, width), BF),
        ),
        in_specs=vmem(4),
        out_specs=tuple(vmem(2)),
        compiler_params=params(24),
        cost_estimate=pl.CostEstimate(
            flops=2 * EXPERTS * ROWS * count * width, bytes_accessed=3 << 20, transcendentals=0
        ),
        name="route",
    )(choice_t, prio_row, prio_col, cot)


def pack_body(where_ref, qkv_ref, out_ref, router_ref, gains_ref, pack_ref):
    rows = pack_ref.shape[1]
    start = pl.multiple_of(where_ref[0] * rows, rows)
    for s in range(3):
        pack_ref[s] = qkv_ref[s, pl.ds(start, rows), :]
    pack_ref[3] = out_ref[pl.ds(start, rows), :]
    depth = router_ref.shape[0]
    wide = jnp.concatenate(
        [router_ref[...].astype(F32), jnp.zeros((depth, 128 - EXPERTS), F32)], axis=1
    )
    small = jnp.concatenate(
        [wide.T[0:EXPERTS], gains_ref[...].astype(F32), jnp.zeros((6, depth), F32)], axis=0
    )
    pack_ref[4, :, 0:depth] = small.astype(BF)
    pack_ref[4, :, depth:] = jnp.zeros((rows, pack_ref.shape[2] - depth), BF)


def pack_weights(rep, qkv, out, router, gains, rows):
    width = out.shape[1]
    return pl.pallas_call(
        pack_body,
        out_shape=jax.ShapeDtypeStruct((5, rows, width), BF),
        in_specs=[pl.BlockSpec(memory_space=pltpu.SMEM)] + vmem(4),
        out_specs=vmem(1)[0],
        compiler_params=params(8),
        name="pack_weights",
    )(rep.reshape(1), qkv, out, router, gains)


def gather_weights(rep, shard, reps, shards_n, qkv, out, router, gains):
    rows = qkv.shape[1] // reps
    pack = pack_weights(rep, qkv, out, router, gains, rows)
    far = [
        lax.ppermute(pack, "shard", [(i, i ^ dz) for i in range(shards_n)])
        for dz in range(1, shards_n)
    ]
    near = jnp.stack([piece[0:4] for piece in far])
    smalls = jnp.stack([piece[4] for piece in [pack] + far])
    spread = [near] + [
        lax.ppermute(near, "rep", [(i, i ^ k) for i in range(reps)]) for k in range(2, reps, 2)
    ]
    twin = [lax.ppermute(piece, "rep", [(i, i ^ 1) for i in range(reps)]) for piece in spread]
    pieces = []
    for own, other in zip(spread, twin, strict=True):
        pieces += [own, other]
    return smalls, pieces


def fill_weights(rep, shard, qkv_ref, out_ref, smalls_ref, piece_refs, full_ref, small_ref):
    depth = out_ref.shape[0]
    own = pl.multiple_of(shard * depth, depth)
    for s in range(3):
        full_ref[s, pl.ds(own, depth), :] = qkv_ref[s]
    full_ref[3, pl.ds(own, depth), :] = out_ref[...]
    small_ref[:, pl.ds(own, depth)] = smalls_ref[0, :, 0:depth]
    for far in range(1, smalls_ref.shape[0]):
        base = pl.multiple_of((shard ^ far) * depth, depth)
        small_ref[:, pl.ds(base, depth)] = smalls_ref[far, :, 0:depth]
        for k, piece in enumerate(piece_refs):
            rows = piece.shape[2]
            start = pl.multiple_of(base + (rep ^ k) * rows, rows)
            for s in range(4):
                full_ref[s, pl.ds(start, rows), :] = piece[far - 1, s]


def head_masks(count):
    lane = iota((count, 2 * HEAD_DIM), 1)
    return [lane < HEAD_DIM, lane >= HEAD_DIM]


def forward_body(fast, n_pieces, *refs):
    if fast:
        where_ref, x_ref, seg_row_ref, seg_col_ref, index_ref, qkv_ref, out_ref, smalls_ref = refs[:8]
        piece_refs = refs[8 : 8 + n_pieces]
        refs = refs[8 + n_pieces :]
    else:
        x_ref, seg_row_ref, seg_col_ref, index_ref, qkv_ref, out_ref, router_ref, gains_ref = refs[:8]
        refs = refs[8:]
    (sent_ref, full_ref, small_ref, weights_ref, proj_ref, n1_ref, mixed_ref, resid_ref, n2_ref, gate_ref) = refs
    if fast:
        fill_weights(
            where_ref[0], where_ref[1], qkv_ref, out_ref, smalls_ref, piece_refs, full_ref, small_ref
        )
    else:
        full_ref[0:3] = qkv_ref[...]
        full_ref[3] = out_ref[...]
        small_ref[...] = jnp.concatenate(
            [
                router_ref[...].astype(F32),
                gains_ref[...].astype(F32),
                jnp.zeros((6, out_ref.shape[1]), F32),
            ],
            axis=0,
        ).astype(BF)
    x = x_ref[0].astype(F32)
    count, width = x.shape
    small = small_ref[...].astype(F32)
    unit1, _ = unit_of(x)
    n1 = (unit1 * small[8:9, :]).astype(BF)
    n1_ref[...] = n1
    for s in range(3):
        proj_ref[s] = dot_nn(n1, full_ref[s]).astype(BF)
    bias = jnp.where(seg_col_ref[...] == seg_row_ref[...], 0.0, -1e30).astype(F32)
    masks = head_masks(count)
    for pair in range(HEADS // 2):
        lanes = slice(pair * 2 * HEAD_DIM, (pair + 1) * 2 * HEAD_DIM)
        q, k, v = proj_ref[0, :, lanes], proj_ref[1, :, lanes], proj_ref[2, :, lanes]
        q = q * BF(HEAD_DIM**-0.5)
        halves = []
        for half in range(2):
            scores = dot_nt(jnp.where(masks[half], q, BF(0)), k) + bias
            top = jnp.max(scores, axis=-1, keepdims=True)
            terms = jnp.exp(scores - top)
            total = jnp.sum(terms, axis=-1, keepdims=True)
            weights = (terms * (1.0 / total)).astype(BF)
            weights_ref[2 * pair + half] = weights
            halves.append(dot_nn(weights, v))
        mixed_ref[:, lanes] = jnp.where(masks[0], halves[0], halves[1]).astype(BF)
    resid = x + dot_nn(mixed_ref[...], full_ref[3])
    resid_ref[...] = resid
    unit2, _ = unit_of(resid)
    n2 = (unit2 * small[9:10, :]).astype(BF)
    n2_ref[...] = n2
    logits = dot_nt(small_ref[...], n2)[0:EXPERTS]
    terms = jnp.exp(logits - jnp.max(logits, axis=0, keepdims=True))
    gates = terms / jnp.sum(terms, axis=0, keepdims=True)
    gate_ref[...] = gates
    index = index_ref[...]
    for e in range(EXPERTS):
        row = iota((ROWS, count), 0) + e * ROWS
        pick = (row == index[0:1, :]) | (row == index[1:2, :])
        pick = jnp.where(pick, 1.0, 0.0).astype(BF)
        rows = dot_nn(pick, n2)
        side = dot_nt(piece_rows(gates[e : e + 1, :]).astype(BF), pick)
        side = jnp.concatenate([side, jnp.zeros((8, width - ROWS), F32)], axis=1)
        sent_ref[e] = jnp.concatenate([rows[0:SLOTS], side], axis=0).astype(BF)


def forward(fast, where, x, seg_row, seg_col, index, weights_in, pieces):
    _, count, width = x.shape
    body = lambda *refs: forward_body(fast, len(pieces), *refs)
    operands = [x, seg_row, seg_col, index, *weights_in, *pieces]
    specs = vmem(len(operands))
    if fast:
        operands = [where] + operands
        specs = [pl.BlockSpec(memory_space=pltpu.SMEM)] + specs
    shapes = (
        ((EXPERTS, ROWS, width), BF),
        ((4, width, width), BF),
        ((16, width), BF),
        ((HEADS, count, count), BF),
        ((3, count, width), BF),
        ((count, width), BF),
        ((count, width), BF),
        ((count, width), F32),
        ((count, width), BF),
        ((EXPERTS, count), F32),
    )
    return pl.pallas_call(
        body,
        out_shape=tuple(jax.ShapeDtypeStruct(*s) for s in shapes),
        in_specs=specs,
        out_specs=tuple(vmem(len(shapes))),
        compiler_params=params(48),
        cost_estimate=pl.CostEstimate(
            flops=8 << 30, bytes_accessed=16 << 20, transcendentals=HEADS * count * count
        ),
        name="forward",
    )(*operands)


def expert_body(first, last, n_out, where_ref, n2_ref, cot_ref, w_in_ref, w_out_ref, *refs):
    if first:
        acc_in = None
    else:
        acc_in, refs = refs[:2], refs[2:]
    if last:
        back_ref, out_ref = refs[:2]
    else:
        acc_out = refs[:2]
    chunk_refs = refs[2 : 2 + n_out]
    rows_ref, gso_ref, rows_t_ref, gso_t_ref, gate_ref, eo_ref, gsi_ref = refs[2 + n_out :]
    step = pl.program_id(0)
    groups = n2_ref.shape[0]

    @pl.when(step == 0)
    def _():
        row = iota((ROWS, 1), 0)
        eye = jnp.where(iota((ROWS, ROWS), 0) == iota((ROWS, ROWS), 1), 1.0, 0.0).astype(BF)
        for g in range(groups):
            rows = n2_ref[g]
            side = rows.astype(F32)[SLOTS:, 0:ROWS].astype(BF)
            gate = jnp.sum(dot_nt(eye, side), axis=1, keepdims=True)
            span = slice(g * ROWS, (g + 1) * ROWS)
            gate_ref[span] = gate
            rows_ref[span] = jnp.where(row < SLOTS, rows, BF(0))
            gso_ref[span] = (gate * cot_ref[g].astype(F32)).astype(BF)
        rows_t_ref[...] = rows_ref[...].T
        gso_t_ref[...] = gso_ref[...].T
        if first:
            eo_ref[...] = jnp.zeros_like(eo_ref)
            gsi_ref[...] = jnp.zeros_like(gsi_ref)
        else:
            eo_ref[...] = acc_in[0][...]
            gsi_ref[...] = acc_in[1][...]

    w_in, w_out = w_in_ref[0], w_out_ref[0]
    u = dot_nn(rows_ref[...], w_in)
    t = jnp.tanh(GELU_A * (u + GELU_B * (u * u * u)))
    half = 0.5 * (1.0 + t)
    hidden = (u * half).astype(BF)
    slope = half + 0.5 * u * (1.0 - t * t) * (GELU_A * (1.0 + 3.0 * GELU_B * (u * u)))
    grad_pre = (dot_nn(gso_ref[...], w_out) * slope).astype(BF)
    eo_ref[...] += dot_nt(hidden, w_out)
    gsi_ref[...] += dot_nt(grad_pre, w_in)
    for k in range(n_out):
        depth = chunk_refs[k].shape[1]
        start = pl.multiple_of((where_ref[1] ^ k) * depth, depth)
        chunk_refs[k][0] = dot_nn(rows_t_ref[pl.ds(start, depth), :], grad_pre).astype(BF)
        chunk_refs[k][1] = dot_nn(gso_t_ref[pl.ds(start, depth), :], hidden).astype(BF)

    @pl.when(step == pl.num_programs(0) - 1)
    def _():
        if not last:
            acc_out[0][...] = eo_ref[...]
            acc_out[1][...] = gsi_ref[...]
            return
        ones = jnp.ones((8, n2_ref.shape[2]), BF)
        for g in range(groups):
            span = slice(g * ROWS, (g + 1) * ROWS)
            out = (gate_ref[span] * eo_ref[span]).astype(BF)
            out_ref[g] = out
            product = out.astype(F32) * cot_ref[g].astype(F32)
            high = product.astype(BF)
            low = (product - high.astype(F32)).astype(BF)
            inner = dot_nt(ones, high) + dot_nt(ones, low)
            side = piece_rows(inner[0:1, :])
            side = jnp.concatenate([side, jnp.zeros((8, out.shape[1] - ROWS), F32)], axis=1)
            back_ref[g] = jnp.concatenate([gsi_ref[span][0:SLOTS], side], axis=0).astype(BF)


def expert_block(block, blocks, peers, where, n2, cot, w_in, w_out, acc):
    groups, _, width = n2.shape
    hidden_n = w_in.shape[2] // blocks
    steps = hidden_n // FF_STEP
    first, last = block == 0, block == blocks - 1
    total = groups * ROWS
    depth = width // peers
    whole = lambda *shape: pl.BlockSpec(shape, lambda i, w: (0,) * len(shape))
    weight = pl.BlockSpec((1, width, FF_STEP), lambda i, w: (w[0], 0, block * steps + i))
    payload = jax.ShapeDtypeStruct((groups, ROWS, width), BF)
    running = jax.ShapeDtypeStruct((total, width), F32)
    out_shape = [payload] * 2 if last else [running] * 2
    out_specs = [whole(groups, ROWS, width)] * 2 if last else [whole(total, width)] * 2
    out_shape += [jax.ShapeDtypeStruct((2, depth, hidden_n), BF)] * peers
    out_specs += [pl.BlockSpec((2, depth, FF_STEP), lambda i, w: (0, 0, i))] * peers
    in_specs = [whole(groups, ROWS, width)] * 2 + [weight] * 2
    operands = [n2, cot, w_in, w_out]
    if not first:
        in_specs += [whole(total, width)] * 2
        operands += list(acc)
    body = lambda *refs: expert_body(first, last, peers, *refs)
    return pl.pallas_call(
        body,
        out_shape=tuple(out_shape),
        grid_spec=pltpu.PrefetchScalarGridSpec(
            num_scalar_prefetch=1,
            grid=(steps,),
            in_specs=in_specs,
            out_specs=tuple(out_specs),
            scratch_shapes=[
                pltpu.VMEM((total, width), BF),
                pltpu.VMEM((total, width), BF),
                pltpu.VMEM((width, total), BF),
                pltpu.VMEM((width, total), BF),
                pltpu.VMEM((total, 1), F32),
                pltpu.VMEM((total, width), F32),
                pltpu.VMEM((total, width), F32),
            ],
        ),
        compiler_params=params(50),
        cost_estimate=pl.CostEstimate(
            flops=12 * total * width * hidden_n,
            bytes_accessed=8 * width * hidden_n + 16 * total * width,
            transcendentals=total * hidden_n,
        ),
        name="experts",
    )(where, *operands)


def place_grads(fast, reps, shards_n, pack_ref, which, grad, small_rows=None):
    if not fast:
        pack_ref[which] = grad.astype(BF)
        return
    width = grad.shape[0]
    depth = width // shards_n
    rows = depth // reps
    grad = grad.astype(BF)
    for z in range(shards_n):
        for r in range(reps):
            start = z * depth + r * rows
            pack_ref[r, z, which * rows : (which + 1) * rows, :] = grad[start : start + rows]


def backward_body(fast, reps, shards_n, *refs):
    (back_ref, x_ref, cot_ref, index_ref, full_ref, small_ref, weights_ref, proj_ref, n1_ref) = refs[:9]
    (mixed_ref, resid_ref, n2_ref, gate_ref, grad_x_ref, pack_ref, sums_ref, gp_ref) = refs[9:]
    count, width = resid_ref.shape
    small = small_ref[...].astype(F32)
    index = index_ref[...]
    gates = gate_ref[...]
    grad_n2 = jnp.zeros((count, width), F32)
    rows_h = []
    for e in range(EXPERTS):
        row = iota((ROWS, count), 0) + e * ROWS
        pick = (row == index[0:1, :]) | (row == index[1:2, :])
        pick = jnp.where(pick, 1.0, 0.0).astype(BF)
        back = back_ref[e]
        side = back.astype(F32)[SLOTS:, 0:ROWS].astype(BF)
        rows_h.append(jnp.sum(dot_nn(side, pick), axis=0, keepdims=True))
        grad_n2 = grad_n2 + dot_tn(pick, back)
    inner = jnp.concatenate(rows_h, axis=0)
    grad_logits = (inner - gates * jnp.sum(inner, axis=0, keepdims=True)).astype(BF)
    wide_logits = jnp.concatenate(
        [grad_logits.astype(F32), jnp.zeros((8, count), F32)], axis=0
    ).astype(BF)
    grad_n2 = grad_n2 + dot_tn(wide_logits, small_ref[...])
    grad_router = dot_nn(wide_logits, n2_ref[...])[0:EXPERTS]
    unit2, inv2 = unit_of(resid_ref[...])
    grad_gain2 = jnp.sum(grad_n2 * unit2, axis=0, keepdims=True)
    a = grad_n2 * small[9:10, :]
    grad_resid = cot_ref[0].astype(F32) + inv2 * (
        a
        - jnp.mean(a, axis=-1, keepdims=True)
        - unit2 * jnp.mean(a * unit2, axis=-1, keepdims=True)
    )
    branch = grad_resid.astype(BF)
    place_grads(fast, reps, shards_n, pack_ref, 3, dot_tn(mixed_ref[...], branch))
    grad_mixed = dot_nt(branch, full_ref[3]).astype(BF)
    masks = head_masks(count)
    factor = HEAD_DIM**-0.5
    for pair in range(HEADS // 2):
        lanes = slice(pair * 2 * HEAD_DIM, (pair + 1) * 2 * HEAD_DIM)
        q, k, v = proj_ref[0, :, lanes], proj_ref[1, :, lanes], proj_ref[2, :, lanes]
        gm = grad_mixed[:, lanes]
        parts = []
        for half in range(2):
            weights = weights_ref[2 * pair + half]
            probs = weights.astype(F32)
            grad_probs = dot_nt(jnp.where(masks[half], gm, BF(0)), v)
            total = jnp.sum(probs * grad_probs, axis=-1, keepdims=True)
            grad_scores = (probs * (grad_probs - total)).astype(BF)
            parts.append(
                (dot_nn(grad_scores, k), dot_tn(grad_scores, q), dot_tn(weights, gm))
            )
        for s in range(3):
            both = jnp.where(masks[0], parts[0][s], parts[1][s])
            gp_ref[s, :, lanes] = (both * factor if s < 2 else both).astype(BF)
    n1 = n1_ref[...]
    grad_n1 = jnp.zeros((count, width), F32)
    for s in range(3):
        grads = gp_ref[s]
        place_grads(fast, reps, shards_n, pack_ref, s, dot_tn(n1, grads))
        grad_n1 = grad_n1 + dot_nt(grads, full_ref[s])
    unit1, inv1 = unit_of(x_ref[0].astype(F32))
    grad_gain1 = jnp.sum(grad_n1 * unit1, axis=0, keepdims=True)
    b = grad_n1 * small[8:9, :]
    grad_x = grad_resid + inv1 * (
        b
        - jnp.mean(b, axis=-1, keepdims=True)
        - unit1 * jnp.mean(b * unit1, axis=-1, keepdims=True)
    )
    grad_x_ref[0] = grad_x.astype(BF)
    sums = jnp.concatenate(
        [grad_router, grad_gain1, grad_gain2, jnp.zeros((6, width), F32)], axis=0
    )
    if not fast:
        sums_ref[...] = sums
        return
    depth = width // shards_n
    rows = depth // reps
    for z in range(shards_n):
        for r in range(reps):
            two = sums[2 * r : 2 * r + 2, z * depth : (z + 1) * depth]
            two = jnp.concatenate([two, jnp.zeros((6, depth), F32)], axis=0)
            two = jnp.concatenate([two, jnp.zeros((8, width - depth), F32)], axis=1)
            sums_ref[r, z] = two
            pack_ref[r, z, 4 * rows :, :] = two.astype(BF)


def backward(fast, reps, shards_n, operands):
    x = operands[1]
    _, count, width = x.shape
    if fast:
        rows = width // shards_n // reps
        pack = jax.ShapeDtypeStruct((reps, shards_n, 4 * rows + 8, width), BF)
        sums = jax.ShapeDtypeStruct((reps, shards_n, 8, width), F32)
    else:
        pack = jax.ShapeDtypeStruct((4, width, width), BF)
        sums = jax.ShapeDtypeStruct((16, width), F32)
    return pl.pallas_call(
        lambda *refs: backward_body(fast, reps, shards_n, *refs),
        out_shape=(jax.ShapeDtypeStruct(x.shape, BF), pack, sums),
        in_specs=vmem(len(operands)),
        out_specs=tuple(vmem(3)),
        scratch_shapes=[pltpu.VMEM((3, count, width), BF)],
        compiler_params=params(48),
        cost_estimate=pl.CostEstimate(
            flops=16 << 30, bytes_accessed=16 << 20, transcendentals=0
        ),
        name="backward",
    )(*operands)


def result_body(out_ref, index_ref, resid_ref, result_ref):
    total = resid_ref[...]
    count = total.shape[0]
    index = index_ref[...]
    for e in range(EXPERTS):
        row = iota((ROWS, count), 0) + e * ROWS
        pick = (row == index[0:1, :]) | (row == index[1:2, :])
        total = total + dot_tn(jnp.where(pick, 1.0, 0.0).astype(BF), out_ref[e])
    result_ref[0] = total.astype(BF)


def combine(out, index, resid):
    count, width = resid.shape
    return pl.pallas_call(
        result_body,
        out_shape=jax.ShapeDtypeStruct((1, count, width), BF),
        in_specs=vmem(3),
        out_specs=vmem(1)[0],
        compiler_params=params(24),
        cost_estimate=pl.CostEstimate(
            flops=2 * EXPERTS * ROWS * count * width, bytes_accessed=3 << 20, transcendentals=0
        ),
        name="combine",
    )(out, index, resid)


def widen_body(n_src, first, where_ref, *refs):
    srcs = refs[:n_src]
    w_in_ref, w_out_ref = refs[-2:]
    step = pl.program_id(0)
    for i in range(n_src):

        @pl.when(step == i)
        def _(i=i):
            w_in_ref[0] = srcs[i][0].astype(F32)
            w_out_ref[0] = srcs[i][1].astype(F32)


def widen(block, blocks, where, sources, experts_n, peers, hidden, so_far):
    _, depth, cols = sources[0].shape
    n_src = len(sources)
    out = jax.ShapeDtypeStruct((experts_n, depth * peers, hidden), F32)
    spot = pl.BlockSpec(
        (1, depth, cols), lambda i, w: (w[0] ^ (i // peers), w[1] ^ (i % peers), block)
    )
    whole = pl.BlockSpec((2, depth, cols), lambda i, w: (0, 0, 0))
    in_specs = [whole] * n_src
    operands = list(sources)
    aliases = {}
    if so_far is not None:
        in_specs += [pl.BlockSpec(memory_space=pl.ANY)] * 2
        aliases = {1 + n_src: 0, 2 + n_src: 1}
        operands += list(so_far)
    return pl.pallas_call(
        lambda *refs: widen_body(n_src, so_far is None, *refs),
        out_shape=(out, out),
        grid_spec=pltpu.PrefetchScalarGridSpec(
            num_scalar_prefetch=1,
            grid=(n_src,),
            in_specs=in_specs,
            out_specs=(spot, spot),
        ),
        input_output_aliases=aliases,
        compiler_params=params(32),
        cost_estimate=pl.CostEstimate(
            flops=0, bytes_accessed=n_src * 12 * depth * cols, transcendentals=0
        ),
        name="widen",
    )(where, *operands)


def finish_body(rows, parts_ref, qkv_ref, out_ref, router_ref, gains_ref):
    reps = parts_ref.shape[0]
    depth = out_ref.shape[0]
    smalls = []
    for r in range(reps):
        for s in range(3):
            qkv_ref[s, r * rows : (r + 1) * rows, :] = parts_ref[
                r, s * rows : (s + 1) * rows, :
            ].astype(F32)
        out_ref[r * rows : (r + 1) * rows, :] = parts_ref[r, 3 * rows : 4 * rows, :].astype(F32)
        smalls.append(parts_ref[r].astype(F32)[4 * rows : 4 * rows + 2, 0:depth])
    small = jnp.concatenate(smalls, axis=0)
    wide = jnp.concatenate([small, jnp.zeros((depth - small.shape[0], depth), F32)], axis=0)
    router_ref[...] = wide.T[:, 0:EXPERTS]
    gains_ref[...] = small[EXPERTS : EXPERTS + 2]


def finish(parts, rows):
    reps, _, width = parts.shape
    depth = rows * reps
    return pl.pallas_call(
        lambda *refs: finish_body(rows, *refs),
        out_shape=(
            jax.ShapeDtypeStruct((3, depth, width), F32),
            jax.ShapeDtypeStruct((depth, width), F32),
            jax.ShapeDtypeStruct((depth, EXPERTS), F32),
            jax.ShapeDtypeStruct((2, depth), F32),
        ),
        in_specs=vmem(1),
        out_specs=tuple(vmem(4)),
        compiler_params=params(16),
        name="finish",
    )(parts)


def shards(reps, shards_n, *args):
    tokens, segments, choices, priority, cotangent = args[:5]
    qkv_weights, out_weight, router_weight, gains, w_in, w_out = args[5:]
    rep, shard = lax.axis_index("rep"), lax.axis_index("shard")
    width, hidden = w_in.shape[1:]
    owned = w_in.shape[0]
    peers = reps // owned
    depth = width // shards_n
    fast = depth % (16 * reps) == 0 and depth == 128 and owned == 2 and peers <= 4
    column = [
        [(c * owned + e % owned) * shards_n + e // owned for e in range(EXPERTS)]
        for c in range(peers)
    ]

    def to_experts(rows):
        return lax.all_to_all(rows, AXES, 0, 0, axis_index_groups=column, tiled=True)

    where = jnp.stack([rep % owned, rep // owned]).astype(jnp.int32)
    index, cot_sent = route(
        choices[0].T, priority, priority.reshape(-1, 1), cotangent
    )
    seg_col = segments.reshape(-1, 1)
    if fast:
        smalls, pieces = gather_weights(
            rep, shard, reps, shards_n, qkv_weights, out_weight, router_weight, gains
        )
        place = jnp.stack([rep, shard]).astype(jnp.int32)
        weights_in = (qkv_weights, out_weight, smalls)
    else:
        place, pieces = None, []
        weights_in = (
            lax.all_gather(qkv_weights, "shard", axis=1, tiled=True),
            lax.all_gather(out_weight, "shard", axis=0, tiled=True),
            lax.all_gather(router_weight, "shard", axis=0, tiled=True).T,
            lax.all_gather(gains, "shard", axis=1, tiled=True),
        )
    cot_in = to_experts(cot_sent)
    (sent, full, small, weights, proj, n1, mixed, resid, n2, gates) = forward(
        fast, place, tokens, segments, seg_col, index, weights_in, pieces
    )
    n2_in = to_experts(sent)

    blocks = FF_BLOCKS
    direct = fast
    chunk_where = where if direct else where * jnp.array([1, 0], jnp.int32)
    acc, chunks = None, []
    for block in range(blocks):
        made = expert_block(block, blocks, peers, chunk_where, n2_in, cot_in, w_in, w_out, acc)
        acc = made[:2]
        chunks.append(made[2:])
    back_in = to_experts(acc[0])
    out_in = to_experts(acc[1])

    widened = None
    for block in range(blocks):
        chunk = chunks[block]
        if direct:

            def peer(value, k):
                return lax.ppermute(value, "rep", [(i, i ^ k) for i in range(reps)])

            total = chunk[0].astype(F32)
            for k in range(1, peers):
                total = total + peer(chunk[k], k * owned).astype(F32)
            total = total.astype(BF)
            spread = [total] + [peer(total, k * owned) for k in range(1, peers)]
            for other in range(1, owned):
                spread = spread + [peer(part, other) for part in spread[:peers]]
        else:
            total = lax.psum_scatter(
                jnp.concatenate(chunk, axis=1), "rep", scatter_dimension=1, tiled=True
            )
            every = lax.all_gather(total, "rep", axis=1, tiled=True)
            spread = [every[:, k * (width // peers) : (k + 1) * (width // peers)] for k in range(peers)]
        widened = widen(block, blocks, chunk_where, spread, owned, peers, hidden, widened)
    grad_w_in, grad_w_out = widened

    grad_tokens, pack, sums = backward(
        fast,
        reps,
        shards_n,
        [back_in, tokens, cotangent, index, full, small, weights, proj, n1, mixed, resid, n2, gates],
    )
    result = combine(out_in, index, resid)
    if fast:
        rows = depth // reps
        plane = lax.all_to_all(pack, "rep", 0, 0, tiled=True)
        plane = jnp.sum(plane.astype(F32), axis=0).astype(BF)
        line = lax.all_to_all(plane, "shard", 0, 0, tiled=True)
        share = jnp.sum(line.astype(F32), axis=0).astype(BF)
        parts = lax.all_gather(share, "rep", axis=0, tiled=False)
        grad_qkv, grad_out, grad_router, grad_gains = finish(parts, rows)
    else:
        owned_rows = lax.psum_scatter(pack, "shard", scatter_dimension=1, tiled=True)
        owned_rows = lax.psum(owned_rows, "rep").astype(F32)
        grad_qkv, grad_out = owned_rows[0:3], owned_rows[3]
        sums = lax.psum(sums, AXES)
        mine = lax.dynamic_slice_in_dim(sums, shard * depth, depth, axis=1)
        grad_router, grad_gains = mine[0:EXPERTS].T, mine[EXPERTS : EXPERTS + 2]
    return (
        result,
        grad_tokens,
        grad_qkv,
        grad_out,
        grad_router,
        grad_gains,
        grad_w_in,
        grad_w_out,
    )


def solution(mesh):
    reps, shards_n = mesh.shape["rep"], mesh.shape["shard"]
    rows = P(("rep", "shard"), None, None)
    flat = P(("rep", "shard"), None)
    first = P("shard", None)
    stack = P("shard", None, None)
    second = P(None, "shard", None)
    return jax.shard_map(
        lambda *args: shards(reps, shards_n, *args),
        mesh=mesh,
        in_specs=(
            rows, flat, rows, flat, rows, second, first, first, P(None, "shard"), stack, stack,
        ),
        out_specs=(rows, rows, second, first, first, P(None, "shard"), stack, stack),
        check_vma=False,
    )
```

```python
import jax
import jax.numpy as jnp
from jax import lax
from jax.experimental import pallas as pl
from jax.experimental.pallas import tpu as pltpu
from jax.sharding import PartitionSpec as P

HEADS = 8
HEAD_DIM = 64
EXPERTS = 8
CAPACITY = 135
ROWS = 144
SLOTS = 136
EPS = 1e-06
F32 = jnp.float32
BF = jnp.bfloat16
AXES = ("rep", "shard")
FF_STEP = 512
KEPT = 7
SMALL = pl.CostEstimate(flops=1000, bytes_accessed=1000, transcendentals=0)
GELU_A = 0.7978845608028654
GELU_B = 0.044715


def dot_nn(a, b):
    return lax.dot_general(a, b, (((1,), (0,)), ((), ())), preferred_element_type=F32)


def dot_nt(a, b):
    return lax.dot_general(a, b, (((1,), (1,)), ((), ())), preferred_element_type=F32)


def dot_tn(a, b):
    return lax.dot_general(a, b, (((0,), (0,)), ((), ())), preferred_element_type=F32)


def after(value, *others):
    return lax.optimization_barrier((value, *others))[0]


def iota(shape, dim):
    return lax.broadcasted_iota(jnp.int32, shape, dim)


def unit_of(values):
    mean = jnp.mean(values, axis=-1, keepdims=True)
    centered = values - mean
    inv = lax.rsqrt(jnp.mean(centered * centered, axis=-1, keepdims=True) + EPS)
    return centered * inv, inv


def split3(values):
    high = values.astype(BF)
    rest = values - high.astype(F32)
    mid = rest.astype(BF)
    low = (rest - mid.astype(F32)).astype(BF)
    return high, mid, low


def piece_rows(values):
    high, mid, low = split3(values)
    shape = (8, values.shape[1])
    row = iota(shape, 0)
    parts = [jnp.broadcast_to(part.astype(F32), shape) for part in (high, mid, low)]
    return jnp.where(
        row == 0, parts[0], jnp.where(row == 1, parts[1], jnp.where(row == 2, parts[2], 0.0))
    )


def far(value):
    return pltpu.with_memory_space_constraint(value, pltpu.HBM)


def near(value):
    return pltpu.with_memory_space_constraint(value, pltpu.VMEM)


def vmem(n):
    return [pl.BlockSpec(memory_space=pltpu.VMEM)] * n


def params(mib):
    return pltpu.CompilerParams(vmem_limit_bytes=mib << 20)


def route_body(choice_ref, prio_ref, cot_ref, index_ref, sent_ref):
    count = cot_ref.shape[-2]
    choice = choice_ref[...]
    experts = iota((EXPERTS, count), 0)
    first = jnp.where(choice[0:1, :] == experts, 1.0, 0.0)
    second = jnp.where(choice[1:2, :] == experts, 1.0, 0.0)
    order = jnp.where(iota((count, count), 0) == prio_ref[...], 1.0, 0.0).astype(BF)
    earlier = jnp.where(iota((count, count), 0) < iota((count, count), 1), 1.0, 0.0).astype(BF)
    both = jnp.concatenate([first, second], axis=0).astype(BF)
    before = dot_nn(dot_nt(both, order).astype(BF), earlier)
    held = jnp.sum(first, axis=1, keepdims=True)
    before = jnp.concatenate([before[0:EXPERTS], before[EXPERTS:] + held], axis=0)
    before = dot_nn(jnp.minimum(before, 255.0).astype(BF), order)
    slot0 = jnp.sum(first * before[0:EXPERTS], axis=0, keepdims=True)
    slot1 = jnp.sum(second * before[EXPERTS:], axis=0, keepdims=True)
    slot = jnp.concatenate([slot0, slot1], axis=0).astype(jnp.int32)
    index = jnp.where(slot < CAPACITY, choice * ROWS + slot, -1)
    index_ref[...] = index
    cot = cot_ref[0]
    for e in range(EXPERTS):
        row = iota((ROWS, count), 0) + e * ROWS
        pick = (row == index[0:1, :]) | (row == index[1:2, :])
        sent_ref[e] = dot_nn(jnp.where(pick, 1.0, 0.0).astype(BF), cot).astype(BF)


def route(choice_t, prio, cot):
    _, count, width = cot.shape
    return pl.pallas_call(
        route_body,
        out_shape=(
            jax.ShapeDtypeStruct((2, count), jnp.int32),
            pltpu.HBM((EXPERTS, ROWS, width), BF),
        ),
        in_specs=vmem(3),
        out_specs=tuple(vmem(2)),
        compiler_params=params(12),
        cost_estimate=SMALL,
        name="route",
    )(far(choice_t), far(prio), far(cot))


def pack_body(where_ref, qkv_ref, out_ref, router_ref, gains_ref, pack_ref):
    rows = pack_ref.shape[1]
    start = pl.multiple_of(where_ref[0] * rows, rows)
    for s in range(3):
        pack_ref[s] = qkv_ref[s, pl.ds(start, rows), :]
    pack_ref[3] = out_ref[pl.ds(start, rows), :]
    depth = router_ref.shape[1]
    small = jnp.concatenate(
        [router_ref[...].astype(F32), gains_ref[...].astype(F32), jnp.zeros((6, depth), F32)],
        axis=0,
    )
    pack_ref[4, :, 0:depth] = small.astype(BF)
    pack_ref[4, :, depth:] = jnp.zeros((rows, pack_ref.shape[2] - depth), BF)


def pack_weights(rep, qkv, out, router, gains, rows):
    width = out.shape[1]
    return pl.pallas_call(
        pack_body,
        out_shape=jax.ShapeDtypeStruct((5, rows, width), BF),
        in_specs=[pl.BlockSpec(memory_space=pltpu.SMEM)] + vmem(4),
        out_specs=vmem(1)[0],
        compiler_params=params(4),
        name="pack_weights",
    )(rep.reshape(1), far(qkv), far(out), far(router), far(gains))


def gather_weights(rep, shard, reps, shards_n, qkv, out, router, gains):
    rows = qkv.shape[1] // reps
    pack = pack_weights(rep, qkv, out, router, gains, rows)
    lines = [
        lax.ppermute(pack, "shard", [(i, i ^ dz) for i in range(shards_n)])
        for dz in range(1, shards_n)
    ]
    block = jnp.stack([piece[0:4] for piece in lines])
    smalls = jnp.stack([piece[4] for piece in [pack] + lines])
    spread = [block] + [
        lax.ppermute(block, "rep", [(i, i ^ k) for i in range(reps)]) for k in range(2, reps, 2)
    ]
    twin = [lax.ppermute(piece, "rep", [(i, i ^ 1) for i in range(reps)]) for piece in spread]
    pieces = []
    for own, other in zip(spread, twin, strict=True):
        pieces += [own, other]
    return smalls, pieces, lines


def fill_weights(rep, shard, qkv_ref, out_ref, smalls_ref, piece_refs, full_ref, small_ref):
    depth = out_ref.shape[0]
    own = pl.multiple_of(shard * depth, depth)
    for s in range(3):
        full_ref[s, pl.ds(own, depth), :] = qkv_ref[s]
    full_ref[3, pl.ds(own, depth), :] = out_ref[...]
    small_ref[:, pl.ds(own, depth)] = smalls_ref[0, :, 0:depth]
    for far in range(1, smalls_ref.shape[0]):
        base = pl.multiple_of((shard ^ far) * depth, depth)
        small_ref[:, pl.ds(base, depth)] = smalls_ref[far, :, 0:depth]
        for k, piece in enumerate(piece_refs):
            rows = piece.shape[2]
            start = pl.multiple_of(base + (rep ^ k) * rows, rows)
            for s in range(4):
                full_ref[s, pl.ds(start, rows), :] = piece[far - 1, s]


def head_masks(count):
    lane = iota((count, 2 * HEAD_DIM), 1)
    return [lane < HEAD_DIM, lane >= HEAD_DIM]


def kept_shapes(count, width):
    return (
        ((4, width, width), BF),
        ((HEADS, count, count), BF),
        ((3, count, width), BF),
        ((count, width), BF),
        ((count, width), BF),
        ((count, width), F32),
        ((count, width), BF),
    )


def forward_body(fast, n_pieces, *refs):
    if fast:
        where_ref, x_ref, seg_ref, index_ref, qkv_ref, out_ref, smalls_ref = refs[:7]
        piece_refs = refs[7 : 7 + n_pieces]
        refs = refs[7 + n_pieces :]
    else:
        x_ref, seg_ref, index_ref, qkv_ref, out_ref, router_ref, gains_ref = refs[:7]
        refs = refs[7:]
    sent_ref, small_ref, gate_ref, *kept = refs[: 3 + KEPT]
    full_ref, weights_ref, proj_ref, n1_ref, mixed_ref, resid_ref, n2_ref = held = refs[3 + KEPT : -1]
    sem = refs[-1]

    def keep(*which):
        for i in which:
            pltpu.make_async_copy(held[i], kept[i], sem.at[i]).start()

    if fast:
        fill_weights(
            where_ref[0], where_ref[1], qkv_ref, out_ref, smalls_ref, piece_refs, full_ref, small_ref
        )
    else:
        full_ref[0:3] = qkv_ref[...]
        full_ref[3] = out_ref[...]
        small_ref[...] = jnp.concatenate(
            [
                router_ref[...].astype(F32),
                gains_ref[...].astype(F32),
                jnp.zeros((6, out_ref.shape[1]), F32),
            ],
            axis=0,
        ).astype(BF)
    keep(0)
    x = x_ref[0].astype(F32)
    count, width = x.shape
    small = small_ref[...].astype(F32)
    unit1, _ = unit_of(x)
    n1 = (unit1 * small[8:9, :]).astype(BF)
    n1_ref[...] = n1
    for s in range(3):
        proj_ref[s] = dot_nn(n1, full_ref[s]).astype(BF)
    keep(2, 3)
    document = jnp.where(iota((8, count), 0) == seg_ref[...], 1.0, 0.0).astype(BF)
    bias = jnp.where(dot_tn(document, document) > 0.5, 0.0, -1e30)
    masks = head_masks(count)
    for pair in range(HEADS // 2):
        lanes = slice(pair * 2 * HEAD_DIM, (pair + 1) * 2 * HEAD_DIM)
        q, k, v = proj_ref[0, :, lanes], proj_ref[1, :, lanes], proj_ref[2, :, lanes]
        q = q * BF(HEAD_DIM**-0.5)
        halves = []
        for half in range(2):
            scores = dot_nt(jnp.where(masks[half], q, BF(0)), k) + bias
            top = jnp.max(scores, axis=-1, keepdims=True)
            terms = jnp.exp(scores - top)
            total = jnp.sum(terms, axis=-1, keepdims=True)
            weights = (terms * (1.0 / total)).astype(BF)
            weights_ref[2 * pair + half] = weights
            halves.append(dot_nn(weights, v))
        mixed_ref[:, lanes] = jnp.where(masks[0], halves[0], halves[1]).astype(BF)
    keep(1, 4)
    resid = x + dot_nn(mixed_ref[...], full_ref[3])
    resid_ref[...] = resid
    keep(5)
    unit2, _ = unit_of(resid)
    n2 = (unit2 * small[9:10, :]).astype(BF)
    n2_ref[...] = n2
    keep(6)
    logits = dot_nt(small_ref[...], n2)[0:EXPERTS]
    terms = jnp.exp(logits - jnp.max(logits, axis=0, keepdims=True))
    gates = terms / jnp.sum(terms, axis=0, keepdims=True)
    gate_ref[...] = gates
    index = index_ref[...]
    for e in range(EXPERTS):
        row = iota((ROWS, count), 0) + e * ROWS
        pick = (row == index[0:1, :]) | (row == index[1:2, :])
        pick = jnp.where(pick, 1.0, 0.0).astype(BF)
        rows = dot_nn(pick, n2)
        side = dot_nt(piece_rows(gates[e : e + 1, :]).astype(BF), pick)
        side = jnp.concatenate([side, jnp.zeros((8, width - ROWS), F32)], axis=1)
        sent_ref[e] = jnp.concatenate([rows[0:SLOTS], side], axis=0).astype(BF)
    for i in range(KEPT):
        pltpu.make_async_copy(held[i], kept[i], sem.at[i]).wait()


def forward(fast, where, x, seg, index, weights_in, pieces):
    _, count, width = x.shape
    body = lambda *refs: forward_body(fast, len(pieces), *refs)
    operands = [far(x), far(seg), index, *(far(w) for w in weights_in[:2]), *weights_in[2:], *pieces]
    specs = vmem(len(operands))
    if fast:
        operands = [where] + operands
        specs = [pl.BlockSpec(memory_space=pltpu.SMEM)] + specs
    shown = (
        pltpu.HBM((EXPERTS, ROWS, width), BF),
        jax.ShapeDtypeStruct((16, width), BF),
        jax.ShapeDtypeStruct((EXPERTS, count), F32),
    )
    kept = kept_shapes(count, width)
    return pl.pallas_call(
        body,
        out_shape=(*shown, *(pltpu.HBM(*k) for k in kept)),
        in_specs=specs,
        out_specs=(*vmem(3), *([pl.BlockSpec(memory_space=pltpu.HBM)] * KEPT)),
        scratch_shapes=[*(pltpu.VMEM(*k) for k in kept), pltpu.SemaphoreType.DMA((KEPT,))],
        compiler_params=params(40),
        cost_estimate=SMALL,
        name="forward",
    )(*operands)


def expert_rows(n2_ref, cot_ref, w_in_ref, w_out_ref, back_ref, out_ref, span, scratch):
    hidden_ref, pre_ref, rows_ref, gso_ref = scratch
    row = iota((ROWS, 1), 0)
    eye = jnp.where(iota((ROWS, ROWS), 0) == iota((ROWS, ROWS), 1), 1.0, 0.0).astype(BF)
    gates, rows_all, gso_all = [], [], []
    for g in range(2):
        rows = n2_ref[g]
        side = rows.astype(F32)[SLOTS:, 0:ROWS].astype(BF)
        gate = jnp.sum(dot_nt(eye, side), axis=1, keepdims=True)
        gates.append(gate)
        rows_all.append(jnp.where(row < SLOTS, rows, BF(0)))
        gso_all.append((gate * cot_ref[g].astype(F32)).astype(BF))
    rows, gso = jnp.concatenate(rows_all, axis=0), jnp.concatenate(gso_all, axis=0)
    rows_ref[span], gso_ref[span] = rows, gso
    for start in range(0, w_in_ref.shape[2], FF_STEP):
        cols = slice(start, start + FF_STEP)
        u = dot_nn(rows, w_in_ref[0, :, cols])
        square = u * u
        t = jnp.tanh(GELU_A * (u + GELU_B * (u * square)))
        half = 0.5 * (1.0 + t)
        hidden = u * half
        slope = half + hidden * (1.0 - t) * (GELU_A * (1.0 + 3.0 * GELU_B * square))
        hidden_ref[span, cols] = hidden.astype(BF)
        pre_ref[span, cols] = (dot_nn(gso, w_out_ref[0, :, cols]) * slope).astype(BF)
    grad_in = dot_nt(pre_ref[span], w_in_ref[0])
    result = dot_nt(hidden_ref[span], w_out_ref[0])
    ones = jnp.ones((8, rows.shape[1]), BF)
    for g in range(2):
        part = slice(g * ROWS, (g + 1) * ROWS)
        out = (gates[g] * result[part]).astype(BF)
        out_ref[g] = out
        product = out.astype(F32) * cot_ref[g].astype(F32)
        high = product.astype(BF)
        low = (product - high.astype(F32)).astype(BF)
        inner = dot_nt(ones, high) + dot_nt(ones, low)
        side = piece_rows(inner[0:1, :])
        side = jnp.concatenate([side, jnp.zeros((8, out.shape[1] - ROWS), F32)], axis=1)
        back_ref[g] = jnp.concatenate([grad_in[part][0:SLOTS], side], axis=0).astype(BF)


def experts_body(where_ref, *refs):
    expert_rows(*refs[:6], slice(None), refs[6:])


def experts(where, n2, cot, w_in, w_out):
    groups, _, width = n2.shape
    hidden_n = w_in.shape[2]
    total = groups * ROWS
    weight = pl.BlockSpec((1, width, hidden_n), lambda i, w: (w[0], 0, 0))
    payload = pl.BlockSpec((2, ROWS, width), lambda i, w: (i, 0, 0))
    narrow = pl.BlockSpec((2 * ROWS, width), lambda i, w: (i, 0))
    wide = pl.BlockSpec((2 * ROWS, hidden_n), lambda i, w: (i, 0))
    return pl.pallas_call(
        experts_body,
        out_shape=(
            [pltpu.HBM((groups, ROWS, width), BF)] * 2
            + [pltpu.HBM((total, hidden_n), BF)] * 2
            + [pltpu.HBM((total, width), BF)] * 2
        ),
        grid_spec=pltpu.PrefetchScalarGridSpec(
            num_scalar_prefetch=1,
            grid=(groups // 2,),
            in_specs=[payload, payload, weight, weight],
            out_specs=[payload, payload, wide, wide, narrow, narrow],
        ),
        compiler_params=params(40),
        cost_estimate=SMALL,
        name="experts",
    )(where, n2, cot, far(w_in), far(w_out))


def expert_grads_body(split, where_ref, hidden_ref, pre_ref, rows_ref, gso_ref, *refs):
    grad_refs, sum_ref = refs[:-1], refs[-1]
    step, steps = pl.program_id(0), pl.num_programs(0)
    for half, (left, right) in enumerate(((rows_ref, pre_ref), (gso_ref, hidden_ref))):
        grad = dot_tn(left[...], right[...]).astype(BF)
        if not split:
            grad_refs[0][half] = grad
            continue
        sum_ref[half] = grad
    if not split:
        return
    depth = sum_ref.shape[1] // 4
    for late in range(2):

        @pl.when((step < steps // 2) if late == 0 else (step >= steps // 2))
        def _(late=late):
            for half in range(2):
                for k in range(4):
                    start = pl.multiple_of((where_ref[1] ^ k) * depth, depth)
                    goes = k == 3 or k == 1 + late
                    ref = grad_refs[2 * late + (0 if goes else 1)]
                    ref[int(k == 3 or k == 2 - late), half] = sum_ref[half, pl.ds(start, depth), :]


def expert_grads(where, split, hidden, pre, rows, gso):
    total, width = rows.shape
    hidden_n = hidden.shape[1]
    steps = hidden_n // FF_STEP
    narrow = pl.BlockSpec((total, width), lambda i, w: (0, 0))
    wide = pl.BlockSpec((total, FF_STEP), lambda i, w: (0, i))
    if split:
        part = (2, 2, width // 4, FF_STEP)
        first = pl.BlockSpec(part, lambda i, w: (0, 0, 0, jnp.minimum(i, steps // 2 - 1)))
        second = pl.BlockSpec(part, lambda i, w: (0, 0, 0, jnp.maximum(i - steps // 2, 0)))
        grad_specs = [first, first, second, second]
        grad_shapes = [jax.ShapeDtypeStruct((2, 2, width // 4, hidden_n // 2), BF)] * 4
    else:
        grad_specs = [pl.BlockSpec((2, width, FF_STEP), lambda i, w: (0, 0, i))]
        grad_shapes = [pltpu.HBM((2, width, hidden_n), BF)]
    return pl.pallas_call(
        lambda *refs: expert_grads_body(split, *refs),
        out_shape=grad_shapes,
        grid_spec=pltpu.PrefetchScalarGridSpec(
            num_scalar_prefetch=1,
            grid=(steps,),
            in_specs=[wide, wide, narrow, narrow],
            out_specs=grad_specs,
            scratch_shapes=[pltpu.VMEM((2, width, FF_STEP), BF)],
        ),
        compiler_params=params(30),
        cost_estimate=SMALL,
        name="expert_grads",
    )(where, far(hidden), far(pre), far(rows), far(gso))


def place_grads(fast, reps, shards_n, pack_ref, which, grad):
    if not fast:
        pack_ref[which] = grad.astype(BF)
        return
    width = grad.shape[0]
    depth = width // shards_n
    rows = depth // reps
    grad = grad.astype(BF)
    for z in range(shards_n):
        for r in range(reps):
            start = z * depth + r * rows
            span = slice(which * rows, (which + 1) * rows)
            pack_ref[r % 2, z, r // 2, span, :] = grad[start : start + rows]


def backward_body(fast, reps, shards_n, where_ref, *refs):
    core = where_ref[0]
    back_ref, x_ref, cot_ref, index_ref, small_ref, gate_ref, *kept = refs[: 6 + KEPT]
    if fast:
        grad_x_ref, mine_ref, twin_ref, pack_ref, gp_ref = refs[6 + KEPT : 11 + KEPT]
        refs = refs[11 + KEPT :]
    else:
        grad_x_ref, pack_ref, sums_ref, gp_ref = refs[6 + KEPT : 10 + KEPT]
        refs = refs[10 + KEPT :]
    full_ref, weights_ref, proj_ref, n1_ref, mixed_ref, resid_ref, n2_ref = held = refs[:-1]
    sem = refs[-1]
    for i in (5, 6, 4, 0, 2, 1, 3):
        pltpu.make_async_copy(kept[i], held[i], sem.at[i]).start()

    def need(*which):
        for i in which:
            pltpu.make_async_copy(kept[i], held[i], sem.at[i]).wait()

    count, width = resid_ref.shape
    small = small_ref[...].astype(F32)
    index = index_ref[...]
    gates = gate_ref[...]
    grad_n2 = jnp.zeros((count, width), F32)
    rows_h = []
    for e in range(EXPERTS):
        row = iota((ROWS, count), 0) + e * ROWS
        pick = (row == index[0:1, :]) | (row == index[1:2, :])
        pick = jnp.where(pick, 1.0, 0.0).astype(BF)
        back = back_ref[e]
        side = back.astype(F32)[SLOTS:, 0:ROWS].astype(BF)
        rows_h.append(jnp.sum(dot_nn(side, pick), axis=0, keepdims=True))
        grad_n2 = grad_n2 + dot_tn(pick, back)
    inner = jnp.concatenate(rows_h, axis=0)
    grad_logits = (inner - gates * jnp.sum(inner, axis=0, keepdims=True)).astype(BF)
    wide_logits = jnp.concatenate(
        [grad_logits.astype(F32), jnp.zeros((8, count), F32)], axis=0
    ).astype(BF)
    grad_n2 = grad_n2 + dot_tn(wide_logits, small_ref[...])
    need(5, 6)
    grad_router = dot_nn(wide_logits, n2_ref[...])[0:EXPERTS]
    unit2, inv2 = unit_of(resid_ref[...])
    grad_gain2 = jnp.sum(grad_n2 * unit2, axis=0, keepdims=True)
    a = grad_n2 * small[9:10, :]
    grad_resid = cot_ref[0].astype(F32) + inv2 * (
        a
        - jnp.mean(a, axis=-1, keepdims=True)
        - unit2 * jnp.mean(a * unit2, axis=-1, keepdims=True)
    )
    branch = grad_resid.astype(BF)
    need(4, 0)
    place_grads(fast, reps, shards_n, pack_ref, 3, dot_tn(mixed_ref[...], branch))
    grad_mixed = dot_nt(branch, full_ref[3]).astype(BF)
    need(2, 1)
    masks = head_masks(count)
    factor = HEAD_DIM**-0.5
    for pair in range(HEADS // 2):
        lanes = slice(pair * 2 * HEAD_DIM, (pair + 1) * 2 * HEAD_DIM)
        q, k, v = proj_ref[0, :, lanes], proj_ref[1, :, lanes], proj_ref[2, :, lanes]
        gm = grad_mixed[:, lanes]
        parts = []
        for half in range(2):
            weights = weights_ref[2 * pair + half]
            probs = weights.astype(F32)
            grad_probs = dot_nt(jnp.where(masks[half], gm, BF(0)), v)
            total = jnp.sum(probs * grad_probs, axis=-1, keepdims=True)
            grad_scores = (probs * (grad_probs - total)).astype(BF)
            parts.append(
                (dot_nn(grad_scores, k), dot_tn(grad_scores, q), dot_tn(weights, gm))
            )
        for s in range(3):
            both = jnp.where(masks[0], parts[0][s], parts[1][s])
            gp_ref[s, :, lanes] = (both * factor if s < 2 else both).astype(BF)
    need(3)
    n1 = n1_ref[...]
    grad_n1 = jnp.zeros((count, width), F32)
    for s in range(3):
        grads = gp_ref[s]
        place_grads(fast, reps, shards_n, pack_ref, s, dot_tn(n1, grads))
        grad_n1 = grad_n1 + dot_nt(grads, full_ref[s])
    unit1, inv1 = unit_of(x_ref[0].astype(F32))
    grad_gain1 = jnp.sum(grad_n1 * unit1, axis=0, keepdims=True)
    b = grad_n1 * small[8:9, :]
    grad_x = grad_resid + inv1 * (
        b
        - jnp.mean(b, axis=-1, keepdims=True)
        - unit1 * jnp.mean(b * unit1, axis=-1, keepdims=True)
    )
    grad_x_ref[0] = grad_x.astype(BF)
    sums = jnp.concatenate(
        [grad_router, grad_gain1, grad_gain2, jnp.zeros((6, width), F32)], axis=0
    )
    if not fast:
        sums_ref[...] = sums
        return
    depth = width // shards_n
    rows = depth // reps
    for z in range(shards_n):
        for r in range(reps):
            two = sums[2 * r : 2 * r + 2, z * depth : (z + 1) * depth]
            two = jnp.concatenate([two, jnp.zeros((6, depth), F32)], axis=0)
            two = jnp.concatenate([two, jnp.zeros((8, width - depth), F32)], axis=1)
            pack_ref[r % 2, z, r // 2, 4 * rows :, :] = two.astype(BF)
    copies = [
        pltpu.make_async_copy(pack_ref.at[core ^ i], (mine_ref, twin_ref)[i], sem.at[i])
        for i in range(2)
    ]
    for copy in copies:
        copy.start()
    for copy in copies:
        copy.wait()


def backward(fast, reps, shards_n, where, operands):
    x = operands[1]
    _, count, width = x.shape
    outs = [jax.ShapeDtypeStruct(x.shape, BF)]
    scratch = [pltpu.VMEM((3, count, width), BF)]
    if fast:
        part = (shards_n, reps // 2, 4 * (width // shards_n // reps) + 8, width)
        outs += [pltpu.HBM(part, BF)] * 2
        out_specs = vmem(1) + [pl.BlockSpec(memory_space=pltpu.HBM)] * 2
        scratch = [pltpu.VMEM((2, *part), BF)] + scratch
    else:
        outs += [
            jax.ShapeDtypeStruct((4, width, width), BF),
            jax.ShapeDtypeStruct((16, width), F32),
        ]
        out_specs = vmem(3)
    return pl.pallas_call(
        lambda *refs: backward_body(fast, reps, shards_n, *refs),
        out_shape=tuple(outs),
        in_specs=[pl.BlockSpec(memory_space=pltpu.SMEM)]
        + vmem(len(operands) - KEPT)
        + [pl.BlockSpec(memory_space=pltpu.HBM)] * KEPT,
        out_specs=tuple(out_specs),
        scratch_shapes=[
            *scratch,
            *(pltpu.VMEM(*k) for k in kept_shapes(count, width)),
            pltpu.SemaphoreType.DMA((KEPT,)),
        ],
        compiler_params=params(40),
        cost_estimate=SMALL,
        name="backward",
    )(where, operands[0], *(far(v) for v in operands[1:3]), *operands[3:6], *(far(v) for v in operands[6:]))


def result_body(out_ref, index_ref, resid_ref, result_ref):
    total = resid_ref[...]
    count = total.shape[0]
    index = index_ref[...]
    for e in range(EXPERTS):
        row = iota((ROWS, count), 0) + e * ROWS
        pick = (row == index[0:1, :]) | (row == index[1:2, :])
        total = total + dot_tn(jnp.where(pick, 1.0, 0.0).astype(BF), out_ref[e])
    result_ref[0] = total.astype(BF)


def combine(out, index, resid):
    count, width = resid.shape
    return pl.pallas_call(
        result_body,
        out_shape=jax.ShapeDtypeStruct((1, count, width), BF),
        in_specs=vmem(3),
        out_specs=vmem(1)[0],
        compiler_params=params(8),
        cost_estimate=SMALL,
        name="combine",
    )(far(out), index, far(resid))


def plain(body, outs, *operands):
    return pl.pallas_call(
        body,
        out_shape=tuple(outs) if len(outs) > 1 else outs[0],
        in_specs=vmem(len(operands)),
        out_specs=tuple(vmem(len(outs))) if len(outs) > 1 else vmem(1)[0],
        compiler_params=params(16),
        cost_estimate=SMALL,
        name=body.__name__,
    )(*operands)


def first_sums(stay0_ref, come0_ref, stay1_ref, come1_ref, keep_ref, go0_ref, go1_ref):
    for half, (stay, come, go) in enumerate(
        ((stay0_ref, come0_ref, go0_ref), (stay1_ref, come1_ref, go1_ref))
    ):
        keep_ref[half] = (stay[0].astype(F32) + come[0].astype(F32)).astype(BF)
        go[...] = (stay[1].astype(F32) + come[1].astype(F32)).astype(BF)


def second_sums(keep_ref, come0_ref, come1_ref, sum_ref):
    for half, come in enumerate((come0_ref, come1_ref)):
        sum_ref[half] = (keep_ref[half].astype(F32) + come[...].astype(F32)).astype(BF)


def pair_sum(a_ref, b_ref, sum_ref):
    sum_ref[...] = (a_ref[...].astype(F32) + b_ref[...].astype(F32)).astype(BF)


def lead_sum(parts_ref, sum_ref):
    total = parts_ref[0].astype(F32)
    for i in range(1, parts_ref.shape[0]):
        total = total + parts_ref[i].astype(F32)
    sum_ref[...] = total.astype(BF)


def widen_body(every_ref, w_in_ref, w_out_ref):
    cols = every_ref.shape[-1]
    for half in range(2):
        span = slice(half * cols, (half + 1) * cols)
        w_in_ref[0, :, span] = every_ref[0, half, 0].astype(F32)
        w_out_ref[0, :, span] = every_ref[0, half, 1].astype(F32)


def widen(every, owned):
    reps, _, _, depth, cols = every.shape
    out = pltpu.HBM((owned, depth * (reps // owned), 2 * cols), F32)
    spot = pl.BlockSpec((1, depth, 2 * cols), lambda i: (i % owned, i // owned, 0))
    return pl.pallas_call(
        widen_body,
        out_shape=(out, out),
        grid=(reps,),
        in_specs=[pl.BlockSpec((1, *every.shape[1:]), lambda i: (i, 0, 0, 0, 0))],
        out_specs=(spot, spot),
        compiler_params=params(12),
        cost_estimate=SMALL,
        name="widen",
    )(far(every))


def finish_body(rows, parts_ref, qkv_ref, out_ref, router_ref, gains_ref):
    reps = parts_ref.shape[0]
    depth = out_ref.shape[0]
    smalls = []
    for r in range(reps):
        for s in range(3):
            qkv_ref[s, r * rows : (r + 1) * rows, :] = parts_ref[
                r, s * rows : (s + 1) * rows, :
            ].astype(F32)
        out_ref[r * rows : (r + 1) * rows, :] = parts_ref[r, 3 * rows : 4 * rows, :].astype(F32)
        smalls.append(parts_ref[r].astype(F32)[4 * rows : 4 * rows + 2, 0:depth])
    small = jnp.concatenate(smalls, axis=0)
    router_ref[...] = small[0:EXPERTS]
    gains_ref[...] = small[EXPERTS : EXPERTS + 2]


def finish(parts, rows):
    reps, _, width = parts.shape
    depth = rows * reps
    return pl.pallas_call(
        lambda *refs: finish_body(rows, *refs),
        out_shape=(
            jax.ShapeDtypeStruct((3, depth, width), F32),
            jax.ShapeDtypeStruct((depth, width), F32),
            jax.ShapeDtypeStruct((EXPERTS, depth), F32),
            jax.ShapeDtypeStruct((2, depth), F32),
        ),
        in_specs=vmem(1),
        out_specs=tuple(vmem(4)),
        compiler_params=params(4),
        name="finish",
    )(parts)


def shards(reps, shards_n, *args):
    tokens, segments, choices, priority, cotangent = args[:5]
    qkv_weights, out_weight, router_weight, gains, w_in, w_out = args[5:]
    rep, shard = lax.axis_index("rep"), lax.axis_index("shard")
    width, hidden = w_in.shape[1:]
    owned = w_in.shape[0]
    peers = reps // owned
    depth = width // shards_n
    fast = depth % (16 * reps) == 0 and depth == 128 and owned == 2 and peers == 4
    if not fast and owned != 1:
        raise NotImplementedError("mesh")
    column = [
        [(c * owned + e % owned) * shards_n + e // owned for e in range(EXPERTS)]
        for c in range(peers)
    ]

    def to_experts(rows):
        return lax.all_to_all(rows, AXES, 0, 0, axis_index_groups=column, tiled=True)

    where = jnp.stack([rep % owned, rep // owned]).astype(jnp.int32)
    index, cot_sent = route(choices[0].T, priority, cotangent)
    if fast:
        smalls, pieces, lines = gather_weights(
            rep, shard, reps, shards_n, qkv_weights, out_weight, router_weight.T, gains
        )
        place = jnp.stack([rep, shard]).astype(jnp.int32)
        weights_in = (qkv_weights, out_weight, smalls)
    else:
        place, pieces, lines = None, [], []
        weights_in = (
            lax.all_gather(qkv_weights, "shard", axis=1, tiled=True),
            lax.all_gather(out_weight, "shard", axis=0, tiled=True),
            lax.all_gather(router_weight, "shard", axis=0, tiled=True).T,
            lax.all_gather(gains, "shard", axis=1, tiled=True),
        )
    cot_in = to_experts(after(cot_sent, *lines))
    sent, small, gates, *kept = forward(
        fast, place, tokens, segments, index, weights_in, pieces
    )
    n2_in = to_experts(sent)

    def peer(value, k):
        return lax.ppermute(value, "rep", [(i, i ^ k) for i in range(reps)])

    back, out, *parts_in = experts(where, n2_in, cot_in, w_in, w_out)
    grads = expert_grads(where, fast, *parts_in)
    back_in = to_experts(back)
    if fast:
        axes = ((owned, 2 * owned), (2 * owned, owned))
        halves = [peer(grads[2 * half], axes[half][0]) for half in range(2)]
        back_in, *halves = lax.optimization_barrier((back_in, *halves))
        part = halves[0].shape[1:]
        small_part = jax.ShapeDtypeStruct(part, BF)
        keep, *leaves = plain(
            first_sums,
            [jax.ShapeDtypeStruct((2, *part), BF), small_part, small_part],
            grads[1],
            halves[0],
            grads[3],
            halves[1],
        )
        arrived = [peer(leaves[half], axes[half][1]) for half in range(2)]
    out_in = to_experts(after(out, back_in))
    grad_tokens, *packs = backward(
        fast,
        reps,
        shards_n,
        where,
        [back_in, tokens, cotangent, index, small, gates, *kept],
    )
    result = combine(out_in, index, kept[5])
    if fast:
        arrived = lax.optimization_barrier((packs[0], out_in, *arrived))[2:]
        total = plain(second_sums, [jax.ShapeDtypeStruct(keep.shape, BF)], keep, *arrived)
        every = lax.all_gather(total, "rep", axis=0, tiled=False)
        mine, twin = packs
        chip = plain(pair_sum, [jax.ShapeDtypeStruct(mine.shape, BF)], mine, peer(twin, 1))
        line = lax.all_to_all(chip, "shard", 0, 0, tiled=True)
        line = after(line, result)
        line = plain(lead_sum, [jax.ShapeDtypeStruct(line.shape[1:], BF)], line)
        plane_groups = [[p * owned + c for p in range(peers)] for c in range(owned)]
        plane = lax.all_to_all(line, "rep", 0, 0, axis_index_groups=plane_groups, tiled=True)
        share = plain(lead_sum, [jax.ShapeDtypeStruct(plane.shape[1:], BF)], plane)
        parts = lax.all_gather(share, "rep", axis=0, tiled=False)
        grad_qkv, grad_out, grad_router, grad_gains = finish(parts, depth // reps)
        grad_router = grad_router.T
        grad_w_in, grad_w_out = widen(every, owned)
    else:
        share = lax.psum_scatter(grads[0], "rep", scatter_dimension=1, tiled=True)
        every = lax.all_gather(share, "rep", axis=1, tiled=True).astype(F32)
        grad_w_in, grad_w_out = every[0:1], every[1:2]
        pack, sums = packs
        owned_rows = lax.psum_scatter(pack, "shard", scatter_dimension=1, tiled=True)
        owned_rows = lax.psum(owned_rows, "rep").astype(F32)
        grad_qkv, grad_out = owned_rows[0:3], owned_rows[3]
        sums = lax.psum(sums, AXES)
        mine = lax.dynamic_slice_in_dim(sums, shard * depth, depth, axis=1)
        grad_router, grad_gains = mine[0:EXPERTS].T, mine[EXPERTS : EXPERTS + 2]
    return (
        result,
        grad_tokens,
        grad_qkv,
        grad_out,
        grad_router,
        grad_gains,
        grad_w_in,
        grad_w_out,
    )


def solution(mesh):
    reps, shards_n = mesh.shape["rep"], mesh.shape["shard"]
    rows = P(("rep", "shard"), None, None)
    flat = P(("rep", "shard"), None)
    first = P("shard", None)
    stack = P("shard", None, None)
    second = P(None, "shard", None)
    return jax.shard_map(
        lambda *args: shards(reps, shards_n, *args),
        mesh=mesh,
        in_specs=(
            rows, flat, rows, flat, rows, second, first, first, P(None, "shard"), stack, stack,
        ),
        out_specs=(rows, rows, second, first, first, P(None, "shard"), stack, stack),
        check_vma=False,
    )
```

```python
import jax
import jax.numpy as jnp
from jax import lax
from jax.experimental import pallas as pl
from jax.experimental.pallas import tpu as pltpu
from jax.sharding import PartitionSpec as P

HEADS = 8
HEAD_DIM = 64
EXPERTS = 8
CAPACITY = 135
ROWS = 144
SLOTS = 136
EPS = 1e-06
F32 = jnp.float32
BF = jnp.bfloat16
AXES = ("rep", "shard")
FF_STEP = 512
KEPT = 7
SMALL = pl.CostEstimate(flops=1000, bytes_accessed=1000, transcendentals=0)
GELU_A = 0.7978845608028654
GELU_B = 0.044715


def dot_nn(a, b):
    return lax.dot_general(a, b, (((1,), (0,)), ((), ())), preferred_element_type=F32)


def dot_nt(a, b):
    return lax.dot_general(a, b, (((1,), (1,)), ((), ())), preferred_element_type=F32)


def dot_tn(a, b):
    return lax.dot_general(a, b, (((0,), (0,)), ((), ())), preferred_element_type=F32)


def after(value, *others):
    return lax.optimization_barrier((value, *others))[0]


def iota(shape, dim):
    return lax.broadcasted_iota(jnp.int32, shape, dim)


def unit_of(values):
    mean = jnp.mean(values, axis=-1, keepdims=True)
    centered = values - mean
    inv = lax.rsqrt(jnp.mean(centered * centered, axis=-1, keepdims=True) + EPS)
    return centered * inv, inv


def split3(values):
    high = values.astype(BF)
    rest = values - high.astype(F32)
    mid = rest.astype(BF)
    low = (rest - mid.astype(F32)).astype(BF)
    return high, mid, low


def piece_rows(values):
    high, mid, low = split3(values)
    shape = (8, values.shape[1])
    row = iota(shape, 0)
    parts = [jnp.broadcast_to(part.astype(F32), shape) for part in (high, mid, low)]
    return jnp.where(
        row == 0, parts[0], jnp.where(row == 1, parts[1], jnp.where(row == 2, parts[2], 0.0))
    )


def far(value):
    return pltpu.with_memory_space_constraint(value, pltpu.HBM)


def near(value):
    return pltpu.with_memory_space_constraint(value, pltpu.VMEM)


def vmem(n):
    return [pl.BlockSpec(memory_space=pltpu.VMEM)] * n


def params(mib):
    return pltpu.CompilerParams(vmem_limit_bytes=mib << 20)


def route_body(choice_ref, prio_ref, cot_ref, index_ref, sent_ref):
    count = cot_ref.shape[-2]
    choice = choice_ref[...]
    experts = iota((EXPERTS, count), 0)
    first = jnp.where(choice[0:1, :] == experts, 1.0, 0.0)
    second = jnp.where(choice[1:2, :] == experts, 1.0, 0.0)
    order = jnp.where(iota((count, count), 0) == prio_ref[...], 1.0, 0.0).astype(BF)
    earlier = jnp.where(iota((count, count), 0) < iota((count, count), 1), 1.0, 0.0).astype(BF)
    both = jnp.concatenate([first, second], axis=0).astype(BF)
    before = dot_nn(dot_nt(both, order).astype(BF), earlier)
    held = jnp.sum(first, axis=1, keepdims=True)
    before = jnp.concatenate([before[0:EXPERTS], before[EXPERTS:] + held], axis=0)
    before = dot_nn(jnp.minimum(before, 255.0).astype(BF), order)
    slot0 = jnp.sum(first * before[0:EXPERTS], axis=0, keepdims=True)
    slot1 = jnp.sum(second * before[EXPERTS:], axis=0, keepdims=True)
    slot = jnp.concatenate([slot0, slot1], axis=0).astype(jnp.int32)
    index = jnp.where(slot < CAPACITY, choice * ROWS + slot, -1)
    index_ref[...] = index
    cot = cot_ref[0]
    for e in range(EXPERTS):
        row = iota((ROWS, count), 0) + e * ROWS
        pick = (row == index[0:1, :]) | (row == index[1:2, :])
        sent_ref[e] = dot_nn(jnp.where(pick, 1.0, 0.0).astype(BF), cot).astype(BF)


def route(choice_t, prio, cot):
    _, count, width = cot.shape
    return pl.pallas_call(
        route_body,
        out_shape=(
            jax.ShapeDtypeStruct((2, count), jnp.int32),
            pltpu.HBM((EXPERTS, ROWS, width), BF),
        ),
        in_specs=vmem(3),
        out_specs=tuple(vmem(2)),
        compiler_params=params(12),
        cost_estimate=SMALL,
        name="route",
    )(far(choice_t), far(prio), far(cot))


def pack_body(where_ref, qkv_ref, out_ref, router_ref, gains_ref, pack_ref):
    rows = pack_ref.shape[1]
    start = pl.multiple_of(where_ref[0] * rows, rows)
    for s in range(3):
        pack_ref[s] = qkv_ref[s, pl.ds(start, rows), :]
    pack_ref[3] = out_ref[pl.ds(start, rows), :]
    depth = router_ref.shape[1]
    small = jnp.concatenate(
        [router_ref[...].astype(F32), gains_ref[...].astype(F32), jnp.zeros((6, depth), F32)],
        axis=0,
    )
    pack_ref[4, :, 0:depth] = small.astype(BF)
    pack_ref[4, :, depth:] = jnp.zeros((rows, pack_ref.shape[2] - depth), BF)


def pack_weights(rep, qkv, out, router, gains, rows):
    width = out.shape[1]
    return pl.pallas_call(
        pack_body,
        out_shape=jax.ShapeDtypeStruct((5, rows, width), BF),
        in_specs=[pl.BlockSpec(memory_space=pltpu.SMEM)] + vmem(4),
        out_specs=vmem(1)[0],
        compiler_params=params(4),
        name="pack_weights",
    )(rep.reshape(1), far(qkv), far(out), far(router), far(gains))


def gather_weights(rep, shard, reps, shards_n, qkv, out, router, gains):
    rows = qkv.shape[1] // reps
    pack = pack_weights(rep, qkv, out, router, gains, rows)
    lines = [
        lax.ppermute(pack, "shard", [(i, i ^ dz) for i in range(shards_n)])
        for dz in range(1, shards_n)
    ]
    block = jnp.stack([piece[0:4] for piece in lines])
    smalls = jnp.stack([piece[4] for piece in [pack] + lines])
    spread = [block] + [
        lax.ppermute(block, "rep", [(i, i ^ k) for i in range(reps)]) for k in range(2, reps, 2)
    ]
    twin = [lax.ppermute(piece, "rep", [(i, i ^ 1) for i in range(reps)]) for piece in spread]
    pieces = []
    for own, other in zip(spread, twin, strict=True):
        pieces += [own, other]
    return smalls, pieces, lines


def fill_weights(rep, shard, qkv_ref, out_ref, smalls_ref, piece_refs, full_ref, small_ref):
    depth = out_ref.shape[0]
    own = pl.multiple_of(shard * depth, depth)
    for s in range(3):
        full_ref[s, pl.ds(own, depth), :] = qkv_ref[s]
    full_ref[3, pl.ds(own, depth), :] = out_ref[...]
    small_ref[:, pl.ds(own, depth)] = smalls_ref[0, :, 0:depth]
    for far in range(1, smalls_ref.shape[0]):
        base = pl.multiple_of((shard ^ far) * depth, depth)
        small_ref[:, pl.ds(base, depth)] = smalls_ref[far, :, 0:depth]
        for k, piece in enumerate(piece_refs):
            rows = piece.shape[2]
            start = pl.multiple_of(base + (rep ^ k) * rows, rows)
            for s in range(4):
                full_ref[s, pl.ds(start, rows), :] = piece[far - 1, s]


def head_masks(count):
    lane = iota((count, 2 * HEAD_DIM), 1)
    return [lane < HEAD_DIM, lane >= HEAD_DIM]


def kept_shapes(count, width):
    return (
        ((4, width, width), BF),
        ((HEADS, count, count), BF),
        ((3, count, width), BF),
        ((count, width), BF),
        ((count, width), BF),
        ((count, width), F32),
        ((count, width), BF),
    )


def forward_body(fast, n_pieces, *refs):
    if fast:
        where_ref, x_ref, seg_ref, index_ref, qkv_ref, out_ref, smalls_ref = refs[:7]
        piece_refs = refs[7 : 7 + n_pieces]
        refs = refs[7 + n_pieces :]
    else:
        x_ref, seg_ref, index_ref, qkv_ref, out_ref, router_ref, gains_ref = refs[:7]
        refs = refs[7:]
    sent_ref, small_ref, gate_ref, *kept = refs[: 3 + KEPT]
    full_ref, weights_ref, proj_ref, n1_ref, mixed_ref, resid_ref, n2_ref = held = refs[3 + KEPT : -1]
    sem = refs[-1]

    def keep(*which):
        for i in which:
            pltpu.make_async_copy(held[i], kept[i], sem.at[i]).start()

    if fast:
        fill_weights(
            where_ref[0], where_ref[1], qkv_ref, out_ref, smalls_ref, piece_refs, full_ref, small_ref
        )
    else:
        full_ref[0:3] = qkv_ref[...]
        full_ref[3] = out_ref[...]
        small_ref[...] = jnp.concatenate(
            [
                router_ref[...].astype(F32),
                gains_ref[...].astype(F32),
                jnp.zeros((6, out_ref.shape[1]), F32),
            ],
            axis=0,
        ).astype(BF)
    keep(0)
    x = x_ref[0].astype(F32)
    count, width = x.shape
    small = small_ref[...].astype(F32)
    unit1, _ = unit_of(x)
    n1 = (unit1 * small[8:9, :]).astype(BF)
    n1_ref[...] = n1
    for s in range(3):
        proj_ref[s] = dot_nn(n1, full_ref[s]).astype(BF)
    keep(2, 3)
    document = jnp.where(iota((8, count), 0) == seg_ref[...], 1.0, 0.0).astype(BF)
    bias = jnp.where(dot_tn(document, document) > 0.5, 0.0, -1e30)
    masks = head_masks(count)
    for pair in range(HEADS // 2):
        lanes = slice(pair * 2 * HEAD_DIM, (pair + 1) * 2 * HEAD_DIM)
        q, k, v = proj_ref[0, :, lanes], proj_ref[1, :, lanes], proj_ref[2, :, lanes]
        q = q * BF(HEAD_DIM**-0.5)
        halves = []
        for half in range(2):
            scores = dot_nt(jnp.where(masks[half], q, BF(0)), k) + bias
            top = jnp.max(scores, axis=-1, keepdims=True)
            terms = jnp.exp(scores - top)
            total = jnp.sum(terms, axis=-1, keepdims=True)
            weights = (terms * (1.0 / total)).astype(BF)
            weights_ref[2 * pair + half] = weights
            halves.append(dot_nn(weights, v))
        mixed_ref[:, lanes] = jnp.where(masks[0], halves[0], halves[1]).astype(BF)
    keep(1, 4)
    resid = x + dot_nn(mixed_ref[...], full_ref[3])
    resid_ref[...] = resid
    keep(5)
    unit2, _ = unit_of(resid)
    n2 = (unit2 * small[9:10, :]).astype(BF)
    n2_ref[...] = n2
    keep(6)
    logits = dot_nt(small_ref[...], n2)[0:EXPERTS]
    terms = jnp.exp(logits - jnp.max(logits, axis=0, keepdims=True))
    gates = terms / jnp.sum(terms, axis=0, keepdims=True)
    gate_ref[...] = gates
    index = index_ref[...]
    for e in range(EXPERTS):
        row = iota((ROWS, count), 0) + e * ROWS
        pick = (row == index[0:1, :]) | (row == index[1:2, :])
        pick = jnp.where(pick, 1.0, 0.0).astype(BF)
        rows = dot_nn(pick, n2)
        side = dot_nt(piece_rows(gates[e : e + 1, :]).astype(BF), pick)
        side = jnp.concatenate([side, jnp.zeros((8, width - ROWS), F32)], axis=1)
        sent_ref[e] = jnp.concatenate([rows[0:SLOTS], side], axis=0).astype(BF)
    for i in range(KEPT):
        pltpu.make_async_copy(held[i], kept[i], sem.at[i]).wait()


def forward(fast, where, x, seg, index, weights_in, pieces):
    _, count, width = x.shape
    body = lambda *refs: forward_body(fast, len(pieces), *refs)
    operands = [far(x), far(seg), index, *(far(w) for w in weights_in[:2]), *weights_in[2:], *pieces]
    specs = vmem(len(operands))
    if fast:
        operands = [where] + operands
        specs = [pl.BlockSpec(memory_space=pltpu.SMEM)] + specs
    shown = (
        pltpu.HBM((EXPERTS, ROWS, width), BF),
        jax.ShapeDtypeStruct((16, width), BF),
        jax.ShapeDtypeStruct((EXPERTS, count), F32),
    )
    kept = kept_shapes(count, width)
    return pl.pallas_call(
        body,
        out_shape=(*shown, *(pltpu.HBM(*k) for k in kept)),
        in_specs=specs,
        out_specs=(*vmem(3), *([pl.BlockSpec(memory_space=pltpu.HBM)] * KEPT)),
        scratch_shapes=[*(pltpu.VMEM(*k) for k in kept), pltpu.SemaphoreType.DMA((KEPT,))],
        compiler_params=params(40),
        cost_estimate=SMALL,
        name="forward",
    )(*operands)


def cot_hidden_body(where_ref, cot_ref, w_out_ref, through_ref):
    rows = jnp.concatenate([cot_ref[0], cot_ref[1]], axis=0)
    for start in range(0, w_out_ref.shape[2], FF_STEP):
        cols = slice(start, start + FF_STEP)
        through_ref[:, cols] = dot_nn(rows, w_out_ref[0, :, cols])


def cot_hidden(where, cot, w_out):
    groups, _, width = cot.shape
    hidden_n = w_out.shape[2]
    return pl.pallas_call(
        cot_hidden_body,
        out_shape=pltpu.HBM((groups * ROWS, hidden_n), F32),
        grid_spec=pltpu.PrefetchScalarGridSpec(
            num_scalar_prefetch=1,
            grid=(groups // 2,),
            in_specs=[
                pl.BlockSpec((2, ROWS, width), lambda i, w: (i, 0, 0)),
                pl.BlockSpec((1, width, hidden_n), lambda i, w: (w[0], 0, 0)),
            ],
            out_specs=pl.BlockSpec((2 * ROWS, hidden_n), lambda i, w: (i, 0)),
        ),
        compiler_params=params(24),
        cost_estimate=SMALL,
        name="cot_hidden",
    )(where, cot, far(w_out))


def expert_rows(n2_ref, cot_ref, through_ref, w_in_ref, w_out_ref, back_ref, out_ref, span, scratch):
    hidden_ref, pre_ref, rows_ref, gso_ref = scratch
    row = iota((ROWS, 1), 0)
    eye = jnp.where(iota((ROWS, ROWS), 0) == iota((ROWS, ROWS), 1), 1.0, 0.0).astype(BF)
    gates, rows_all, gso_all = [], [], []
    for g in range(2):
        rows = n2_ref[g]
        side = rows.astype(F32)[SLOTS:, 0:ROWS].astype(BF)
        gate = jnp.sum(dot_nt(eye, side), axis=1, keepdims=True)
        gates.append(gate)
        rows_all.append(jnp.where(row < SLOTS, rows, BF(0)))
        gso_all.append((gate * cot_ref[g].astype(F32)).astype(BF))
    rows, gate_col = jnp.concatenate(rows_all, axis=0), jnp.concatenate(gates, axis=0)
    rows_ref[span], gso_ref[span] = rows, jnp.concatenate(gso_all, axis=0)
    for start in range(0, w_in_ref.shape[2], FF_STEP):
        cols = slice(start, start + FF_STEP)
        u = dot_nn(rows, w_in_ref[0, :, cols])
        square = u * u
        t = jnp.tanh(GELU_A * (u + GELU_B * (u * square)))
        half = 0.5 * (1.0 + t)
        hidden = u * half
        slope = half + hidden * (1.0 - t) * (GELU_A * (1.0 + 3.0 * GELU_B * square))
        hidden_ref[span, cols] = hidden.astype(BF)
        pre_ref[span, cols] = (through_ref[:, cols] * (gate_col * slope)).astype(BF)
    grad_in = dot_nt(pre_ref[span], w_in_ref[0])
    result = dot_nt(hidden_ref[span], w_out_ref[0])
    ones = jnp.ones((8, rows.shape[1]), BF)
    for g in range(2):
        part = slice(g * ROWS, (g + 1) * ROWS)
        out = (gates[g] * result[part]).astype(BF)
        out_ref[g] = out
        product = out.astype(F32) * cot_ref[g].astype(F32)
        high = product.astype(BF)
        low = (product - high.astype(F32)).astype(BF)
        inner = dot_nt(ones, high) + dot_nt(ones, low)
        side = piece_rows(inner[0:1, :])
        side = jnp.concatenate([side, jnp.zeros((8, out.shape[1] - ROWS), F32)], axis=1)
        back_ref[g] = jnp.concatenate([grad_in[part][0:SLOTS], side], axis=0).astype(BF)


def experts_body(where_ref, *refs):
    expert_rows(*refs[:7], slice(None), refs[7:])


def experts(where, n2, cot, through, w_in, w_out):
    groups, _, width = n2.shape
    hidden_n = w_in.shape[2]
    total = groups * ROWS
    weight = pl.BlockSpec((1, width, hidden_n), lambda i, w: (w[0], 0, 0))
    payload = pl.BlockSpec((2, ROWS, width), lambda i, w: (i, 0, 0))
    narrow = pl.BlockSpec((2 * ROWS, width), lambda i, w: (i, 0))
    wide = pl.BlockSpec((2 * ROWS, hidden_n), lambda i, w: (i, 0))
    return pl.pallas_call(
        experts_body,
        out_shape=(
            [pltpu.HBM((groups, ROWS, width), BF)] * 2
            + [pltpu.HBM((total, hidden_n), BF)] * 2
            + [pltpu.HBM((total, width), BF)] * 2
        ),
        grid_spec=pltpu.PrefetchScalarGridSpec(
            num_scalar_prefetch=1,
            grid=(groups // 2,),
            in_specs=[payload, payload, wide, weight, weight],
            out_specs=[payload, payload, wide, wide, narrow, narrow],
        ),
        compiler_params=params(44),
        cost_estimate=SMALL,
        name="experts",
    )(where, n2, cot, through, far(w_in), far(w_out))


def expert_grads_body(split, where_ref, hidden_ref, pre_ref, rows_ref, gso_ref, *refs):
    grad_refs, sum_ref = refs[:-1], refs[-1]
    step, steps = pl.program_id(0), pl.num_programs(0)
    for half, (left, right) in enumerate(((rows_ref, pre_ref), (gso_ref, hidden_ref))):
        grad = dot_tn(left[...], right[...]).astype(BF)
        if not split:
            grad_refs[0][half] = grad
            continue
        sum_ref[half] = grad
    if not split:
        return
    depth = sum_ref.shape[1] // 4
    for late in range(2):

        @pl.when((step < steps // 2) if late == 0 else (step >= steps // 2))
        def _(late=late):
            for half in range(2):
                for k in range(4):
                    start = pl.multiple_of((where_ref[1] ^ k) * depth, depth)
                    goes = k == 3 or k == 1 + late
                    ref = grad_refs[2 * late + (0 if goes else 1)]
                    ref[int(k == 3 or k == 2 - late), half] = sum_ref[half, pl.ds(start, depth), :]


def expert_grads(where, split, hidden, pre, rows, gso):
    total, width = rows.shape
    hidden_n = hidden.shape[1]
    steps = hidden_n // FF_STEP
    narrow = pl.BlockSpec((total, width), lambda i, w: (0, 0))
    wide = pl.BlockSpec((total, FF_STEP), lambda i, w: (0, i))
    if split:
        part = (2, 2, width // 4, FF_STEP)
        first = pl.BlockSpec(part, lambda i, w: (0, 0, 0, jnp.minimum(i, steps // 2 - 1)))
        second = pl.BlockSpec(part, lambda i, w: (0, 0, 0, jnp.maximum(i - steps // 2, 0)))
        grad_specs = [first, first, second, second]
        grad_shapes = [jax.ShapeDtypeStruct((2, 2, width // 4, hidden_n // 2), BF)] * 4
    else:
        grad_specs = [pl.BlockSpec((2, width, FF_STEP), lambda i, w: (0, 0, i))]
        grad_shapes = [pltpu.HBM((2, width, hidden_n), BF)]
    return pl.pallas_call(
        lambda *refs: expert_grads_body(split, *refs),
        out_shape=grad_shapes,
        grid_spec=pltpu.PrefetchScalarGridSpec(
            num_scalar_prefetch=1,
            grid=(steps,),
            in_specs=[wide, wide, narrow, narrow],
            out_specs=grad_specs,
            scratch_shapes=[pltpu.VMEM((2, width, FF_STEP), BF)],
        ),
        compiler_params=params(30),
        cost_estimate=SMALL,
        name="expert_grads",
    )(where, far(hidden), far(pre), far(rows), far(gso))


def place_grads(fast, reps, shards_n, pack_ref, which, grad):
    if not fast:
        pack_ref[which] = grad.astype(BF)
        return
    width = grad.shape[0]
    depth = width // shards_n
    rows = depth // reps
    grad = grad.astype(BF)
    for z in range(shards_n):
        for r in range(reps):
            start = z * depth + r * rows
            span = slice(which * rows, (which + 1) * rows)
            pack_ref[r % 2, z, r // 2, span, :] = grad[start : start + rows]


def backward_body(fast, reps, shards_n, where_ref, *refs):
    core = where_ref[0]
    back_ref, x_ref, cot_ref, index_ref, small_ref, gate_ref, *kept = refs[: 6 + KEPT]
    if fast:
        grad_x_ref, mine_ref, twin_ref, pack_ref, gp_ref = refs[6 + KEPT : 11 + KEPT]
        refs = refs[11 + KEPT :]
    else:
        grad_x_ref, pack_ref, sums_ref, gp_ref = refs[6 + KEPT : 10 + KEPT]
        refs = refs[10 + KEPT :]
    full_ref, weights_ref, proj_ref, n1_ref, mixed_ref, resid_ref, n2_ref = held = refs[:-1]
    sem = refs[-1]
    for i in (5, 6, 4, 0, 2, 1, 3):
        pltpu.make_async_copy(kept[i], held[i], sem.at[i]).start()

    def need(*which):
        for i in which:
            pltpu.make_async_copy(kept[i], held[i], sem.at[i]).wait()

    count, width = resid_ref.shape
    small = small_ref[...].astype(F32)
    index = index_ref[...]
    gates = gate_ref[...]
    grad_n2 = jnp.zeros((count, width), F32)
    rows_h = []
    for e in range(EXPERTS):
        row = iota((ROWS, count), 0) + e * ROWS
        pick = (row == index[0:1, :]) | (row == index[1:2, :])
        pick = jnp.where(pick, 1.0, 0.0).astype(BF)
        back = back_ref[e]
        side = back.astype(F32)[SLOTS:, 0:ROWS].astype(BF)
        rows_h.append(jnp.sum(dot_nn(side, pick), axis=0, keepdims=True))
        grad_n2 = grad_n2 + dot_tn(pick, back)
    inner = jnp.concatenate(rows_h, axis=0)
    grad_logits = (inner - gates * jnp.sum(inner, axis=0, keepdims=True)).astype(BF)
    wide_logits = jnp.concatenate(
        [grad_logits.astype(F32), jnp.zeros((8, count), F32)], axis=0
    ).astype(BF)
    grad_n2 = grad_n2 + dot_tn(wide_logits, small_ref[...])
    need(5, 6)
    grad_router = dot_nn(wide_logits, n2_ref[...])[0:EXPERTS]
    unit2, inv2 = unit_of(resid_ref[...])
    grad_gain2 = jnp.sum(grad_n2 * unit2, axis=0, keepdims=True)
    a = grad_n2 * small[9:10, :]
    grad_resid = cot_ref[0].astype(F32) + inv2 * (
        a
        - jnp.mean(a, axis=-1, keepdims=True)
        - unit2 * jnp.mean(a * unit2, axis=-1, keepdims=True)
    )
    branch = grad_resid.astype(BF)
    need(4, 0)
    place_grads(fast, reps, shards_n, pack_ref, 3, dot_tn(mixed_ref[...], branch))
    grad_mixed = dot_nt(branch, full_ref[3]).astype(BF)
    need(2, 1)
    masks = head_masks(count)
    factor = HEAD_DIM**-0.5
    for pair in range(HEADS // 2):
        lanes = slice(pair * 2 * HEAD_DIM, (pair + 1) * 2 * HEAD_DIM)
        q, k, v = proj_ref[0, :, lanes], proj_ref[1, :, lanes], proj_ref[2, :, lanes]
        gm = grad_mixed[:, lanes]
        parts = []
        for half in range(2):
            weights = weights_ref[2 * pair + half]
            probs = weights.astype(F32)
            grad_probs = dot_nt(jnp.where(masks[half], gm, BF(0)), v)
            total = jnp.sum(probs * grad_probs, axis=-1, keepdims=True)
            grad_scores = (probs * (grad_probs - total)).astype(BF)
            parts.append(
                (dot_nn(grad_scores, k), dot_tn(grad_scores, q), dot_tn(weights, gm))
            )
        for s in range(3):
            both = jnp.where(masks[0], parts[0][s], parts[1][s])
            gp_ref[s, :, lanes] = (both * factor if s < 2 else both).astype(BF)
    need(3)
    n1 = n1_ref[...]
    grad_n1 = jnp.zeros((count, width), F32)
    for s in range(3):
        grads = gp_ref[s]
        place_grads(fast, reps, shards_n, pack_ref, s, dot_tn(n1, grads))
        grad_n1 = grad_n1 + dot_nt(grads, full_ref[s])
    unit1, inv1 = unit_of(x_ref[0].astype(F32))
    grad_gain1 = jnp.sum(grad_n1 * unit1, axis=0, keepdims=True)
    b = grad_n1 * small[8:9, :]
    grad_x = grad_resid + inv1 * (
        b
        - jnp.mean(b, axis=-1, keepdims=True)
        - unit1 * jnp.mean(b * unit1, axis=-1, keepdims=True)
    )
    grad_x_ref[0] = grad_x.astype(BF)
    sums = jnp.concatenate(
        [grad_router, grad_gain1, grad_gain2, jnp.zeros((6, width), F32)], axis=0
    )
    if not fast:
        sums_ref[...] = sums
        return
    depth = width // shards_n
    rows = depth // reps
    for z in range(shards_n):
        for r in range(reps):
            two = sums[2 * r : 2 * r + 2, z * depth : (z + 1) * depth]
            two = jnp.concatenate([two, jnp.zeros((6, depth), F32)], axis=0)
            two = jnp.concatenate([two, jnp.zeros((8, width - depth), F32)], axis=1)
            pack_ref[r % 2, z, r // 2, 4 * rows :, :] = two.astype(BF)
    copies = [
        pltpu.make_async_copy(pack_ref.at[core ^ i], (mine_ref, twin_ref)[i], sem.at[i])
        for i in range(2)
    ]
    for copy in copies:
        copy.start()
    for copy in copies:
        copy.wait()


def backward(fast, reps, shards_n, where, operands):
    x = operands[1]
    _, count, width = x.shape
    outs = [jax.ShapeDtypeStruct(x.shape, BF)]
    scratch = [pltpu.VMEM((3, count, width), BF)]
    if fast:
        part = (shards_n, reps // 2, 4 * (width // shards_n // reps) + 8, width)
        outs += [pltpu.HBM(part, BF)] * 2
        out_specs = vmem(1) + [pl.BlockSpec(memory_space=pltpu.HBM)] * 2
        scratch = [pltpu.VMEM((2, *part), BF)] + scratch
    else:
        outs += [
            jax.ShapeDtypeStruct((4, width, width), BF),
            jax.ShapeDtypeStruct((16, width), F32),
        ]
        out_specs = vmem(3)
    return pl.pallas_call(
        lambda *refs: backward_body(fast, reps, shards_n, *refs),
        out_shape=tuple(outs),
        in_specs=[pl.BlockSpec(memory_space=pltpu.SMEM)]
        + vmem(len(operands) - KEPT)
        + [pl.BlockSpec(memory_space=pltpu.HBM)] * KEPT,
        out_specs=tuple(out_specs),
        scratch_shapes=[
            *scratch,
            *(pltpu.VMEM(*k) for k in kept_shapes(count, width)),
            pltpu.SemaphoreType.DMA((KEPT,)),
        ],
        compiler_params=params(40),
        cost_estimate=SMALL,
        name="backward",
    )(where, operands[0], *(far(v) for v in operands[1:3]), *operands[3:6], *(far(v) for v in operands[6:]))


def result_body(out_ref, index_ref, resid_ref, result_ref):
    total = resid_ref[...]
    count = total.shape[0]
    index = index_ref[...]
    for e in range(EXPERTS):
        row = iota((ROWS, count), 0) + e * ROWS
        pick = (row == index[0:1, :]) | (row == index[1:2, :])
        total = total + dot_tn(jnp.where(pick, 1.0, 0.0).astype(BF), out_ref[e])
    result_ref[0] = total.astype(BF)


def combine(out, index, resid):
    count, width = resid.shape
    return pl.pallas_call(
        result_body,
        out_shape=jax.ShapeDtypeStruct((1, count, width), BF),
        in_specs=vmem(3),
        out_specs=vmem(1)[0],
        compiler_params=params(8),
        cost_estimate=SMALL,
        name="combine",
    )(far(out), index, far(resid))


def plain(body, outs, *operands):
    return pl.pallas_call(
        body,
        out_shape=tuple(outs) if len(outs) > 1 else outs[0],
        in_specs=vmem(len(operands)),
        out_specs=tuple(vmem(len(outs))) if len(outs) > 1 else vmem(1)[0],
        compiler_params=params(16),
        cost_estimate=SMALL,
        name=body.__name__,
    )(*operands)


def first_sums(stay0_ref, come0_ref, stay1_ref, come1_ref, keep_ref, go0_ref, go1_ref):
    for half, (stay, come, go) in enumerate(
        ((stay0_ref, come0_ref, go0_ref), (stay1_ref, come1_ref, go1_ref))
    ):
        keep_ref[half] = (stay[0].astype(F32) + come[0].astype(F32)).astype(BF)
        go[...] = (stay[1].astype(F32) + come[1].astype(F32)).astype(BF)


def second_sums(keep_ref, come0_ref, come1_ref, sum_ref):
    for half, come in enumerate((come0_ref, come1_ref)):
        sum_ref[half] = (keep_ref[half].astype(F32) + come[...].astype(F32)).astype(BF)


def pair_sum(a_ref, b_ref, sum_ref):
    sum_ref[...] = (a_ref[...].astype(F32) + b_ref[...].astype(F32)).astype(BF)


def lead_sum(parts_ref, sum_ref):
    total = parts_ref[0].astype(F32)
    for i in range(1, parts_ref.shape[0]):
        total = total + parts_ref[i].astype(F32)
    sum_ref[...] = total.astype(BF)


def widen_body(places, aliased, where_ref, *refs):
    n = len(places)
    taken, wide, sem_in, sem_out = refs[-4:]
    outs = refs[-6:-4]
    srcs = refs[: len(refs) - 6 - 2 * aliased]
    _, depth, cols = srcs[0].shape[-3:]
    pieces = [ref.at[half] for ref in srcs for half in range(2)] if len(srcs) < n else srcs
    fetch = [pltpu.make_async_copy(pieces[i], taken.at[i], sem_in.at[i]) for i in range(n)]
    for copy in fetch:
        copy.start()
    sent = []
    for i, (other, k, half) in enumerate(places):
        fetch[i].wait()
        row = pl.multiple_of((where_ref[1] ^ k) * depth, depth)
        for which in range(2):
            wide[i, which] = taken[i, which].astype(F32)
            spot = outs[which].at[
                where_ref[0] ^ other, pl.ds(row, depth), half * cols : (half + 1) * cols
            ]
            copy = pltpu.make_async_copy(wide.at[i, which], spot, sem_out.at[i, which])
            copy.start()
            sent.append(copy)
    for copy in sent:
        copy.wait()


def widen(where, places, sources, shape, so_far=None):
    n = len(places)
    part = sources[0].shape[-3:]
    aliased = so_far is not None
    held = pl.BlockSpec(memory_space=pltpu.HBM)
    operands = [far(source) for source in sources] + (list(so_far) if aliased else [])
    return pl.pallas_call(
        lambda *refs: widen_body(places, aliased, *refs),
        out_shape=(pltpu.HBM(shape, F32), pltpu.HBM(shape, F32)),
        in_specs=[pl.BlockSpec(memory_space=pltpu.SMEM)] + [held] * len(operands),
        out_specs=(held, held),
        scratch_shapes=[
            pltpu.VMEM((n, *part), BF),
            pltpu.VMEM((n, *part), F32),
            pltpu.SemaphoreType.DMA((n,)),
            pltpu.SemaphoreType.DMA((n, 2)),
        ],
        input_output_aliases={len(sources) + 1: 0, len(sources) + 2: 1} if aliased else {},
        compiler_params=params(24),
        cost_estimate=SMALL,
        name="widen",
    )(where, *operands)


def finish_body(rows, parts_ref, qkv_ref, out_ref, router_ref, gains_ref):
    reps = parts_ref.shape[0]
    depth = out_ref.shape[0]
    smalls = []
    for r in range(reps):
        for s in range(3):
            qkv_ref[s, r * rows : (r + 1) * rows, :] = parts_ref[
                r, s * rows : (s + 1) * rows, :
            ].astype(F32)
        out_ref[r * rows : (r + 1) * rows, :] = parts_ref[r, 3 * rows : 4 * rows, :].astype(F32)
        smalls.append(parts_ref[r].astype(F32)[4 * rows : 4 * rows + 2, 0:depth])
    small = jnp.concatenate(smalls, axis=0)
    router_ref[...] = small[0:EXPERTS]
    gains_ref[...] = small[EXPERTS : EXPERTS + 2]


def finish(parts, rows):
    reps, _, width = parts.shape
    depth = rows * reps
    return pl.pallas_call(
        lambda *refs: finish_body(rows, *refs),
        out_shape=(
            jax.ShapeDtypeStruct((3, depth, width), F32),
            jax.ShapeDtypeStruct((depth, width), F32),
            jax.ShapeDtypeStruct((EXPERTS, depth), F32),
            jax.ShapeDtypeStruct((2, depth), F32),
        ),
        in_specs=vmem(1),
        out_specs=tuple(vmem(4)),
        compiler_params=params(4),
        name="finish",
    )(parts)


def shards(reps, shards_n, *args):
    tokens, segments, choices, priority, cotangent = args[:5]
    qkv_weights, out_weight, router_weight, gains, w_in, w_out = args[5:]
    rep, shard = lax.axis_index("rep"), lax.axis_index("shard")
    width, hidden = w_in.shape[1:]
    owned = w_in.shape[0]
    peers = reps // owned
    depth = width // shards_n
    fast = depth % (16 * reps) == 0 and depth == 128 and owned == 2 and peers == 4
    if not fast and owned != 1:
        raise NotImplementedError("mesh")
    column = [
        [(c * owned + e % owned) * shards_n + e // owned for e in range(EXPERTS)]
        for c in range(peers)
    ]

    def to_experts(rows):
        return lax.all_to_all(rows, AXES, 0, 0, axis_index_groups=column, tiled=True)

    where = jnp.stack([rep % owned, rep // owned]).astype(jnp.int32)
    index, cot_sent = route(choices[0].T, priority, cotangent)
    if fast:
        smalls, pieces, lines = gather_weights(
            rep, shard, reps, shards_n, qkv_weights, out_weight, router_weight.T, gains
        )
        place = jnp.stack([rep, shard]).astype(jnp.int32)
        weights_in = (qkv_weights, out_weight, smalls)
    else:
        place, pieces, lines = None, [], []
        weights_in = (
            lax.all_gather(qkv_weights, "shard", axis=1, tiled=True),
            lax.all_gather(out_weight, "shard", axis=0, tiled=True),
            lax.all_gather(router_weight, "shard", axis=0, tiled=True).T,
            lax.all_gather(gains, "shard", axis=1, tiled=True),
        )
    cot_in = to_experts(after(cot_sent, *lines))
    sent, small, gates, *kept = forward(
        fast, place, tokens, segments, index, weights_in, pieces
    )
    n2_in = to_experts(sent)

    def peer(value, k):
        return lax.ppermute(value, "rep", [(i, i ^ k) for i in range(reps)])

    through = cot_hidden(where, cot_in, w_out)
    back, out, *parts_in = experts(where, n2_in, cot_in, through, w_in, w_out)
    grads = expert_grads(where, fast, *parts_in)
    back_in = to_experts(back)
    out_in = to_experts(after(out, back_in))
    if fast:
        axes = ((owned, 2 * owned), (2 * owned, owned))
        halves = [peer(grads[2 * half], axes[half][0]) for half in range(2)]
        part = halves[0].shape[1:]
        small_part = jax.ShapeDtypeStruct(part, BF)
        keep, *leaves = plain(
            first_sums,
            [jax.ShapeDtypeStruct((2, *part), BF), small_part, small_part],
            grads[1],
            halves[0],
            grads[3],
            halves[1],
        )
        arrived = [peer(leaves[half], axes[half][1]) for half in range(2)]
        back_in = after(back_in, keep)
    grad_tokens, *packs = backward(
        fast,
        reps,
        shards_n,
        where,
        [back_in, tokens, cotangent, index, small, gates, *kept],
    )
    result = combine(out_in, index, kept[5])
    if fast:
        mine, twin, *arrived = lax.optimization_barrier((*packs, *arrived))
        total = plain(second_sums, [jax.ShapeDtypeStruct(keep.shape, BF)], keep, *arrived)
        twin = after(twin, total)
        chip = plain(pair_sum, [jax.ShapeDtypeStruct(mine.shape, BF)], mine, peer(twin, 1))
        line = lax.all_to_all(chip, "shard", 0, 0, tiled=True)
        line = after(line, result)
        line = plain(lead_sum, [jax.ShapeDtypeStruct(line.shape[1:], BF)], line)
        early = [total] + [peer(total, k * owned) for k in (1, 2)]
        late = [
            peer(early[axes[half][0] // owned][half], 3 * owned - axes[half][0]) for half in range(2)
        ]
        early += [peer(value, 1) for value in early]
        shape = (owned, width, hidden)
        places = [(other, k, half) for other in range(2) for k in range(3) for half in range(2)]
        so_far = widen(where, places, early, shape)
        plane_groups = [[p * owned + c for p in range(peers)] for c in range(owned)]
        plane = lax.all_to_all(line, "rep", 0, 0, axis_index_groups=plane_groups, tiled=True)
        plane, *so_far = lax.optimization_barrier((plane, *so_far))
        share = plain(lead_sum, [jax.ShapeDtypeStruct(plane.shape[1:], BF)], plane)
        share, *late = lax.optimization_barrier((share, *late))
        late += [peer(value, 1) for value in late]
        parts = lax.all_gather(share, "rep", axis=0, tiled=False)
        grad_qkv, grad_out, grad_router, grad_gains = finish(parts, depth // reps)
        grad_router = grad_router.T
        places = [(other, 3, half) for other in range(2) for half in range(2)]
        grad_w_in, grad_w_out = widen(where, places, late, shape, so_far)
    else:
        share = lax.psum_scatter(grads[0], "rep", scatter_dimension=1, tiled=True)
        every = lax.all_gather(share, "rep", axis=1, tiled=True).astype(F32)
        grad_w_in, grad_w_out = every[0:1], every[1:2]
        pack, sums = packs
        owned_rows = lax.psum_scatter(pack, "shard", scatter_dimension=1, tiled=True)
        owned_rows = lax.psum(owned_rows, "rep").astype(F32)
        grad_qkv, grad_out = owned_rows[0:3], owned_rows[3]
        sums = lax.psum(sums, AXES)
        mine = lax.dynamic_slice_in_dim(sums, shard * depth, depth, axis=1)
        grad_router, grad_gains = mine[0:EXPERTS].T, mine[EXPERTS : EXPERTS + 2]
    return (
        result,
        grad_tokens,
        grad_qkv,
        grad_out,
        grad_router,
        grad_gains,
        grad_w_in,
        grad_w_out,
    )


def solution(mesh):
    reps, shards_n = mesh.shape["rep"], mesh.shape["shard"]
    rows = P(("rep", "shard"), None, None)
    flat = P(("rep", "shard"), None)
    first = P("shard", None)
    stack = P("shard", None, None)
    second = P(None, "shard", None)
    return jax.shard_map(
        lambda *args: shards(reps, shards_n, *args),
        mesh=mesh,
        in_specs=(
            rows, flat, rows, flat, rows, second, first, first, P(None, "shard"), stack, stack,
        ),
        out_specs=(rows, rows, second, first, first, P(None, "shard"), stack, stack),
        check_vma=False,
    )
```

```python
import jax
import jax.numpy as jnp
from jax import lax
from jax.experimental import pallas as pl
from jax.experimental.pallas import tpu as pltpu
from jax.sharding import PartitionSpec as P

HEADS = 8
HEAD_DIM = 64
EXPERTS = 8
CAPACITY = 135
ROWS = 136
EPS = 1e-06
F32 = jnp.float32
BF = jnp.bfloat16
AXES = ("rep", "shard")
FF_STEP = 512
KEPT = 5
SMALL = pl.CostEstimate(flops=1000, bytes_accessed=1000, transcendentals=0)
GELU_A = 0.7978845608028654
GELU_B = 0.044715


def dot_nn(a, b):
    return lax.dot_general(a, b, (((1,), (0,)), ((), ())), preferred_element_type=F32)


def dot_nt(a, b):
    return lax.dot_general(a, b, (((1,), (1,)), ((), ())), preferred_element_type=F32)


def dot_tn(a, b):
    return lax.dot_general(a, b, (((0,), (0,)), ((), ())), preferred_element_type=F32)


def after(value, *others):
    return lax.optimization_barrier((value, *others))[0]


def iota(shape, dim):
    return lax.broadcasted_iota(jnp.int32, shape, dim)


def unit_of(values):
    mean = jnp.mean(values, axis=-1, keepdims=True)
    centered = values - mean
    inv = lax.rsqrt(jnp.mean(centered * centered, axis=-1, keepdims=True) + EPS)
    return centered * inv, inv


def split3(values):
    high = values.astype(BF)
    rest = values - high.astype(F32)
    mid = rest.astype(BF)
    low = (rest - mid.astype(F32)).astype(BF)
    return high, mid, low


def piece_rows(values):
    high, mid, low = split3(values)
    shape = (8, values.shape[1])
    row = iota(shape, 0)
    parts = [jnp.broadcast_to(part.astype(F32), shape) for part in (high, mid, low)]
    return jnp.where(
        row == 0, parts[0], jnp.where(row == 1, parts[1], jnp.where(row == 2, parts[2], 0.0))
    )


def side_row(pieces, width):
    wide = jnp.concatenate([pieces, jnp.zeros((8, width - ROWS), F32)], axis=1)
    row = iota((8, width), 0)
    moved = jnp.where(
        row == 0,
        wide,
        jnp.where(row == 1, pltpu.roll(wide, ROWS, 1), pltpu.roll(wide, 2 * ROWS, 1)),
    )
    return jnp.sum(jnp.where(row < 3, moved, 0.0), axis=0, keepdims=True)


def side_parts(side):
    width = side.shape[1]
    wide = jnp.broadcast_to(side, (8, width))
    row = iota((8, width), 0)
    back = jnp.where(
        row == 0,
        wide,
        jnp.where(row == 1, pltpu.roll(wide, width - ROWS, 1), pltpu.roll(wide, width - 2 * ROWS, 1)),
    )
    return jnp.where(row < 3, back, 0.0)[:, 0:ROWS]


def far(value):
    return pltpu.with_memory_space_constraint(value, pltpu.HBM)


def near(value):
    return pltpu.with_memory_space_constraint(value, pltpu.VMEM)


def vmem(n):
    return [pl.BlockSpec(memory_space=pltpu.VMEM)] * n


def params(mib):
    return pltpu.CompilerParams(vmem_limit_bytes=mib << 20)


def route_body(choice_ref, prio_ref, cot_ref, index_ref, sent_ref):
    count = cot_ref.shape[-2]
    choice = choice_ref[...]
    experts = iota((EXPERTS, count), 0)
    first = jnp.where(choice[0:1, :] == experts, 1.0, 0.0)
    second = jnp.where(choice[1:2, :] == experts, 1.0, 0.0)
    order = jnp.where(iota((count, count), 0) == prio_ref[...], 1.0, 0.0).astype(BF)
    earlier = jnp.where(iota((count, count), 0) < iota((count, count), 1), 1.0, 0.0).astype(BF)
    both = jnp.concatenate([first, second], axis=0).astype(BF)
    before = dot_nn(dot_nt(both, order).astype(BF), earlier)
    held = jnp.sum(first, axis=1, keepdims=True)
    before = jnp.concatenate([before[0:EXPERTS], before[EXPERTS:] + held], axis=0)
    before = dot_nn(jnp.minimum(before, 255.0).astype(BF), order)
    slot0 = jnp.sum(first * before[0:EXPERTS], axis=0, keepdims=True)
    slot1 = jnp.sum(second * before[EXPERTS:], axis=0, keepdims=True)
    slot = jnp.concatenate([slot0, slot1], axis=0).astype(jnp.int32)
    index = jnp.where(slot < CAPACITY, choice * ROWS + slot, -1)
    index_ref[...] = index
    cot = cot_ref[0]
    for e in range(EXPERTS):
        row = iota((ROWS, count), 0) + e * ROWS
        pick = (row == index[0:1, :]) | (row == index[1:2, :])
        sent_ref[e] = dot_nn(jnp.where(pick, 1.0, 0.0).astype(BF), cot).astype(BF)


def route(choice_t, prio, cot):
    _, count, width = cot.shape
    return pl.pallas_call(
        route_body,
        out_shape=(
            jax.ShapeDtypeStruct((2, count), jnp.int32),
            pltpu.HBM((EXPERTS, ROWS, width), BF),
        ),
        in_specs=vmem(3),
        out_specs=tuple(vmem(2)),
        compiler_params=params(12),
        cost_estimate=SMALL,
        name="route",
    )(far(choice_t), far(prio), far(cot))


def pack_body(where_ref, qkv_ref, out_ref, router_ref, gains_ref, pack_ref):
    rows = pack_ref.shape[1]
    start = pl.multiple_of(where_ref[0] * rows, rows)
    for s in range(3):
        pack_ref[s] = qkv_ref[s, pl.ds(start, rows), :]
    pack_ref[3] = out_ref[pl.ds(start, rows), :]
    depth = router_ref.shape[1]
    small = jnp.concatenate(
        [router_ref[...].astype(F32), gains_ref[...].astype(F32), jnp.zeros((6, depth), F32)],
        axis=0,
    )
    pack_ref[4, :, 0:depth] = small.astype(BF)
    pack_ref[4, :, depth:] = jnp.zeros((rows, pack_ref.shape[2] - depth), BF)


def pack_weights(rep, qkv, out, router, gains, rows):
    width = out.shape[1]
    return pl.pallas_call(
        pack_body,
        out_shape=jax.ShapeDtypeStruct((5, rows, width), BF),
        in_specs=[pl.BlockSpec(memory_space=pltpu.SMEM)] + vmem(4),
        out_specs=vmem(1)[0],
        compiler_params=params(4),
        name="pack_weights",
    )(rep.reshape(1), far(qkv), far(out), far(router), far(gains))


def gather_weights(rep, shard, reps, shards_n, qkv, out, router, gains):
    rows = qkv.shape[1] // reps
    pack = pack_weights(rep, qkv, out, router, gains, rows)
    lines = [
        lax.ppermute(pack, "shard", [(i, i ^ dz) for i in range(shards_n)])
        for dz in range(1, shards_n)
    ]
    block = jnp.stack([piece[0:4] for piece in lines])
    smalls = jnp.stack([piece[4] for piece in [pack] + lines])
    spread = [block] + [
        lax.ppermute(block, "rep", [(i, i ^ k) for i in range(reps)]) for k in range(2, reps, 2)
    ]
    twin = [lax.ppermute(piece, "rep", [(i, i ^ 1) for i in range(reps)]) for piece in spread]
    pieces = []
    for own, other in zip(spread, twin, strict=True):
        pieces += [own, other]
    return smalls, pieces, lines


def fill_weights(rep, shard, qkv_ref, out_ref, smalls_ref, piece_refs, full_ref, small_ref):
    depth = out_ref.shape[0]
    own = pl.multiple_of(shard * depth, depth)
    for s in range(3):
        full_ref[s, pl.ds(own, depth), :] = qkv_ref[s]
    full_ref[3, pl.ds(own, depth), :] = out_ref[...]
    small_ref[:, pl.ds(own, depth)] = smalls_ref[0, :, 0:depth]
    for far in range(1, smalls_ref.shape[0]):
        base = pl.multiple_of((shard ^ far) * depth, depth)
        small_ref[:, pl.ds(base, depth)] = smalls_ref[far, :, 0:depth]
        for k, piece in enumerate(piece_refs):
            rows = piece.shape[2]
            start = pl.multiple_of(base + (rep ^ k) * rows, rows)
            for s in range(4):
                full_ref[s, pl.ds(start, rows), :] = piece[far - 1, s]


def head_masks(count):
    lane = iota((count, 2 * HEAD_DIM), 1)
    return [lane < HEAD_DIM, lane >= HEAD_DIM]


def kept_shapes(count, width):
    return (
        ((4, width, width), BF),
        ((HEADS, count, count), BF),
        ((3, count, width), BF),
        ((count, width), BF),
        ((count, width), F32),
    )


def kept_copies(sources, targets, sem):
    copies = {
        i: pltpu.make_async_copy(sources[i], targets[i], sem.at[i]) for i in range(KEPT) if i != 1
    }
    for pair in range(HEADS // 2):
        heads = pl.ds(2 * pair, 2)
        copies[1, pair] = pltpu.make_async_copy(
            sources[1].at[heads], targets[1].at[heads], sem.at[KEPT + pair]
        )
    return copies


def forward_body(fast, n_pieces, *refs):
    if fast:
        where_ref, x_ref, seg_ref, index_ref, qkv_ref, out_ref, smalls_ref = refs[:7]
        piece_refs = refs[7 : 7 + n_pieces]
        refs = refs[7 + n_pieces :]
    else:
        x_ref, seg_ref, index_ref, qkv_ref, out_ref, router_ref, gains_ref = refs[:7]
        refs = refs[7:]
    sent_ref, small_ref, gate_ref, *kept = refs[: 3 + KEPT]
    full_ref, weights_ref, proj_ref, mixed_ref, resid_ref = held = refs[3 + KEPT : -1]
    copies = kept_copies(held, kept, refs[-1])
    if fast:
        fill_weights(
            where_ref[0], where_ref[1], qkv_ref, out_ref, smalls_ref, piece_refs, full_ref, small_ref
        )
    else:
        full_ref[0:3] = qkv_ref[...]
        full_ref[3] = out_ref[...]
        small_ref[...] = jnp.concatenate(
            [
                router_ref[...].astype(F32),
                gains_ref[...].astype(F32),
                jnp.zeros((6, out_ref.shape[1]), F32),
            ],
            axis=0,
        ).astype(BF)
    copies[0].start()
    x = x_ref[0].astype(F32)
    count, width = x.shape
    small = small_ref[...].astype(F32)
    unit1, _ = unit_of(x)
    n1 = (unit1 * small[8:9, :]).astype(BF)
    for s in range(3):
        proj_ref[s] = dot_nn(n1, full_ref[s]).astype(BF)
    copies[2].start()
    document = jnp.where(iota((8, count), 0) == seg_ref[...], 1.0, 0.0).astype(BF)
    bias = jnp.where(dot_tn(document, document) > 0.5, 0.0, -1e30)
    masks = head_masks(count)
    for pair in range(HEADS // 2):
        lanes = slice(pair * 2 * HEAD_DIM, (pair + 1) * 2 * HEAD_DIM)
        q, k, v = proj_ref[0, :, lanes], proj_ref[1, :, lanes], proj_ref[2, :, lanes]
        q = q * BF(HEAD_DIM**-0.5)
        halves = []
        for half in range(2):
            scores = dot_nt(jnp.where(masks[half], q, BF(0)), k) + bias
            top = jnp.max(scores, axis=-1, keepdims=True)
            terms = jnp.exp(scores - top)
            total = jnp.sum(terms, axis=-1, keepdims=True)
            weights = (terms * (1.0 / total)).astype(BF)
            weights_ref[2 * pair + half] = weights
            halves.append(dot_nn(weights, v))
        copies[1, pair].start()
        mixed_ref[:, lanes] = jnp.where(masks[0], halves[0], halves[1]).astype(BF)
    copies[3].start()
    resid = x + dot_nn(mixed_ref[...], full_ref[3])
    resid_ref[...] = resid
    copies[4].start()
    unit2, _ = unit_of(resid)
    n2 = (unit2 * small[9:10, :]).astype(BF)
    logits = dot_nt(small_ref[...], n2)[0:EXPERTS]
    terms = jnp.exp(logits - jnp.max(logits, axis=0, keepdims=True))
    gates = terms / jnp.sum(terms, axis=0, keepdims=True)
    gate_ref[...] = gates
    index = index_ref[...]
    for e in range(EXPERTS):
        row = iota((ROWS, count), 0) + e * ROWS
        pick = (row == index[0:1, :]) | (row == index[1:2, :])
        pick = jnp.where(pick, 1.0, 0.0).astype(BF)
        rows = dot_nn(pick, n2)
        side = side_row(dot_nt(piece_rows(gates[e : e + 1, :]).astype(BF), pick), width)
        last = iota((ROWS, 1), 0) == CAPACITY
        sent_ref[e] = jnp.where(last, side, rows).astype(BF)
    for copy in copies.values():
        copy.wait()


def forward(fast, where, x, seg, index, weights_in, pieces):
    _, count, width = x.shape
    body = lambda *refs: forward_body(fast, len(pieces), *refs)
    operands = [far(x), far(seg), index, *(far(w) for w in weights_in[:2]), *weights_in[2:], *pieces]
    specs = vmem(len(operands))
    if fast:
        operands = [where] + operands
        specs = [pl.BlockSpec(memory_space=pltpu.SMEM)] + specs
    shown = (
        pltpu.HBM((EXPERTS, ROWS, width), BF),
        jax.ShapeDtypeStruct((16, width), BF),
        jax.ShapeDtypeStruct((EXPERTS, count), F32),
    )
    kept = kept_shapes(count, width)
    return pl.pallas_call(
        body,
        out_shape=(*shown, *(pltpu.HBM(*k) for k in kept)),
        in_specs=specs,
        out_specs=(*vmem(3), *([pl.BlockSpec(memory_space=pltpu.HBM)] * KEPT)),
        scratch_shapes=[
            *(pltpu.VMEM(*k) for k in kept),
            pltpu.SemaphoreType.DMA((KEPT + HEADS // 2,)),
        ],
        compiler_params=params(40),
        cost_estimate=SMALL,
        name="forward",
    )(*operands)


def cot_hidden_body(where_ref, cot_ref, w_out_ref, through_ref):
    rows = jnp.concatenate([cot_ref[g].astype(F32) for g in range(2)], axis=0).astype(BF)
    for start in range(0, w_out_ref.shape[2], FF_STEP):
        cols = slice(start, start + FF_STEP)
        through_ref[:, cols] = dot_nn(rows, w_out_ref[0, :, cols])


def cot_hidden(where, cot, w_out):
    groups, _, width = cot.shape
    hidden_n = w_out.shape[2]
    return pl.pallas_call(
        cot_hidden_body,
        out_shape=pltpu.HBM((groups * ROWS, hidden_n), F32),
        grid_spec=pltpu.PrefetchScalarGridSpec(
            num_scalar_prefetch=1,
            grid=(groups // 2,),
            in_specs=[
                pl.BlockSpec((2, ROWS, width), lambda i, w: (i, 0, 0)),
                pl.BlockSpec((1, width, hidden_n), lambda i, w: (w[0], 0, 0)),
            ],
            out_specs=pl.BlockSpec((2 * ROWS, hidden_n), lambda i, w: (i, 0)),
        ),
        compiler_params=params(24),
        cost_estimate=SMALL,
        name="cot_hidden",
    )(where, cot, far(w_out))


def expert_rows(n2_ref, cot_ref, through_ref, w_in_ref, w_out_ref, back_ref, out_ref, span, scratch):
    hidden_ref, pre_ref, rows_ref, gso_ref = scratch
    row = iota((ROWS, 1), 0)
    eye = jnp.where(iota((ROWS, ROWS), 0) == iota((ROWS, ROWS), 1), 1.0, 0.0).astype(BF)
    gates, rows_all, gso_all = [], [], []
    for g in range(2):
        rows = n2_ref[g].astype(F32)
        parts = side_parts(rows[CAPACITY : CAPACITY + 1]).astype(BF)
        gate = jnp.sum(dot_nt(eye, parts), axis=1, keepdims=True)
        gates.append(gate)
        rows_all.append(jnp.where(row < CAPACITY, rows, 0.0))
        gso_all.append(gate * cot_ref[g].astype(F32))
    rows = jnp.concatenate(rows_all, axis=0).astype(BF)
    gate_col = jnp.concatenate(gates, axis=0)
    rows_ref[span], gso_ref[span] = rows, jnp.concatenate(gso_all, axis=0).astype(BF)
    for start in range(0, w_in_ref.shape[2], FF_STEP):
        cols = slice(start, start + FF_STEP)
        u = dot_nn(rows, w_in_ref[0, :, cols])
        square = u * u
        t = jnp.tanh(GELU_A * (u + GELU_B * (u * square)))
        half = 0.5 * (1.0 + t)
        hidden = u * half
        slope = half + hidden * (1.0 - t) * (GELU_A * (1.0 + 3.0 * GELU_B * square))
        hidden_ref[span, cols] = hidden.astype(BF)
        pre_ref[span, cols] = (through_ref[:, cols] * (gate_col * slope)).astype(BF)
    grad_in = dot_nt(pre_ref[span], w_in_ref[0])
    result = dot_nt(hidden_ref[span], w_out_ref[0])
    ones = jnp.ones((8, rows.shape[1]), BF)
    for g in range(2):
        part = slice(g * ROWS, (g + 1) * ROWS)
        out = (gates[g] * result[part]).astype(BF)
        out_ref[g] = out
        product = out.astype(F32) * cot_ref[g].astype(F32)
        high = product.astype(BF)
        low = (product - high.astype(F32)).astype(BF)
        inner = dot_nt(ones, high) + dot_nt(ones, low)
        side = side_row(piece_rows(inner[0:1, :]), out.shape[1])
        back_ref[g] = jnp.where(row == CAPACITY, side, grad_in[part]).astype(BF)


def experts_body(where_ref, *refs):
    expert_rows(*refs[:7], slice(None), refs[7:])


def experts(where, n2, cot, through, w_in, w_out):
    groups, _, width = n2.shape
    hidden_n = w_in.shape[2]
    total = groups * ROWS
    weight = pl.BlockSpec((1, width, hidden_n), lambda i, w: (w[0], 0, 0))
    payload = pl.BlockSpec((2, ROWS, width), lambda i, w: (i, 0, 0))
    narrow = pl.BlockSpec((2 * ROWS, width), lambda i, w: (i, 0))
    wide = pl.BlockSpec((2 * ROWS, hidden_n), lambda i, w: (i, 0))
    return pl.pallas_call(
        experts_body,
        out_shape=(
            [pltpu.HBM((groups, ROWS, width), BF)] * 2
            + [pltpu.HBM((total, hidden_n), BF)] * 2
            + [pltpu.HBM((total, width), BF)] * 2
        ),
        grid_spec=pltpu.PrefetchScalarGridSpec(
            num_scalar_prefetch=1,
            grid=(groups // 2,),
            in_specs=[payload, payload, wide, weight, weight],
            out_specs=[payload, payload, wide, wide, narrow, narrow],
        ),
        compiler_params=params(44),
        cost_estimate=SMALL,
        name="experts",
    )(where, n2, cot, through, far(w_in), far(w_out))


def expert_grads_body(split, where_ref, hidden_ref, pre_ref, rows_ref, gso_ref, *refs):
    grad_refs, sum_ref = refs[:-1], refs[-1]
    step, steps = pl.program_id(0), pl.num_programs(0)
    for half, (left, right) in enumerate(((rows_ref, pre_ref), (gso_ref, hidden_ref))):
        grad = dot_tn(left[...], right[...]).astype(BF)
        if not split:
            grad_refs[0][half] = grad
            continue
        sum_ref[half] = grad
    if not split:
        return
    depth = sum_ref.shape[1] // 4
    for late in range(2):

        @pl.when((step < steps // 2) if late == 0 else (step >= steps // 2))
        def _(late=late):
            for half in range(2):
                for k in range(4):
                    start = pl.multiple_of((where_ref[1] ^ k) * depth, depth)
                    goes = k == 3 or k == 1 + late
                    ref = grad_refs[2 * late + (0 if goes else 1)]
                    ref[int(k == 3 or k == 2 - late), half] = sum_ref[half, pl.ds(start, depth), :]


def expert_grads(where, split, hidden, pre, rows, gso):
    total, width = rows.shape
    hidden_n = hidden.shape[1]
    steps = hidden_n // FF_STEP
    narrow = pl.BlockSpec((total, width), lambda i, w: (0, 0))
    wide = pl.BlockSpec((total, FF_STEP), lambda i, w: (0, i))
    if split:
        part = (2, 2, width // 4, FF_STEP)
        first = pl.BlockSpec(part, lambda i, w: (0, 0, 0, jnp.minimum(i, steps // 2 - 1)))
        second = pl.BlockSpec(part, lambda i, w: (0, 0, 0, jnp.maximum(i - steps // 2, 0)))
        grad_specs = [first, first, second, second]
        grad_shapes = [jax.ShapeDtypeStruct((2, 2, width // 4, hidden_n // 2), BF)] * 4
    else:
        grad_specs = [pl.BlockSpec((2, width, FF_STEP), lambda i, w: (0, 0, i))]
        grad_shapes = [pltpu.HBM((2, width, hidden_n), BF)]
    return pl.pallas_call(
        lambda *refs: expert_grads_body(split, *refs),
        out_shape=grad_shapes,
        grid_spec=pltpu.PrefetchScalarGridSpec(
            num_scalar_prefetch=1,
            grid=(steps,),
            in_specs=[wide, wide, narrow, narrow],
            out_specs=grad_specs,
            scratch_shapes=[pltpu.VMEM((2, width, FF_STEP), BF)],
        ),
        compiler_params=params(30),
        cost_estimate=SMALL,
        name="expert_grads",
    )(where, far(hidden), far(pre), far(rows), far(gso))


def place_grads(fast, reps, shards_n, pack_ref, which, grad):
    if not fast:
        pack_ref[which] = grad.astype(BF)
        return
    width = grad.shape[0]
    depth = width // shards_n
    rows = depth // reps
    grad = grad.astype(BF)
    for z in range(shards_n):
        for r in range(reps):
            start = z * depth + r * rows
            spot = ((r // 2) * 4 + which) * rows
            pack_ref[r % 2, z, spot : spot + rows, :] = grad[start : start + rows]


def backward_body(fast, reps, shards_n, where_ref, *refs):
    core = where_ref[0]
    back_ref, x_ref, cot_ref, index_ref, small_ref, gate_ref, *kept = refs[: 6 + KEPT]
    if fast:
        grad_x_ref, mine_ref, twin_ref, pack_ref, gp_ref = refs[6 + KEPT : 11 + KEPT]
        refs = refs[11 + KEPT :]
    else:
        grad_x_ref, pack_ref, sums_ref, gp_ref = refs[6 + KEPT : 10 + KEPT]
        refs = refs[10 + KEPT :]
    full_ref, weights_ref, proj_ref, mixed_ref, resid_ref = held = refs[:-1]
    sem = refs[-1]
    fetch = kept_copies(kept, held, sem)
    for which in (4, 0, 3, 2, *((1, pair) for pair in range(HEADS // 2))):
        fetch[which].start()
    count, width = resid_ref.shape
    small = small_ref[...].astype(F32)
    index = index_ref[...]
    gates = gate_ref[...]
    grad_n2 = jnp.zeros((count, width), F32)
    rows_h = []
    for e in range(EXPERTS):
        row = iota((ROWS, count), 0) + e * ROWS
        pick = (row == index[0:1, :]) | (row == index[1:2, :])
        pick = jnp.where(pick, 1.0, 0.0).astype(BF)
        back = back_ref[e]
        side = side_parts(back.astype(F32)[CAPACITY : CAPACITY + 1]).astype(BF)
        rows_h.append(jnp.sum(dot_nn(side, pick), axis=0, keepdims=True))
        grad_n2 = grad_n2 + dot_tn(pick, back)
    inner = jnp.concatenate(rows_h, axis=0)
    grad_logits = (inner - gates * jnp.sum(inner, axis=0, keepdims=True)).astype(BF)
    wide_logits = jnp.concatenate(
        [grad_logits.astype(F32), jnp.zeros((8, count), F32)], axis=0
    ).astype(BF)
    grad_n2 = grad_n2 + dot_tn(wide_logits, small_ref[...])
    fetch[4].wait()
    unit2, inv2 = unit_of(resid_ref[...])
    n2 = (unit2 * small[9:10, :]).astype(BF)
    grad_router = dot_nn(wide_logits, n2)[0:EXPERTS]
    grad_gain2 = jnp.sum(grad_n2 * unit2, axis=0, keepdims=True)
    a = grad_n2 * small[9:10, :]
    grad_resid = cot_ref[0].astype(F32) + inv2 * (
        a
        - jnp.mean(a, axis=-1, keepdims=True)
        - unit2 * jnp.mean(a * unit2, axis=-1, keepdims=True)
    )
    branch = grad_resid.astype(BF)
    fetch[0].wait()
    fetch[3].wait()
    place_grads(fast, reps, shards_n, pack_ref, 3, dot_tn(mixed_ref[...], branch))
    grad_mixed = dot_nt(branch, full_ref[3]).astype(BF)
    fetch[2].wait()
    masks = head_masks(count)
    factor = HEAD_DIM**-0.5
    for pair in range(HEADS // 2):
        lanes = slice(pair * 2 * HEAD_DIM, (pair + 1) * 2 * HEAD_DIM)
        q, k, v = proj_ref[0, :, lanes], proj_ref[1, :, lanes], proj_ref[2, :, lanes]
        gm = grad_mixed[:, lanes]
        fetch[1, pair].wait()
        parts = []
        for half in range(2):
            weights = weights_ref[2 * pair + half]
            probs = weights.astype(F32)
            grad_probs = dot_nt(jnp.where(masks[half], gm, BF(0)), v)
            total = jnp.sum(probs * grad_probs, axis=-1, keepdims=True)
            grad_scores = (probs * (grad_probs - total)).astype(BF)
            parts.append(
                (dot_nn(grad_scores, k), dot_tn(grad_scores, q), dot_tn(weights, gm))
            )
        for s in range(3):
            both = jnp.where(masks[0], parts[0][s], parts[1][s])
            gp_ref[s, :, lanes] = (both * factor if s < 2 else both).astype(BF)
    unit1, inv1 = unit_of(x_ref[0].astype(F32))
    n1 = (unit1 * small[8:9, :]).astype(BF)
    grad_n1 = jnp.zeros((count, width), F32)
    for s in range(3):
        grads = gp_ref[s]
        place_grads(fast, reps, shards_n, pack_ref, s, dot_tn(n1, grads))
        grad_n1 = grad_n1 + dot_nt(grads, full_ref[s])
    grad_gain1 = jnp.sum(grad_n1 * unit1, axis=0, keepdims=True)
    b = grad_n1 * small[8:9, :]
    grad_x = grad_resid + inv1 * (
        b
        - jnp.mean(b, axis=-1, keepdims=True)
        - unit1 * jnp.mean(b * unit1, axis=-1, keepdims=True)
    )
    grad_x_ref[0] = grad_x.astype(BF)
    sums = jnp.concatenate(
        [grad_router, grad_gain1, grad_gain2, jnp.zeros((6, width), F32)], axis=0
    )
    if not fast:
        sums_ref[...] = sums
        return
    depth = width // shards_n
    rows = depth // reps
    for z in range(shards_n):
        for half in range(2):
            eight = sums[8 * half : 8 * half + 8, z * depth : (z + 1) * depth]
            eight = jnp.concatenate([eight, jnp.zeros((8, width - depth), F32)], axis=1)
            pack_ref[half, z, 2 * reps * rows :, :] = eight.astype(BF)
    copies = [
        pltpu.make_async_copy(pack_ref.at[core ^ i], (mine_ref, twin_ref)[i], sem.at[i])
        for i in range(2)
    ]
    for copy in copies:
        copy.start()
    for copy in copies:
        copy.wait()


def backward(fast, reps, shards_n, where, operands):
    x = operands[1]
    _, count, width = x.shape
    outs = [jax.ShapeDtypeStruct(x.shape, BF)]
    scratch = [pltpu.VMEM((3, count, width), BF)]
    if fast:
        part = (shards_n, 2 * reps * (width // shards_n // reps) + 8, width)
        outs += [pltpu.HBM(part, BF)] * 2
        out_specs = vmem(1) + [pl.BlockSpec(memory_space=pltpu.HBM)] * 2
        scratch = [pltpu.VMEM((2, *part), BF)] + scratch
    else:
        outs += [
            jax.ShapeDtypeStruct((4, width, width), BF),
            jax.ShapeDtypeStruct((16, width), F32),
        ]
        out_specs = vmem(3)
    return pl.pallas_call(
        lambda *refs: backward_body(fast, reps, shards_n, *refs),
        out_shape=tuple(outs),
        in_specs=[pl.BlockSpec(memory_space=pltpu.SMEM)]
        + vmem(len(operands) - KEPT)
        + [pl.BlockSpec(memory_space=pltpu.HBM)] * KEPT,
        out_specs=tuple(out_specs),
        scratch_shapes=[
            *scratch,
            *(pltpu.VMEM(*k) for k in kept_shapes(count, width)),
            pltpu.SemaphoreType.DMA((KEPT + HEADS // 2,)),
        ],
        compiler_params=params(40),
        cost_estimate=SMALL,
        name="backward",
    )(where, operands[0], *(far(v) for v in operands[1:3]), *operands[3:6], *(far(v) for v in operands[6:]))


def result_body(out_ref, index_ref, resid_ref, result_ref):
    total = resid_ref[...]
    count = total.shape[0]
    index = index_ref[...]
    for e in range(EXPERTS):
        row = iota((ROWS, count), 0) + e * ROWS
        pick = (row == index[0:1, :]) | (row == index[1:2, :])
        total = total + dot_tn(jnp.where(pick, 1.0, 0.0).astype(BF), out_ref[e])
    result_ref[0] = total.astype(BF)


def combine(out, index, resid):
    count, width = resid.shape
    return pl.pallas_call(
        result_body,
        out_shape=jax.ShapeDtypeStruct((1, count, width), BF),
        in_specs=vmem(3),
        out_specs=vmem(1)[0],
        compiler_params=params(8),
        cost_estimate=SMALL,
        name="combine",
    )(far(out), index, far(resid))


def plain(body, outs, *operands):
    return pl.pallas_call(
        body,
        out_shape=tuple(outs) if len(outs) > 1 else outs[0],
        in_specs=vmem(len(operands)),
        out_specs=tuple(vmem(len(outs))) if len(outs) > 1 else vmem(1)[0],
        compiler_params=params(16),
        cost_estimate=SMALL,
        name=body.__name__,
    )(*operands)


def first_sums(stay0_ref, come0_ref, stay1_ref, come1_ref, keep_ref, go0_ref, go1_ref):
    for half, (stay, come, go) in enumerate(
        ((stay0_ref, come0_ref, go0_ref), (stay1_ref, come1_ref, go1_ref))
    ):
        keep_ref[half] = (stay[0].astype(F32) + come[0].astype(F32)).astype(BF)
        go[...] = (stay[1].astype(F32) + come[1].astype(F32)).astype(BF)


def second_sums(keep_ref, come0_ref, come1_ref, sum_ref):
    for half, come in enumerate((come0_ref, come1_ref)):
        sum_ref[half] = (keep_ref[half].astype(F32) + come[...].astype(F32)).astype(BF)


def pair_sum(a_ref, b_ref, sum_ref):
    sum_ref[...] = (a_ref[...].astype(F32) + b_ref[...].astype(F32)).astype(BF)


def lead_sum(parts_ref, sum_ref):
    total = parts_ref[0].astype(F32)
    for i in range(1, parts_ref.shape[0]):
        total = total + parts_ref[i].astype(F32)
    sum_ref[...] = total.astype(BF)


def widen_body(places, aliased, where_ref, *refs):
    n = len(places)
    taken, wide, sem_in, sem_out = refs[-4:]
    outs = refs[-6:-4]
    srcs = refs[: len(refs) - 6 - 2 * aliased]
    _, depth, cols = srcs[0].shape[-3:]
    pieces = [ref.at[half] for ref in srcs for half in range(2)] if len(srcs) < n else srcs
    fetch = [pltpu.make_async_copy(pieces[i], taken.at[i], sem_in.at[i]) for i in range(n)]
    for copy in fetch:
        copy.start()
    sent = []
    for i, (other, k, half) in enumerate(places):
        fetch[i].wait()
        row = pl.multiple_of((where_ref[1] ^ k) * depth, depth)
        for which in range(2):
            wide[i, which] = taken[i, which].astype(F32)
            spot = outs[which].at[
                where_ref[0] ^ other, pl.ds(row, depth), half * cols : (half + 1) * cols
            ]
            copy = pltpu.make_async_copy(wide.at[i, which], spot, sem_out.at[i, which])
            copy.start()
            sent.append(copy)
    for copy in sent:
        copy.wait()


def widen(where, places, sources, shape, so_far=None):
    n = len(places)
    part = sources[0].shape[-3:]
    aliased = so_far is not None
    held = pl.BlockSpec(memory_space=pltpu.HBM)
    operands = [far(source) for source in sources] + (list(so_far) if aliased else [])
    return pl.pallas_call(
        lambda *refs: widen_body(places, aliased, *refs),
        out_shape=(pltpu.HBM(shape, F32), pltpu.HBM(shape, F32)),
        in_specs=[pl.BlockSpec(memory_space=pltpu.SMEM)] + [held] * len(operands),
        out_specs=(held, held),
        scratch_shapes=[
            pltpu.VMEM((n, *part), BF),
            pltpu.VMEM((n, *part), F32),
            pltpu.SemaphoreType.DMA((n,)),
            pltpu.SemaphoreType.DMA((n, 2)),
        ],
        input_output_aliases={len(sources) + 1: 0, len(sources) + 2: 1} if aliased else {},
        compiler_params=params(24),
        cost_estimate=SMALL,
        name="widen",
    )(where, *operands)


def finish_body(rows, parts_ref, qkv_ref, out_ref, router_ref, gains_ref):
    reps = parts_ref.shape[0]
    depth = out_ref.shape[0]
    for r in range(reps):
        for s in range(3):
            qkv_ref[s, r * rows : (r + 1) * rows, :] = parts_ref[
                r, s * rows : (s + 1) * rows, :
            ].astype(F32)
        out_ref[r * rows : (r + 1) * rows, :] = parts_ref[r, 3 * rows : 4 * rows, :].astype(F32)
    smalls = []
    for half in range(2):
        total = jnp.zeros((8, depth), F32)
        for peer in range(reps // 2):
            total = total + parts_ref[2 * peer + half].astype(F32)[4 * rows :, 0:depth]
        smalls.append(total)
    router_ref[...] = smalls[0]
    gains_ref[...] = smalls[1][0:2]


def finish(parts, rows):
    reps, _, width = parts.shape
    depth = rows * reps
    return pl.pallas_call(
        lambda *refs: finish_body(rows, *refs),
        out_shape=(
            jax.ShapeDtypeStruct((3, depth, width), F32),
            jax.ShapeDtypeStruct((depth, width), F32),
            jax.ShapeDtypeStruct((EXPERTS, depth), F32),
            jax.ShapeDtypeStruct((2, depth), F32),
        ),
        in_specs=vmem(1),
        out_specs=tuple(vmem(4)),
        compiler_params=params(4),
        name="finish",
    )(parts)


def shards(reps, shards_n, *args):
    tokens, segments, choices, priority, cotangent = args[:5]
    qkv_weights, out_weight, router_weight, gains, w_in, w_out = args[5:]
    rep, shard = lax.axis_index("rep"), lax.axis_index("shard")
    width, hidden = w_in.shape[1:]
    owned = w_in.shape[0]
    peers = reps // owned
    depth = width // shards_n
    fast = depth % (16 * reps) == 0 and depth == 128 and owned == 2 and peers == 4
    if not fast and owned != 1:
        raise NotImplementedError("mesh")
    column = [
        [(c * owned + e % owned) * shards_n + e // owned for e in range(EXPERTS)]
        for c in range(peers)
    ]

    def to_experts(rows):
        return lax.all_to_all(rows, AXES, 0, 0, axis_index_groups=column, tiled=True)

    where = jnp.stack([rep % owned, rep // owned]).astype(jnp.int32)
    index, cot_sent = route(choices[0].T, priority, cotangent)
    if fast:
        smalls, pieces, lines = gather_weights(
            rep, shard, reps, shards_n, qkv_weights, out_weight, router_weight.T, gains
        )
        place = jnp.stack([rep, shard]).astype(jnp.int32)
        weights_in = (qkv_weights, out_weight, smalls)
    else:
        place, pieces, lines = None, [], []
        weights_in = (
            lax.all_gather(qkv_weights, "shard", axis=1, tiled=True),
            lax.all_gather(out_weight, "shard", axis=0, tiled=True),
            lax.all_gather(router_weight, "shard", axis=0, tiled=True).T,
            lax.all_gather(gains, "shard", axis=1, tiled=True),
        )
    cot_in = to_experts(after(cot_sent, *lines))
    sent, small, gates, *kept = forward(
        fast, place, tokens, segments, index, weights_in, pieces
    )
    n2_in = to_experts(sent)

    def peer(value, k):
        return lax.ppermute(value, "rep", [(i, i ^ k) for i in range(reps)])

    through = cot_hidden(where, cot_in, w_out)
    back, out, *parts_in = experts(where, n2_in, cot_in, through, w_in, w_out)
    grads = expert_grads(where, fast, *parts_in)
    back_in = to_experts(back)
    out_in = to_experts(after(out, back_in))
    if fast:
        axes = ((owned, 2 * owned), (2 * owned, owned))
        halves = [peer(grads[2 * half], axes[half][0]) for half in range(2)]
        part = halves[0].shape[1:]
        small_part = jax.ShapeDtypeStruct(part, BF)
        keep, *leaves = plain(
            first_sums,
            [jax.ShapeDtypeStruct((2, *part), BF), small_part, small_part],
            grads[1],
            halves[0],
            grads[3],
            halves[1],
        )
        arrived = [peer(leaves[half], axes[half][1]) for half in range(2)]
        back_in = after(back_in, keep)
    grad_tokens, *packs = backward(
        fast,
        reps,
        shards_n,
        where,
        [back_in, tokens, cotangent, index, small, gates, *kept],
    )
    result = combine(out_in, index, kept[4])
    if fast:
        mine, twin, *arrived = lax.optimization_barrier((*packs, *arrived))
        total = plain(second_sums, [jax.ShapeDtypeStruct(keep.shape, BF)], keep, *arrived)
        twin = after(twin, total)
        chip = plain(pair_sum, [jax.ShapeDtypeStruct(mine.shape, BF)], mine, peer(twin, 1))
        line = lax.all_to_all(after(chip, out_in), "shard", 0, 0, tiled=True)
        line = plain(lead_sum, [jax.ShapeDtypeStruct(line.shape[1:], BF)], line)
        tall = 2 * depth
        own_small = line[tall:]
        line = line[:tall].reshape(peers, tall // peers, width)
        early = [total] + [peer(total, k * owned) for k in (1, 2)]
        late = [
            peer(early[axes[half][0] // owned][half], 3 * owned - axes[half][0]) for half in range(2)
        ]
        early += [peer(value, 1) for value in early]
        shape = (owned, width, hidden)
        places = [(other, k, half) for other in range(2) for k in range(3) for half in range(2)]
        so_far = widen(where, places, early, shape)
        plane_groups = [[p * owned + c for p in range(peers)] for c in range(owned)]
        plane = lax.all_to_all(line, "rep", 0, 0, axis_index_groups=plane_groups, tiled=True)
        plane, *so_far = lax.optimization_barrier((plane, *so_far))
        share = plain(lead_sum, [jax.ShapeDtypeStruct(plane.shape[1:], BF)], plane)
        share = jnp.concatenate([share, own_small], axis=0)
        share, *late = lax.optimization_barrier((share, *late))
        late += [peer(value, 1) for value in late]
        parts = lax.all_to_all(
            jnp.broadcast_to(share, (reps, *share.shape)), "rep", 0, 0, tiled=True
        )
        places = [(other, 3, half) for other in range(2) for half in range(2)]
        grad_w_in, grad_w_out = widen(where, places, late, shape, so_far)
        parts = after(parts, grad_w_in, result)
        grad_qkv, grad_out, grad_router, grad_gains = finish(parts, depth // reps)
        grad_router = grad_router.T
    else:
        share = lax.psum_scatter(grads[0], "rep", scatter_dimension=1, tiled=True)
        every = lax.all_gather(share, "rep", axis=1, tiled=True).astype(F32)
        grad_w_in, grad_w_out = every[0:1], every[1:2]
        pack, sums = packs
        owned_rows = lax.psum_scatter(pack, "shard", scatter_dimension=1, tiled=True)
        owned_rows = lax.psum(owned_rows, "rep").astype(F32)
        grad_qkv, grad_out = owned_rows[0:3], owned_rows[3]
        sums = lax.psum(sums, AXES)
        mine = lax.dynamic_slice_in_dim(sums, shard * depth, depth, axis=1)
        grad_router, grad_gains = mine[0:EXPERTS].T, mine[EXPERTS : EXPERTS + 2]
    return (
        result,
        grad_tokens,
        grad_qkv,
        grad_out,
        grad_router,
        grad_gains,
        grad_w_in,
        grad_w_out,
    )


def solution(mesh):
    reps, shards_n = mesh.shape["rep"], mesh.shape["shard"]
    rows = P(("rep", "shard"), None, None)
    flat = P(("rep", "shard"), None)
    first = P("shard", None)
    stack = P("shard", None, None)
    second = P(None, "shard", None)
    return jax.shard_map(
        lambda *args: shards(reps, shards_n, *args),
        mesh=mesh,
        in_specs=(
            rows, flat, rows, flat, rows, second, first, first, P(None, "shard"), stack, stack,
        ),
        out_specs=(rows, rows, second, first, first, P(None, "shard"), stack, stack),
        check_vma=False,
    )
```

```python
import jax
import jax.numpy as jnp
from jax import lax
from jax.experimental import pallas as pl
from jax.experimental.pallas import tpu as pltpu
from jax.sharding import PartitionSpec as P

HEADS = 8
HEAD_DIM = 64
EXPERTS = 8
CAPACITY = 135
ROWS = 136
EPS = 1e-06
F32 = jnp.float32
BF = jnp.bfloat16
AXES = ("rep", "shard")
FF_STEP = 512
KEPT = 5
SMALL = pl.CostEstimate(flops=1000, bytes_accessed=1000, transcendentals=0)
GELU_A = 0.7978845608028654
GELU_B = 0.044715


def dot_nn(a, b):
    return lax.dot_general(a, b, (((1,), (0,)), ((), ())), preferred_element_type=F32)


def dot_nt(a, b):
    return lax.dot_general(a, b, (((1,), (1,)), ((), ())), preferred_element_type=F32)


def dot_tn(a, b):
    return lax.dot_general(a, b, (((0,), (0,)), ((), ())), preferred_element_type=F32)


def after(value, *others):
    return lax.optimization_barrier((value, *others))[0]


def iota(shape, dim):
    return lax.broadcasted_iota(jnp.int32, shape, dim)


def unit_of(values):
    mean = jnp.mean(values, axis=-1, keepdims=True)
    centered = values - mean
    inv = lax.rsqrt(jnp.mean(centered * centered, axis=-1, keepdims=True) + EPS)
    return centered * inv, inv


def split3(values):
    high = values.astype(BF)
    rest = values - high.astype(F32)
    mid = rest.astype(BF)
    low = (rest - mid.astype(F32)).astype(BF)
    return high, mid, low


def piece_rows(values):
    high, mid, low = split3(values)
    shape = (8, values.shape[1])
    row = iota(shape, 0)
    parts = [jnp.broadcast_to(part.astype(F32), shape) for part in (high, mid, low)]
    return jnp.where(
        row == 0, parts[0], jnp.where(row == 1, parts[1], jnp.where(row == 2, parts[2], 0.0))
    )


def side_row(pieces, width):
    wide = jnp.concatenate([pieces, jnp.zeros((8, width - ROWS), F32)], axis=1)
    row = iota((8, width), 0)
    moved = jnp.where(
        row == 0,
        wide,
        jnp.where(row == 1, pltpu.roll(wide, ROWS, 1), pltpu.roll(wide, 2 * ROWS, 1)),
    )
    return jnp.sum(jnp.where(row < 3, moved, 0.0), axis=0, keepdims=True)


def side_parts(side):
    width = side.shape[1]
    wide = jnp.broadcast_to(side, (8, width))
    row = iota((8, width), 0)
    back = jnp.where(
        row == 0,
        wide,
        jnp.where(row == 1, pltpu.roll(wide, width - ROWS, 1), pltpu.roll(wide, width - 2 * ROWS, 1)),
    )
    return jnp.where(row < 3, back, 0.0)[:, 0:ROWS]


def far(value):
    return pltpu.with_memory_space_constraint(value, pltpu.HBM)


def near(value):
    return pltpu.with_memory_space_constraint(value, pltpu.VMEM)


def vmem(n):
    return [pl.BlockSpec(memory_space=pltpu.VMEM)] * n


def params(mib):
    return pltpu.CompilerParams(vmem_limit_bytes=mib << 20)


def route_body(choice_ref, prio_ref, cot_ref, index_ref, sent_ref):
    count = cot_ref.shape[-2]
    choice = choice_ref[...]
    experts = iota((EXPERTS, count), 0)
    first = jnp.where(choice[0:1, :] == experts, 1.0, 0.0)
    second = jnp.where(choice[1:2, :] == experts, 1.0, 0.0)
    order = jnp.where(iota((count, count), 0) == prio_ref[...], 1.0, 0.0).astype(BF)
    earlier = jnp.where(iota((count, count), 0) < iota((count, count), 1), 1.0, 0.0).astype(BF)
    both = jnp.concatenate([first, second], axis=0).astype(BF)
    before = dot_nn(dot_nt(both, order).astype(BF), earlier)
    held = jnp.sum(first, axis=1, keepdims=True)
    before = jnp.concatenate([before[0:EXPERTS], before[EXPERTS:] + held], axis=0)
    before = dot_nn(jnp.minimum(before, 255.0).astype(BF), order)
    slot0 = jnp.sum(first * before[0:EXPERTS], axis=0, keepdims=True)
    slot1 = jnp.sum(second * before[EXPERTS:], axis=0, keepdims=True)
    slot = jnp.concatenate([slot0, slot1], axis=0).astype(jnp.int32)
    index = jnp.where(slot < CAPACITY, choice * ROWS + slot, -1)
    index_ref[...] = index
    cot = cot_ref[0]
    for e in range(EXPERTS):
        row = iota((ROWS, count), 0) + e * ROWS
        pick = (row == index[0:1, :]) | (row == index[1:2, :])
        sent_ref[e] = dot_nn(jnp.where(pick, 1.0, 0.0).astype(BF), cot).astype(BF)


def route(choice_t, prio, cot):
    _, count, width = cot.shape
    return pl.pallas_call(
        route_body,
        out_shape=(
            jax.ShapeDtypeStruct((2, count), jnp.int32),
            pltpu.HBM((EXPERTS, ROWS, width), BF),
        ),
        in_specs=vmem(3),
        out_specs=tuple(vmem(2)),
        compiler_params=params(12),
        cost_estimate=SMALL,
        name="route",
    )(far(choice_t), far(prio), far(cot))


def pack_body(where_ref, qkv_ref, out_ref, router_ref, gains_ref, pack_ref):
    rows = pack_ref.shape[1]
    start = pl.multiple_of(where_ref[0] * rows, rows)
    for s in range(3):
        pack_ref[s] = qkv_ref[s, pl.ds(start, rows), :]
    pack_ref[3] = out_ref[pl.ds(start, rows), :]
    depth = router_ref.shape[1]
    small = jnp.concatenate(
        [router_ref[...].astype(F32), gains_ref[...].astype(F32), jnp.zeros((6, depth), F32)],
        axis=0,
    )
    pack_ref[4, :, 0:depth] = small.astype(BF)
    pack_ref[4, :, depth:] = jnp.zeros((rows, pack_ref.shape[2] - depth), BF)


def pack_weights(rep, qkv, out, router, gains, rows):
    width = out.shape[1]
    return pl.pallas_call(
        pack_body,
        out_shape=jax.ShapeDtypeStruct((5, rows, width), BF),
        in_specs=[pl.BlockSpec(memory_space=pltpu.SMEM)] + vmem(4),
        out_specs=vmem(1)[0],
        compiler_params=params(4),
        name="pack_weights",
    )(rep.reshape(1), far(qkv), far(out), far(router), far(gains))


def gather_weights(rep, shard, reps, shards_n, qkv, out, router, gains):
    rows = qkv.shape[1] // reps
    pack = pack_weights(rep, qkv, out, router, gains, rows)
    lines = [
        lax.ppermute(pack, "shard", [(i, i ^ dz) for i in range(shards_n)])
        for dz in range(1, shards_n)
    ]
    block = jnp.stack([piece[0:4] for piece in lines])
    smalls = jnp.stack([piece[4] for piece in [pack] + lines])
    spread = [block] + [
        lax.ppermute(block, "rep", [(i, i ^ k) for i in range(reps)]) for k in range(2, reps, 2)
    ]
    twin = [lax.ppermute(piece, "rep", [(i, i ^ 1) for i in range(reps)]) for piece in spread]
    pieces = []
    for own, other in zip(spread, twin, strict=True):
        pieces += [own, other]
    return smalls, pieces, lines


def fill_weights(rep, shard, qkv_ref, out_ref, smalls_ref, piece_refs, full_ref, small_ref):
    depth = out_ref.shape[0]
    own = pl.multiple_of(shard * depth, depth)
    for s in range(3):
        full_ref[s, pl.ds(own, depth), :] = qkv_ref[s]
    full_ref[3, pl.ds(own, depth), :] = out_ref[...]
    small_ref[:, pl.ds(own, depth)] = smalls_ref[0, :, 0:depth]
    for far in range(1, smalls_ref.shape[0]):
        base = pl.multiple_of((shard ^ far) * depth, depth)
        small_ref[:, pl.ds(base, depth)] = smalls_ref[far, :, 0:depth]
        for k, piece in enumerate(piece_refs):
            rows = piece.shape[2]
            start = pl.multiple_of(base + (rep ^ k) * rows, rows)
            for s in range(4):
                full_ref[s, pl.ds(start, rows), :] = piece[far - 1, s]


def head_masks(count):
    lane = iota((count, 2 * HEAD_DIM), 1)
    return [lane < HEAD_DIM, lane >= HEAD_DIM]


def kept_shapes(count, width):
    return (
        ((4, width, width), BF),
        ((HEADS, count, count), BF),
        ((3, count, width), BF),
        ((count, width), BF),
        ((count, width), F32),
    )


def kept_copies(sources, targets, sem):
    copies = {
        i: pltpu.make_async_copy(sources[i], targets[i], sem.at[i]) for i in range(KEPT) if i != 1
    }
    for pair in range(HEADS // 2):
        heads = pl.ds(2 * pair, 2)
        copies[1, pair] = pltpu.make_async_copy(
            sources[1].at[heads], targets[1].at[heads], sem.at[KEPT + pair]
        )
    return copies


def forward_body(fast, n_pieces, *refs):
    if fast:
        where_ref, x_ref, seg_ref, index_ref, qkv_ref, out_ref, smalls_ref = refs[:7]
        piece_refs = refs[7 : 7 + n_pieces]
        refs = refs[7 + n_pieces :]
    else:
        x_ref, seg_ref, index_ref, qkv_ref, out_ref, router_ref, gains_ref = refs[:7]
        refs = refs[7:]
    sent_ref, small_ref, gate_ref, *kept = refs[: 3 + KEPT]
    full_ref, weights_ref, proj_ref, mixed_ref, resid_ref = held = refs[3 + KEPT : -1]
    copies = kept_copies(held, kept, refs[-1])
    if fast:
        fill_weights(
            where_ref[0], where_ref[1], qkv_ref, out_ref, smalls_ref, piece_refs, full_ref, small_ref
        )
    else:
        full_ref[0:3] = qkv_ref[...]
        full_ref[3] = out_ref[...]
        small_ref[...] = jnp.concatenate(
            [
                router_ref[...].astype(F32),
                gains_ref[...].astype(F32),
                jnp.zeros((6, out_ref.shape[1]), F32),
            ],
            axis=0,
        ).astype(BF)
    copies[0].start()
    x = x_ref[0].astype(F32)
    count, width = x.shape
    small = small_ref[...].astype(F32)
    unit1, _ = unit_of(x)
    n1 = (unit1 * small[8:9, :]).astype(BF)
    for s in range(3):
        proj_ref[s] = dot_nn(n1, full_ref[s]).astype(BF)
    copies[2].start()
    document = jnp.where(iota((8, count), 0) == seg_ref[...], 1.0, 0.0).astype(BF)
    bias = jnp.where(dot_tn(document, document) > 0.5, 0.0, -1e30)
    masks = head_masks(count)
    for pair in range(HEADS // 2):
        lanes = slice(pair * 2 * HEAD_DIM, (pair + 1) * 2 * HEAD_DIM)
        q, k, v = proj_ref[0, :, lanes], proj_ref[1, :, lanes], proj_ref[2, :, lanes]
        q = q * BF(HEAD_DIM**-0.5)
        halves = []
        for half in range(2):
            scores = dot_nt(k, jnp.where(masks[half], q, BF(0))) + bias
            top = jnp.max(scores, axis=0, keepdims=True)
            terms = jnp.exp(scores - top)
            total = jnp.sum(terms, axis=0, keepdims=True)
            weights = (terms * (1.0 / total)).astype(BF)
            weights_ref[2 * pair + half] = weights
            halves.append(dot_tn(weights, v))
        copies[1, pair].start()
        mixed_ref[:, lanes] = jnp.where(masks[0], halves[0], halves[1]).astype(BF)
    copies[3].start()
    resid = x + dot_nn(mixed_ref[...], full_ref[3])
    resid_ref[...] = resid
    copies[4].start()
    unit2, _ = unit_of(resid)
    n2 = (unit2 * small[9:10, :]).astype(BF)
    logits = dot_nt(small_ref[...], n2)[0:EXPERTS]
    terms = jnp.exp(logits - jnp.max(logits, axis=0, keepdims=True))
    gates = terms / jnp.sum(terms, axis=0, keepdims=True)
    gate_ref[...] = gates
    index = index_ref[...]
    for e in range(EXPERTS):
        row = iota((ROWS, count), 0) + e * ROWS
        pick = (row == index[0:1, :]) | (row == index[1:2, :])
        pick = jnp.where(pick, 1.0, 0.0).astype(BF)
        rows = dot_nn(pick, n2)
        side = side_row(dot_nt(piece_rows(gates[e : e + 1, :]).astype(BF), pick), width)
        last = iota((ROWS, 1), 0) == CAPACITY
        sent_ref[e] = jnp.where(last, side, rows).astype(BF)
    for copy in copies.values():
        copy.wait()


def forward(fast, where, x, seg, index, weights_in, pieces):
    _, count, width = x.shape
    body = lambda *refs: forward_body(fast, len(pieces), *refs)
    operands = [far(x), far(seg), index, *(far(w) for w in weights_in[:2]), *weights_in[2:], *pieces]
    specs = vmem(len(operands))
    if fast:
        operands = [where] + operands
        specs = [pl.BlockSpec(memory_space=pltpu.SMEM)] + specs
    shown = (
        pltpu.HBM((EXPERTS, ROWS, width), BF),
        jax.ShapeDtypeStruct((16, width), BF),
        jax.ShapeDtypeStruct((EXPERTS, count), F32),
    )
    kept = kept_shapes(count, width)
    return pl.pallas_call(
        body,
        out_shape=(*shown, *(pltpu.HBM(*k) for k in kept)),
        in_specs=specs,
        out_specs=(*vmem(3), *([pl.BlockSpec(memory_space=pltpu.HBM)] * KEPT)),
        scratch_shapes=[
            *(pltpu.VMEM(*k) for k in kept),
            pltpu.SemaphoreType.DMA((KEPT + HEADS // 2,)),
        ],
        compiler_params=params(40),
        cost_estimate=SMALL,
        name="forward",
    )(*operands)


def cot_hidden_body(where_ref, cot_ref, w_out_ref, through_ref):
    rows = jnp.concatenate([cot_ref[g].astype(F32) for g in range(2)], axis=0).astype(BF)
    for start in range(0, w_out_ref.shape[2], FF_STEP):
        cols = slice(start, start + FF_STEP)
        through_ref[:, cols] = dot_nn(rows, w_out_ref[0, :, cols])


def cot_hidden(where, cot, w_out):
    groups, _, width = cot.shape
    hidden_n = w_out.shape[2]
    return pl.pallas_call(
        cot_hidden_body,
        out_shape=pltpu.HBM((groups * ROWS, hidden_n), F32),
        grid_spec=pltpu.PrefetchScalarGridSpec(
            num_scalar_prefetch=1,
            grid=(groups // 2,),
            in_specs=[
                pl.BlockSpec((2, ROWS, width), lambda i, w: (i, 0, 0)),
                pl.BlockSpec((1, width, hidden_n), lambda i, w: (w[0], 0, 0)),
            ],
            out_specs=pl.BlockSpec((2 * ROWS, hidden_n), lambda i, w: (i, 0)),
        ),
        compiler_params=params(24),
        cost_estimate=SMALL,
        name="cot_hidden",
    )(where, cot, far(w_out))


def expert_rows(n2_ref, cot_ref, through_ref, w_in_ref, w_out_ref, back_ref, out_ref, span, scratch):
    hidden_ref, pre_ref, rows_ref, gso_ref = scratch
    row = iota((ROWS, 1), 0)
    eye = jnp.where(iota((ROWS, ROWS), 0) == iota((ROWS, ROWS), 1), 1.0, 0.0).astype(BF)
    gates, rows_all, gso_all = [], [], []
    for g in range(2):
        rows = n2_ref[g].astype(F32)
        parts = side_parts(rows[CAPACITY : CAPACITY + 1]).astype(BF)
        gate = jnp.sum(dot_nt(eye, parts), axis=1, keepdims=True)
        gates.append(gate)
        rows_all.append(jnp.where(row < CAPACITY, rows, 0.0))
        gso_all.append(gate * cot_ref[g].astype(F32))
    rows = jnp.concatenate(rows_all, axis=0).astype(BF)
    gate_col = jnp.concatenate(gates, axis=0)
    rows_ref[span], gso_ref[span] = rows, jnp.concatenate(gso_all, axis=0).astype(BF)
    for start in range(0, w_in_ref.shape[2], FF_STEP):
        cols = slice(start, start + FF_STEP)
        u = dot_nn(rows, w_in_ref[0, :, cols])
        square = u * u
        t = jnp.tanh(GELU_A * (u + GELU_B * (u * square)))
        half = 0.5 * (1.0 + t)
        hidden = u * half
        slope = half + hidden * (1.0 - t) * (GELU_A * (1.0 + 3.0 * GELU_B * square))
        hidden_ref[span, cols] = hidden.astype(BF)
        pre_ref[span, cols] = (through_ref[:, cols] * (gate_col * slope)).astype(BF)
    grad_in = dot_nt(pre_ref[span], w_in_ref[0])
    result = dot_nt(hidden_ref[span], w_out_ref[0])
    ones = jnp.ones((8, rows.shape[1]), BF)
    for g in range(2):
        part = slice(g * ROWS, (g + 1) * ROWS)
        out = (gates[g] * result[part]).astype(BF)
        out_ref[g] = out
        product = out.astype(F32) * cot_ref[g].astype(F32)
        high = product.astype(BF)
        low = (product - high.astype(F32)).astype(BF)
        inner = dot_nt(ones, high) + dot_nt(ones, low)
        side = side_row(piece_rows(inner[0:1, :]), out.shape[1])
        back_ref[g] = jnp.where(row == CAPACITY, side, grad_in[part]).astype(BF)


def experts_body(where_ref, *refs):
    expert_rows(*refs[:7], slice(None), refs[7:])


def experts(where, n2, cot, through, w_in, w_out):
    groups, _, width = n2.shape
    hidden_n = w_in.shape[2]
    total = groups * ROWS
    weight = pl.BlockSpec((1, width, hidden_n), lambda i, w: (w[0], 0, 0))
    payload = pl.BlockSpec((2, ROWS, width), lambda i, w: (i, 0, 0))
    narrow = pl.BlockSpec((2 * ROWS, width), lambda i, w: (i, 0))
    wide = pl.BlockSpec((2 * ROWS, hidden_n), lambda i, w: (i, 0))
    return pl.pallas_call(
        experts_body,
        out_shape=(
            [pltpu.HBM((groups, ROWS, width), BF)] * 2
            + [pltpu.HBM((total, hidden_n), BF)] * 2
            + [pltpu.HBM((total, width), BF)] * 2
        ),
        grid_spec=pltpu.PrefetchScalarGridSpec(
            num_scalar_prefetch=1,
            grid=(groups // 2,),
            in_specs=[payload, payload, wide, weight, weight],
            out_specs=[payload, payload, wide, wide, narrow, narrow],
        ),
        compiler_params=params(44),
        cost_estimate=SMALL,
        name="experts",
    )(where, n2, cot, through, far(w_in), far(w_out))


def expert_grads_body(split, where_ref, hidden_ref, pre_ref, rows_ref, gso_ref, *refs):
    grad_refs, sum_ref = refs[:-1], refs[-1]
    step, steps = pl.program_id(0), pl.num_programs(0)
    for half, (left, right) in enumerate(((rows_ref, pre_ref), (gso_ref, hidden_ref))):
        grad = dot_tn(left[...], right[...]).astype(BF)
        if not split:
            grad_refs[0][half] = grad
            continue
        sum_ref[half] = grad
    if not split:
        return
    depth = sum_ref.shape[1] // 4
    for late in range(2):

        @pl.when((step < steps // 2) if late == 0 else (step >= steps // 2))
        def _(late=late):
            for half in range(2):
                for k in range(4):
                    start = pl.multiple_of((where_ref[1] ^ k) * depth, depth)
                    goes = k == 3 or k == 1 + late
                    ref = grad_refs[2 * late + (0 if goes else 1)]
                    ref[int(k == 3 or k == 2 - late), half] = sum_ref[half, pl.ds(start, depth), :]


def expert_grads(where, split, hidden, pre, rows, gso):
    total, width = rows.shape
    hidden_n = hidden.shape[1]
    steps = hidden_n // FF_STEP
    narrow = pl.BlockSpec((total, width), lambda i, w: (0, 0))
    wide = pl.BlockSpec((total, FF_STEP), lambda i, w: (0, i))
    if split:
        part = (2, 2, width // 4, FF_STEP)
        first = pl.BlockSpec(part, lambda i, w: (0, 0, 0, jnp.minimum(i, steps // 2 - 1)))
        second = pl.BlockSpec(part, lambda i, w: (0, 0, 0, jnp.maximum(i - steps // 2, 0)))
        grad_specs = [first, first, second, second]
        grad_shapes = [jax.ShapeDtypeStruct((2, 2, width // 4, hidden_n // 2), BF)] * 4
    else:
        grad_specs = [pl.BlockSpec((2, width, FF_STEP), lambda i, w: (0, 0, i))]
        grad_shapes = [pltpu.HBM((2, width, hidden_n), BF)]
    return pl.pallas_call(
        lambda *refs: expert_grads_body(split, *refs),
        out_shape=grad_shapes,
        grid_spec=pltpu.PrefetchScalarGridSpec(
            num_scalar_prefetch=1,
            grid=(steps,),
            in_specs=[wide, wide, narrow, narrow],
            out_specs=grad_specs,
            scratch_shapes=[pltpu.VMEM((2, width, FF_STEP), BF)],
        ),
        compiler_params=params(30),
        cost_estimate=SMALL,
        name="expert_grads",
    )(where, far(hidden), far(pre), far(rows), far(gso))


def place_grads(fast, reps, shards_n, pack_ref, which, grad):
    if not fast:
        pack_ref[which] = grad.astype(BF)
        return
    width = grad.shape[0]
    depth = width // shards_n
    rows = depth // reps
    grad = grad.astype(BF)
    for z in range(shards_n):
        for r in range(reps):
            start = z * depth + r * rows
            spot = ((r // 2) * 4 + which) * rows
            pack_ref[r % 2, z, spot : spot + rows, :] = grad[start : start + rows]


def tokens_back_body(back_ref, cot_ref, index_ref, small_ref, gate_ref, *refs):
    full_far, mixed_far, resid_far, grad_resid_ref, grad_mixed_ref, grad_out_ref, sums_ref = refs[:7]
    out_weight_ref, mixed_ref, resid_ref, sem = refs[7:]
    fetch = [
        pltpu.make_async_copy(source, target, sem.at[i])
        for i, (source, target) in enumerate(
            ((resid_far, resid_ref), (full_far.at[3], out_weight_ref), (mixed_far, mixed_ref))
        )
    ]
    for copy in fetch:
        copy.start()
    count, width = resid_ref.shape
    small = small_ref[...].astype(F32)
    index = index_ref[...]
    gates = gate_ref[...]
    grad_n2 = jnp.zeros((count, width), F32)
    rows_h = []
    for e in range(EXPERTS):
        row = iota((ROWS, count), 0) + e * ROWS
        pick = (row == index[0:1, :]) | (row == index[1:2, :])
        pick = jnp.where(pick, 1.0, 0.0).astype(BF)
        back = back_ref[e]
        side = side_parts(back.astype(F32)[CAPACITY : CAPACITY + 1]).astype(BF)
        rows_h.append(jnp.sum(dot_nn(side, pick), axis=0, keepdims=True))
        grad_n2 = grad_n2 + dot_tn(pick, back)
    inner = jnp.concatenate(rows_h, axis=0)
    grad_logits = (inner - gates * jnp.sum(inner, axis=0, keepdims=True)).astype(BF)
    wide_logits = jnp.concatenate(
        [grad_logits.astype(F32), jnp.zeros((8, count), F32)], axis=0
    ).astype(BF)
    grad_n2 = grad_n2 + dot_tn(wide_logits, small_ref[...])
    fetch[0].wait()
    unit2, inv2 = unit_of(resid_ref[...])
    n2 = (unit2 * small[9:10, :]).astype(BF)
    grad_router = dot_nn(wide_logits, n2)[0:EXPERTS]
    grad_gain2 = jnp.sum(grad_n2 * unit2, axis=0, keepdims=True)
    sums_ref[...] = jnp.concatenate(
        [grad_router, jnp.zeros((1, width), F32), grad_gain2, jnp.zeros((6, width), F32)], axis=0
    )
    a = grad_n2 * small[9:10, :]
    grad_resid = cot_ref[0].astype(F32) + inv2 * (
        a
        - jnp.mean(a, axis=-1, keepdims=True)
        - unit2 * jnp.mean(a * unit2, axis=-1, keepdims=True)
    )
    grad_resid_ref[...] = grad_resid
    branch = grad_resid.astype(BF)
    fetch[1].wait()
    grad_mixed_ref[...] = dot_nt(branch, out_weight_ref[...]).astype(BF)
    fetch[2].wait()
    grad_out_ref[...] = dot_tn(mixed_ref[...], branch).astype(BF)


def tokens_back(back, cot, index, small, gates, full, mixed, resid):
    count, width = resid.shape
    held = pl.BlockSpec(memory_space=pltpu.HBM)
    outs = (
        ((count, width), F32),
        ((count, width), BF),
        ((width, width), BF),
        ((16, width), F32),
    )
    return pl.pallas_call(
        tokens_back_body,
        out_shape=tuple(pltpu.HBM(*o) for o in outs),
        in_specs=vmem(5) + [held] * 3,
        out_specs=tuple(vmem(4)),
        scratch_shapes=[
            pltpu.VMEM((width, width), BF),
            pltpu.VMEM((count, width), BF),
            pltpu.VMEM((count, width), F32),
            pltpu.SemaphoreType.DMA((3,)),
        ],
        compiler_params=params(24),
        cost_estimate=SMALL,
        name="tokens_back",
    )(back, far(cot), index, small, gates, far(full), far(mixed), far(resid))


def backward_body(fast, reps, shards_n, where_ref, *refs):
    core = where_ref[0]
    grad_mixed_ref, small_ref, early_ref = refs[:3]
    sources = refs[3:8]
    if fast:
        gp_far, mine_ref, twin_ref, pack_ref = refs[8:12]
        refs = refs[12:]
    else:
        gp_far, pack_ref, sums_ref = refs[8:11]
        refs = refs[11:]
    gp_ref, proj_ref, weights_ref, full_ref, x_ref, grad_out_ref = refs[:-1]
    held, sem = refs[1:-1], refs[-1]
    pairs = HEADS // 2
    copies = {
        i: pltpu.make_async_copy(sources[i], held[i], sem.at[i]) for i in range(5) if i != 1
    }
    for pair in range(pairs):
        heads = pl.ds(2 * pair, 2)
        copies[1, pair] = pltpu.make_async_copy(
            sources[1].at[heads], weights_ref.at[heads], sem.at[5 + pair]
        )
    for which in (0, *((1, pair) for pair in range(pairs)), 3, 2, 4):
        copies[which].start()
    count, width = grad_mixed_ref.shape
    small = small_ref[...].astype(F32)
    masks = head_masks(count)
    factor = HEAD_DIM**-0.5
    copies[0].wait()
    for pair in range(pairs):
        lanes = slice(pair * 2 * HEAD_DIM, (pair + 1) * 2 * HEAD_DIM)
        q, k, v = proj_ref[0, :, lanes], proj_ref[1, :, lanes], proj_ref[2, :, lanes]
        gm = grad_mixed_ref[:, lanes]
        copies[1, pair].wait()
        parts = []
        for half in range(2):
            weights = weights_ref[2 * pair + half]
            probs = weights.astype(F32)
            grad_probs = dot_nt(v, jnp.where(masks[half], gm, BF(0)))
            total = jnp.sum(probs * grad_probs, axis=0, keepdims=True)
            grad_scores = (probs * (grad_probs - total)).astype(BF)
            parts.append(
                (dot_tn(grad_scores, k), dot_nn(grad_scores, q), dot_nn(weights, gm))
            )
        for s in range(3):
            both = jnp.where(masks[0], parts[0][s], parts[1][s])
            gp_ref[s, :, lanes] = (both * factor if s < 2 else both).astype(BF)
    gp_send = pltpu.make_async_copy(gp_ref, gp_far, sem.at[5 + pairs])
    gp_send.start()
    copies[3].wait()
    unit1, _ = unit_of(x_ref[0].astype(F32))
    n1 = (unit1 * small[8:9, :]).astype(BF)
    copies[2].wait()
    product = jnp.zeros((width, width), F32)
    for s in range(3):
        grad = dot_tn(n1, gp_ref[s])
        place_grads(fast, reps, shards_n, pack_ref, s, grad)
        product = product + full_ref[s].astype(F32) * grad
    copies[4].wait()
    place_grads(fast, reps, shards_n, pack_ref, 3, grad_out_ref[...])
    ones = jnp.ones((8, width), BF)
    high = product.astype(BF)
    low = (product - high.astype(F32)).astype(BF)
    grad_gain1 = (dot_nt(ones, high) + dot_nt(ones, low))[0:1] / small[8:9, :]
    sums = jnp.where(iota((16, width), 0) == 8, grad_gain1, early_ref[...])
    sends = [gp_send]
    if fast:
        depth = width // shards_n
        rows = depth // reps
        for z in range(shards_n):
            for half in range(2):
                eight = sums[8 * half : 8 * half + 8, z * depth : (z + 1) * depth]
                eight = jnp.concatenate([eight, jnp.zeros((8, width - depth), F32)], axis=1)
                pack_ref[half, z, 2 * reps * rows :, :] = eight.astype(BF)
        for i in range(2):
            send = pltpu.make_async_copy(pack_ref.at[core ^ i], (mine_ref, twin_ref)[i], sem.at[i])
            send.start()
            sends.append(send)
    else:
        sums_ref[...] = sums
    for send in sends:
        send.wait()


def backward(fast, reps, shards_n, where, grad_mixed, small, early, proj, weights, full, x, grad_out):
    _, count, width = x.shape
    sources = (proj, weights, full, x, grad_out)
    held = pl.BlockSpec(memory_space=pltpu.HBM)
    outs = [pltpu.HBM((3, count, width), BF)]
    scratch = [pltpu.VMEM((3, count, width), BF)]
    if fast:
        part = (shards_n, 2 * reps * (width // shards_n // reps) + 8, width)
        outs += [pltpu.HBM(part, BF)] * 2
        out_specs = [held] * 3
        scratch = [pltpu.VMEM((2, *part), BF)] + scratch
    else:
        outs += [
            jax.ShapeDtypeStruct((4, width, width), BF),
            jax.ShapeDtypeStruct((16, width), F32),
        ]
        out_specs = [held] + vmem(2)
    return pl.pallas_call(
        lambda *refs: backward_body(fast, reps, shards_n, *refs),
        out_shape=tuple(outs),
        in_specs=[pl.BlockSpec(memory_space=pltpu.SMEM)] + vmem(3) + [held] * 5,
        out_specs=tuple(out_specs),
        scratch_shapes=[
            *scratch,
            *(pltpu.VMEM(v.shape, v.dtype) for v in sources),
            pltpu.SemaphoreType.DMA((6 + HEADS // 2,)),
        ],
        compiler_params=params(40),
        cost_estimate=SMALL,
        name="backward",
    )(where, grad_mixed, small, early, *(far(v) for v in sources))


def input_back_body(gp_ref, full_ref, x_ref, grad_resid_ref, small_ref, grad_x_ref):
    small = small_ref[...].astype(F32)
    grad_n1 = dot_nt(gp_ref[0], full_ref[0])
    for s in range(1, 3):
        grad_n1 = grad_n1 + dot_nt(gp_ref[s], full_ref[s])
    unit1, inv1 = unit_of(x_ref[0].astype(F32))
    b = grad_n1 * small[8:9, :]
    grad_x = grad_resid_ref[...] + inv1 * (
        b
        - jnp.mean(b, axis=-1, keepdims=True)
        - unit1 * jnp.mean(b * unit1, axis=-1, keepdims=True)
    )
    grad_x_ref[0] = grad_x.astype(BF)


def input_back(gp, full, x, grad_resid, small):
    _, width = grad_resid.shape
    return pl.pallas_call(
        input_back_body,
        out_shape=pltpu.HBM(x.shape, BF),
        in_specs=vmem(5),
        out_specs=vmem(1)[0],
        compiler_params=params(20),
        cost_estimate=SMALL,
        name="input_back",
    )(far(gp), far(full), far(x), far(grad_resid), small)


def result_body(out_ref, index_ref, resid_ref, result_ref):
    total = resid_ref[...]
    count = total.shape[0]
    index = index_ref[...]
    for e in range(EXPERTS):
        row = iota((ROWS, count), 0) + e * ROWS
        pick = (row == index[0:1, :]) | (row == index[1:2, :])
        total = total + dot_tn(jnp.where(pick, 1.0, 0.0).astype(BF), out_ref[e])
    result_ref[0] = total.astype(BF)


def combine(out, index, resid):
    count, width = resid.shape
    return pl.pallas_call(
        result_body,
        out_shape=jax.ShapeDtypeStruct((1, count, width), BF),
        in_specs=vmem(3),
        out_specs=vmem(1)[0],
        compiler_params=params(8),
        cost_estimate=SMALL,
        name="combine",
    )(far(out), index, far(resid))


def plain(body, outs, *operands):
    return pl.pallas_call(
        body,
        out_shape=tuple(outs) if len(outs) > 1 else outs[0],
        in_specs=vmem(len(operands)),
        out_specs=tuple(vmem(len(outs))) if len(outs) > 1 else vmem(1)[0],
        compiler_params=params(16),
        cost_estimate=SMALL,
        name=body.__name__,
    )(*operands)


def first_sums(stay0_ref, come0_ref, stay1_ref, come1_ref, keep_ref, go0_ref, go1_ref):
    for half, (stay, come, go) in enumerate(
        ((stay0_ref, come0_ref, go0_ref), (stay1_ref, come1_ref, go1_ref))
    ):
        keep_ref[half] = (stay[0].astype(F32) + come[0].astype(F32)).astype(BF)
        go[...] = (stay[1].astype(F32) + come[1].astype(F32)).astype(BF)


def second_sums(keep_ref, come0_ref, come1_ref, sum_ref):
    for half, come in enumerate((come0_ref, come1_ref)):
        sum_ref[half] = (keep_ref[half].astype(F32) + come[...].astype(F32)).astype(BF)


def pair_sum(a_ref, b_ref, sum_ref):
    sum_ref[...] = (a_ref[...].astype(F32) + b_ref[...].astype(F32)).astype(BF)


def line_sum(parts_ref, tall_ref, small_ref):
    total = parts_ref[0].astype(F32)
    for i in range(1, parts_ref.shape[0]):
        total = total + parts_ref[i].astype(F32)
    rows = tall_ref.shape[0] * tall_ref.shape[1]
    for p in range(tall_ref.shape[0]):
        short = tall_ref.shape[1]
        tall_ref[p] = total[p * short : (p + 1) * short].astype(BF)
    small_ref[...] = total[rows:].astype(BF)


def plane_sum(parts_ref, small_ref, shares_ref):
    total = parts_ref[0].astype(F32)
    for i in range(1, parts_ref.shape[0]):
        total = total + parts_ref[i].astype(F32)
    short = total.shape[0]
    for r in range(shares_ref.shape[0]):
        shares_ref[r, 0:short, :] = total.astype(BF)
        shares_ref[r, short:, :] = small_ref[...]


def widen_body(places, aliased, where_ref, *refs):
    n = len(places)
    taken, wide, sem_in, sem_out = refs[-4:]
    outs = refs[-6:-4]
    srcs = refs[: len(refs) - 6 - 2 * aliased]
    _, depth, cols = srcs[0].shape[-3:]
    pieces = [ref.at[half] for ref in srcs for half in range(2)] if len(srcs) < n else srcs
    fetch = [pltpu.make_async_copy(pieces[i], taken.at[i], sem_in.at[i]) for i in range(n)]
    for copy in fetch:
        copy.start()
    sent = []
    for i, (other, k, half) in enumerate(places):
        fetch[i].wait()
        row = pl.multiple_of((where_ref[1] ^ k) * depth, depth)
        for which in range(2):
            wide[i, which] = taken[i, which].astype(F32)
            spot = outs[which].at[
                where_ref[0] ^ other, pl.ds(row, depth), half * cols : (half + 1) * cols
            ]
            copy = pltpu.make_async_copy(wide.at[i, which], spot, sem_out.at[i, which])
            copy.start()
            sent.append(copy)
    for copy in sent:
        copy.wait()


def widen(where, places, sources, shape, so_far=None):
    n = len(places)
    part = sources[0].shape[-3:]
    aliased = so_far is not None
    held = pl.BlockSpec(memory_space=pltpu.HBM)
    operands = [far(source) for source in sources] + (list(so_far) if aliased else [])
    return pl.pallas_call(
        lambda *refs: widen_body(places, aliased, *refs),
        out_shape=(pltpu.HBM(shape, F32), pltpu.HBM(shape, F32)),
        in_specs=[pl.BlockSpec(memory_space=pltpu.SMEM)] + [held] * len(operands),
        out_specs=(held, held),
        scratch_shapes=[
            pltpu.VMEM((n, *part), BF),
            pltpu.VMEM((n, *part), F32),
            pltpu.SemaphoreType.DMA((n,)),
            pltpu.SemaphoreType.DMA((n, 2)),
        ],
        input_output_aliases={len(sources) + 1: 0, len(sources) + 2: 1} if aliased else {},
        compiler_params=params(24),
        cost_estimate=SMALL,
        name="widen",
    )(where, *operands)


def finish_body(rows, parts_ref, qkv_ref, out_ref, router_ref, gains_ref):
    reps = parts_ref.shape[0]
    depth = out_ref.shape[0]
    for r in range(reps):
        for s in range(3):
            qkv_ref[s, r * rows : (r + 1) * rows, :] = parts_ref[
                r, s * rows : (s + 1) * rows, :
            ].astype(F32)
        out_ref[r * rows : (r + 1) * rows, :] = parts_ref[r, 3 * rows : 4 * rows, :].astype(F32)
    smalls = []
    for half in range(2):
        total = jnp.zeros((8, depth), F32)
        for peer in range(reps // 2):
            total = total + parts_ref[2 * peer + half].astype(F32)[4 * rows :, 0:depth]
        smalls.append(total)
    router_ref[...] = smalls[0]
    gains_ref[...] = smalls[1][0:2]


def finish(parts, rows):
    reps, _, width = parts.shape
    depth = rows * reps
    return pl.pallas_call(
        lambda *refs: finish_body(rows, *refs),
        out_shape=(
            jax.ShapeDtypeStruct((3, depth, width), F32),
            jax.ShapeDtypeStruct((depth, width), F32),
            jax.ShapeDtypeStruct((EXPERTS, depth), F32),
            jax.ShapeDtypeStruct((2, depth), F32),
        ),
        in_specs=vmem(1),
        out_specs=tuple(vmem(4)),
        compiler_params=params(4),
        name="finish",
    )(parts)


def shards(reps, shards_n, *args):
    tokens, segments, choices, priority, cotangent = args[:5]
    qkv_weights, out_weight, router_weight, gains, w_in, w_out = args[5:]
    rep, shard = lax.axis_index("rep"), lax.axis_index("shard")
    width, hidden = w_in.shape[1:]
    owned = w_in.shape[0]
    peers = reps // owned
    depth = width // shards_n
    fast = depth % (16 * reps) == 0 and depth == 128 and owned == 2 and peers == 4
    if not fast and owned != 1:
        raise NotImplementedError("mesh")
    column = [
        [(c * owned + e % owned) * shards_n + e // owned for e in range(EXPERTS)]
        for c in range(peers)
    ]

    def to_experts(rows):
        return lax.all_to_all(rows, AXES, 0, 0, axis_index_groups=column, tiled=True)

    where = jnp.stack([rep % owned, rep // owned]).astype(jnp.int32)
    index, cot_sent = route(choices[0].T, priority, cotangent)
    if fast:
        smalls, pieces, lines = gather_weights(
            rep, shard, reps, shards_n, qkv_weights, out_weight, router_weight.T, gains
        )
        place = jnp.stack([rep, shard]).astype(jnp.int32)
        weights_in = (qkv_weights, out_weight, smalls)
    else:
        place, pieces, lines = None, [], []
        weights_in = (
            lax.all_gather(qkv_weights, "shard", axis=1, tiled=True),
            lax.all_gather(out_weight, "shard", axis=0, tiled=True),
            lax.all_gather(router_weight, "shard", axis=0, tiled=True).T,
            lax.all_gather(gains, "shard", axis=1, tiled=True),
        )
    cot_in = to_experts(after(cot_sent, *lines))
    sent, small, gates, *kept = forward(
        fast, place, tokens, segments, index, weights_in, pieces
    )
    n2_in = to_experts(sent)

    def peer(value, k):
        return lax.ppermute(value, "rep", [(i, i ^ k) for i in range(reps)])

    through = cot_hidden(where, cot_in, w_out)
    back, out, *parts_in = experts(where, n2_in, cot_in, through, w_in, w_out)
    grads = expert_grads(where, fast, *parts_in)
    back_in = to_experts(back)
    out_in = to_experts(after(out, back_in))
    if fast:
        axes = ((owned, 2 * owned), (2 * owned, owned))
        halves = [peer(grads[2 * half], axes[half][0]) for half in range(2)]
        back_in = after(back_in, *grads)
    full, weights, proj, mixed, resid = kept
    grad_resid, grad_mixed, grad_out_w, early_sums = tokens_back(
        back_in, cotangent, index, small, gates, full, mixed, resid
    )
    if fast:
        grad_mixed, *halves = lax.optimization_barrier((grad_mixed, *halves))
        part = halves[0].shape[1:]
        small_part = jax.ShapeDtypeStruct(part, BF)
        keep, *leaves = plain(
            first_sums,
            [jax.ShapeDtypeStruct((2, *part), BF), small_part, small_part],
            grads[1],
            halves[0],
            grads[3],
            halves[1],
        )
        arrived = [peer(leaves[half], axes[half][1]) for half in range(2)]
        grad_mixed = after(grad_mixed, keep)
    grad_proj, *packs = backward(
        fast,
        reps,
        shards_n,
        where,
        grad_mixed,
        small,
        early_sums,
        proj,
        weights,
        full,
        tokens,
        grad_out_w,
    )
    grad_tokens = input_back(grad_proj, full, tokens, grad_resid, small)
    result = combine(out_in, index, kept[4])
    if fast:
        mine, twin, *arrived = lax.optimization_barrier((*packs, *arrived))
        total = plain(second_sums, [jax.ShapeDtypeStruct(keep.shape, BF)], keep, *arrived)
        twin = after(twin, total)
        chip = plain(pair_sum, [jax.ShapeDtypeStruct(mine.shape, BF)], mine, peer(twin, 1))
        line = lax.all_to_all(after(chip, out_in), "shard", 0, 0, tiled=True)
        short = 2 * depth // peers
        line, own_small = plain(
            line_sum,
            [
                jax.ShapeDtypeStruct((peers, short, width), BF),
                jax.ShapeDtypeStruct((8, width), BF),
            ],
            line,
        )
        early = [total] + [peer(total, k * owned) for k in (1, 2)]
        grad_tokens, *early = lax.optimization_barrier((grad_tokens, *early))
        late = [
            peer(early[axes[half][0] // owned][half], 3 * owned - axes[half][0]) for half in range(2)
        ]
        early += [peer(value, 1) for value in early]
        shape = (owned, width, hidden)
        places = [(other, k, half) for other in range(2) for k in range(3) for half in range(2)]
        so_far = widen(where, places, early, shape)
        plane_groups = [[p * owned + c for p in range(peers)] for c in range(owned)]
        plane = lax.all_to_all(line, "rep", 0, 0, axis_index_groups=plane_groups, tiled=True)
        plane, *so_far = lax.optimization_barrier((plane, *so_far))
        share = plain(
            plane_sum, [jax.ShapeDtypeStruct((reps, short + 8, width), BF)], plane, own_small
        )
        share, *late = lax.optimization_barrier((share, *late))
        late += [peer(value, 1) for value in late]
        parts = lax.all_to_all(share, "rep", 0, 0, tiled=True)
        places = [(other, 3, half) for other in range(2) for half in range(2)]
        grad_w_in, grad_w_out = widen(where, places, late, shape, so_far)
        parts = after(parts, grad_w_in, result)
        grad_qkv, grad_out, grad_router, grad_gains = finish(parts, depth // reps)
        grad_router = grad_router.T
    else:
        share = lax.psum_scatter(grads[0], "rep", scatter_dimension=1, tiled=True)
        every = lax.all_gather(share, "rep", axis=1, tiled=True).astype(F32)
        grad_w_in, grad_w_out = every[0:1], every[1:2]
        pack, sums = packs
        owned_rows = lax.psum_scatter(pack, "shard", scatter_dimension=1, tiled=True)
        owned_rows = lax.psum(owned_rows, "rep").astype(F32)
        grad_qkv, grad_out = owned_rows[0:3], owned_rows[3]
        sums = lax.psum(sums, AXES)
        mine = lax.dynamic_slice_in_dim(sums, shard * depth, depth, axis=1)
        grad_router, grad_gains = mine[0:EXPERTS].T, mine[EXPERTS : EXPERTS + 2]
    return (
        result,
        grad_tokens,
        grad_qkv,
        grad_out,
        grad_router,
        grad_gains,
        grad_w_in,
        grad_w_out,
    )


def solution(mesh):
    reps, shards_n = mesh.shape["rep"], mesh.shape["shard"]
    rows = P(("rep", "shard"), None, None)
    flat = P(("rep", "shard"), None)
    first = P("shard", None)
    stack = P("shard", None, None)
    second = P(None, "shard", None)
    return jax.shard_map(
        lambda *args: shards(reps, shards_n, *args),
        mesh=mesh,
        in_specs=(
            rows, flat, rows, flat, rows, second, first, first, P(None, "shard"), stack, stack,
        ),
        out_specs=(rows, rows, second, first, first, P(None, "shard"), stack, stack),
        check_vma=False,
    )
```

```python
import jax
import jax.numpy as jnp
from jax import lax
from jax.experimental import pallas as pl
from jax.experimental.pallas import tpu as pltpu
from jax.sharding import PartitionSpec as P

HEADS = 8
HEAD_DIM = 64
EXPERTS = 8
CAPACITY = 135
ROWS = 136
EPS = 1e-06
F32 = jnp.float32
BF = jnp.bfloat16
AXES = ("rep", "shard")
FF_STEP = 512
KEPT = 5
SMALL = pl.CostEstimate(flops=1000, bytes_accessed=1000, transcendentals=0)
GELU_A = 0.7978845608028654
GELU_B = 0.044715


def dot_nn(a, b):
    return lax.dot_general(a, b, (((1,), (0,)), ((), ())), preferred_element_type=F32)


def dot_nt(a, b):
    return lax.dot_general(a, b, (((1,), (1,)), ((), ())), preferred_element_type=F32)


def dot_tn(a, b):
    return lax.dot_general(a, b, (((0,), (0,)), ((), ())), preferred_element_type=F32)


def after(value, *others):
    return lax.optimization_barrier((value, *others))[0]


def iota(shape, dim):
    return lax.broadcasted_iota(jnp.int32, shape, dim)


def unit_of(values):
    mean = jnp.mean(values, axis=-1, keepdims=True)
    centered = values - mean
    inv = lax.rsqrt(jnp.mean(centered * centered, axis=-1, keepdims=True) + EPS)
    return centered * inv, inv


def split3(values):
    high = values.astype(BF)
    rest = values - high.astype(F32)
    mid = rest.astype(BF)
    low = (rest - mid.astype(F32)).astype(BF)
    return high, mid, low


def piece_rows(values):
    high, mid, low = split3(values)
    shape = (8, values.shape[1])
    row = iota(shape, 0)
    parts = [jnp.broadcast_to(part.astype(F32), shape) for part in (high, mid, low)]
    return jnp.where(
        row == 0, parts[0], jnp.where(row == 1, parts[1], jnp.where(row == 2, parts[2], 0.0))
    )


def side_row(pieces, width):
    wide = jnp.concatenate([pieces, jnp.zeros((8, width - ROWS), F32)], axis=1)
    row = iota((8, width), 0)
    moved = jnp.where(
        row == 0,
        wide,
        jnp.where(row == 1, pltpu.roll(wide, ROWS, 1), pltpu.roll(wide, 2 * ROWS, 1)),
    )
    return jnp.sum(jnp.where(row < 3, moved, 0.0), axis=0, keepdims=True)


def side_parts(side):
    width = side.shape[1]
    wide = jnp.broadcast_to(side, (8, width))
    row = iota((8, width), 0)
    back = jnp.where(
        row == 0,
        wide,
        jnp.where(row == 1, pltpu.roll(wide, width - ROWS, 1), pltpu.roll(wide, width - 2 * ROWS, 1)),
    )
    return jnp.where(row < 3, back, 0.0)[:, 0:ROWS]


def far(value):
    return pltpu.with_memory_space_constraint(value, pltpu.HBM)


def near(value):
    return pltpu.with_memory_space_constraint(value, pltpu.VMEM)


def vmem(n):
    return [pl.BlockSpec(memory_space=pltpu.VMEM)] * n


def params(mib):
    return pltpu.CompilerParams(vmem_limit_bytes=mib << 20)


def route_body(choice_ref, prio_ref, cot_ref, index_ref, sent_ref):
    count = cot_ref.shape[-2]
    choice = choice_ref[...]
    experts = iota((EXPERTS, count), 0)
    first = jnp.where(choice[0:1, :] == experts, 1.0, 0.0)
    second = jnp.where(choice[1:2, :] == experts, 1.0, 0.0)
    order = jnp.where(iota((count, count), 0) == prio_ref[...], 1.0, 0.0).astype(BF)
    earlier = jnp.where(iota((count, count), 0) < iota((count, count), 1), 1.0, 0.0).astype(BF)
    both = jnp.concatenate([first, second], axis=0).astype(BF)
    before = dot_nn(dot_nt(both, order).astype(BF), earlier)
    held = jnp.sum(first, axis=1, keepdims=True)
    before = jnp.concatenate([before[0:EXPERTS], before[EXPERTS:] + held], axis=0)
    before = dot_nn(jnp.minimum(before, 255.0).astype(BF), order)
    slot0 = jnp.sum(first * before[0:EXPERTS], axis=0, keepdims=True)
    slot1 = jnp.sum(second * before[EXPERTS:], axis=0, keepdims=True)
    slot = jnp.concatenate([slot0, slot1], axis=0).astype(jnp.int32)
    index = jnp.where(slot < CAPACITY, choice * ROWS + slot, -1)
    index_ref[...] = index
    cot = cot_ref[0]
    for e in range(EXPERTS):
        row = iota((ROWS, count), 0) + e * ROWS
        pick = (row == index[0:1, :]) | (row == index[1:2, :])
        sent_ref[e] = dot_nn(jnp.where(pick, 1.0, 0.0).astype(BF), cot).astype(BF)


def route(choice_t, prio, cot):
    _, count, width = cot.shape
    return pl.pallas_call(
        route_body,
        out_shape=(
            jax.ShapeDtypeStruct((2, count), jnp.int32),
            pltpu.HBM((EXPERTS, ROWS, width), BF),
        ),
        in_specs=vmem(3),
        out_specs=tuple(vmem(2)),
        compiler_params=params(12),
        cost_estimate=SMALL,
        name="route",
    )(far(choice_t), far(prio), far(cot))


def pack_body(where_ref, qkv_ref, out_ref, router_ref, gains_ref, pack_ref):
    rows = pack_ref.shape[1]
    start = pl.multiple_of(where_ref[0] * rows, rows)
    for s in range(3):
        pack_ref[s] = qkv_ref[s, pl.ds(start, rows), :]
    pack_ref[3] = out_ref[pl.ds(start, rows), :]
    depth = router_ref.shape[1]
    small = jnp.concatenate(
        [router_ref[...].astype(F32), gains_ref[...].astype(F32), jnp.zeros((6, depth), F32)],
        axis=0,
    )
    pack_ref[4, :, 0:depth] = small.astype(BF)
    pack_ref[4, :, depth:] = jnp.zeros((rows, pack_ref.shape[2] - depth), BF)


def pack_weights(rep, qkv, out, router, gains, rows):
    width = out.shape[1]
    return pl.pallas_call(
        pack_body,
        out_shape=jax.ShapeDtypeStruct((5, rows, width), BF),
        in_specs=[pl.BlockSpec(memory_space=pltpu.SMEM)] + vmem(4),
        out_specs=vmem(1)[0],
        compiler_params=params(4),
        name="pack_weights",
    )(rep.reshape(1), far(qkv), far(out), far(router), far(gains))


def gather_weights(rep, shard, reps, shards_n, qkv, out, router, gains):
    rows = qkv.shape[1] // reps
    pack = pack_weights(rep, qkv, out, router, gains, rows)
    lines = [
        lax.ppermute(pack, "shard", [(i, i ^ dz) for i in range(shards_n)])
        for dz in range(1, shards_n)
    ]
    block = jnp.stack([piece[0:4] for piece in lines])
    smalls = jnp.stack([piece[4] for piece in [pack] + lines])
    spread = [block] + [
        lax.ppermute(block, "rep", [(i, i ^ k) for i in range(reps)]) for k in range(2, reps, 2)
    ]
    twin = [lax.ppermute(piece, "rep", [(i, i ^ 1) for i in range(reps)]) for piece in spread]
    pieces = []
    for own, other in zip(spread, twin, strict=True):
        pieces += [own, other]
    return smalls, pieces, lines


def fill_weights(rep, shard, qkv_ref, out_ref, smalls_ref, piece_refs, full_ref, small_ref):
    depth = out_ref.shape[0]
    own = pl.multiple_of(shard * depth, depth)
    for s in range(3):
        full_ref[s, pl.ds(own, depth), :] = qkv_ref[s]
    full_ref[3, pl.ds(own, depth), :] = out_ref[...]
    small_ref[:, pl.ds(own, depth)] = smalls_ref[0, :, 0:depth]
    for far in range(1, smalls_ref.shape[0]):
        base = pl.multiple_of((shard ^ far) * depth, depth)
        small_ref[:, pl.ds(base, depth)] = smalls_ref[far, :, 0:depth]
        for k, piece in enumerate(piece_refs):
            rows = piece.shape[2]
            start = pl.multiple_of(base + (rep ^ k) * rows, rows)
            for s in range(4):
                full_ref[s, pl.ds(start, rows), :] = piece[far - 1, s]


def head_masks(count):
    lane = iota((count, 2 * HEAD_DIM), 1)
    return [lane < HEAD_DIM, lane >= HEAD_DIM]


def kept_shapes(count, width):
    return (
        ((4, width, width), BF),
        ((HEADS, count, count), BF),
        ((3, count, width), BF),
        ((count, width), BF),
        ((count, width), F32),
    )


def kept_copies(sources, targets, sem):
    copies = {
        i: pltpu.make_async_copy(sources[i], targets[i], sem.at[i]) for i in range(KEPT) if i != 1
    }
    for pair in range(HEADS // 2):
        heads = pl.ds(2 * pair, 2)
        copies[1, pair] = pltpu.make_async_copy(
            sources[1].at[heads], targets[1].at[heads], sem.at[KEPT + pair]
        )
    return copies


def forward_body(fast, n_pieces, *refs):
    if fast:
        where_ref, x_ref, seg_ref, index_ref, qkv_ref, out_ref, smalls_ref = refs[:7]
        piece_refs = refs[7 : 7 + n_pieces]
        refs = refs[7 + n_pieces :]
    else:
        x_ref, seg_ref, index_ref, qkv_ref, out_ref, router_ref, gains_ref = refs[:7]
        refs = refs[7:]
    sent_ref, small_ref, gate_ref, *kept = refs[: 3 + KEPT]
    full_ref, weights_ref, proj_ref, mixed_ref, resid_ref = held = refs[3 + KEPT : -1]
    copies = kept_copies(held, kept, refs[-1])
    if fast:
        fill_weights(
            where_ref[0], where_ref[1], qkv_ref, out_ref, smalls_ref, piece_refs, full_ref, small_ref
        )
    else:
        full_ref[0:3] = qkv_ref[...]
        full_ref[3] = out_ref[...]
        small_ref[...] = jnp.concatenate(
            [
                router_ref[...].astype(F32),
                gains_ref[...].astype(F32),
                jnp.zeros((6, out_ref.shape[1]), F32),
            ],
            axis=0,
        ).astype(BF)
    copies[0].start()
    x = x_ref[0].astype(F32)
    count, width = x.shape
    small = small_ref[...].astype(F32)
    unit1, _ = unit_of(x)
    n1 = (unit1 * small[8:9, :]).astype(BF)
    for s in range(3):
        proj_ref[s] = dot_nn(n1, full_ref[s]).astype(BF)
    copies[2].start()
    document = jnp.where(iota((8, count), 0) == seg_ref[...], 1.0, 0.0).astype(BF)
    bias = jnp.where(dot_tn(document, document) > 0.5, 0.0, -1e30)
    masks = head_masks(count)
    for pair in range(HEADS // 2):
        lanes = slice(pair * 2 * HEAD_DIM, (pair + 1) * 2 * HEAD_DIM)
        q, k, v = proj_ref[0, :, lanes], proj_ref[1, :, lanes], proj_ref[2, :, lanes]
        q = q * BF(HEAD_DIM**-0.5)
        halves = []
        for half in range(2):
            scores = dot_nt(k, jnp.where(masks[half], q, BF(0))) + bias
            top = jnp.max(scores, axis=0, keepdims=True)
            terms = jnp.exp(scores - top)
            total = jnp.sum(terms, axis=0, keepdims=True)
            weights = (terms * (1.0 / total)).astype(BF)
            weights_ref[2 * pair + half] = weights
            halves.append(dot_tn(weights, v))
        copies[1, pair].start()
        mixed_ref[:, lanes] = jnp.where(masks[0], halves[0], halves[1]).astype(BF)
    copies[3].start()
    resid = x + dot_nn(mixed_ref[...], full_ref[3])
    resid_ref[...] = resid
    copies[4].start()
    unit2, _ = unit_of(resid)
    n2 = (unit2 * small[9:10, :]).astype(BF)
    logits = dot_nt(small_ref[...], n2)[0:EXPERTS]
    terms = jnp.exp(logits - jnp.max(logits, axis=0, keepdims=True))
    gates = terms / jnp.sum(terms, axis=0, keepdims=True)
    gate_ref[...] = gates
    index = index_ref[...]
    for e in range(EXPERTS):
        row = iota((ROWS, count), 0) + e * ROWS
        pick = (row == index[0:1, :]) | (row == index[1:2, :])
        pick = jnp.where(pick, 1.0, 0.0).astype(BF)
        rows = dot_nn(pick, n2)
        side = side_row(dot_nt(piece_rows(gates[e : e + 1, :]).astype(BF), pick), width)
        last = iota((ROWS, 1), 0) == CAPACITY
        sent_ref[e] = jnp.where(last, side, rows).astype(BF)
    for copy in copies.values():
        copy.wait()


def forward(fast, where, x, seg, index, weights_in, pieces):
    _, count, width = x.shape
    body = lambda *refs: forward_body(fast, len(pieces), *refs)
    operands = [far(x), far(seg), index, *(far(w) for w in weights_in[:2]), *weights_in[2:], *pieces]
    specs = vmem(len(operands))
    if fast:
        operands = [where] + operands
        specs = [pl.BlockSpec(memory_space=pltpu.SMEM)] + specs
    shown = (
        pltpu.HBM((EXPERTS, ROWS, width), BF),
        jax.ShapeDtypeStruct((16, width), BF),
        jax.ShapeDtypeStruct((EXPERTS, count), F32),
    )
    kept = kept_shapes(count, width)
    return pl.pallas_call(
        body,
        out_shape=(*shown, *(pltpu.HBM(*k) for k in kept)),
        in_specs=specs,
        out_specs=(*vmem(3), *([pl.BlockSpec(memory_space=pltpu.HBM)] * KEPT)),
        scratch_shapes=[
            *(pltpu.VMEM(*k) for k in kept),
            pltpu.SemaphoreType.DMA((KEPT + HEADS // 2,)),
        ],
        compiler_params=params(40),
        cost_estimate=SMALL,
        name="forward",
    )(*operands)


def cot_hidden_body(where_ref, cot_ref, w_out_ref, through_ref):
    rows = jnp.concatenate([cot_ref[g].astype(F32) for g in range(2)], axis=0).astype(BF)
    for start in range(0, w_out_ref.shape[2], FF_STEP):
        cols = slice(start, start + FF_STEP)
        through_ref[:, cols] = dot_nn(rows, w_out_ref[0, :, cols])


def cot_hidden(where, cot, w_out):
    groups, _, width = cot.shape
    hidden_n = w_out.shape[2]
    return pl.pallas_call(
        cot_hidden_body,
        out_shape=pltpu.HBM((groups * ROWS, hidden_n), F32),
        grid_spec=pltpu.PrefetchScalarGridSpec(
            num_scalar_prefetch=1,
            grid=(groups // 2,),
            in_specs=[
                pl.BlockSpec((2, ROWS, width), lambda i, w: (i, 0, 0)),
                pl.BlockSpec((1, width, hidden_n), lambda i, w: (w[0], 0, 0)),
            ],
            out_specs=pl.BlockSpec((2 * ROWS, hidden_n), lambda i, w: (i, 0)),
        ),
        compiler_params=params(24),
        cost_estimate=SMALL,
        name="cot_hidden",
    )(where, cot, far(w_out))


def expert_rows(n2_ref, cot_ref, through_ref, w_in_ref, w_out_ref, back_ref, out_ref, span, scratch):
    hidden_ref, pre_ref, rows_ref, gso_ref = scratch
    row = iota((ROWS, 1), 0)
    eye = jnp.where(iota((ROWS, ROWS), 0) == iota((ROWS, ROWS), 1), 1.0, 0.0).astype(BF)
    gates, rows_all, gso_all = [], [], []
    for g in range(2):
        rows = n2_ref[g].astype(F32)
        parts = side_parts(rows[CAPACITY : CAPACITY + 1]).astype(BF)
        gate = jnp.sum(dot_nt(eye, parts), axis=1, keepdims=True)
        gates.append(gate)
        rows_all.append(jnp.where(row < CAPACITY, rows, 0.0))
        gso_all.append(gate * cot_ref[g].astype(F32))
    rows = jnp.concatenate(rows_all, axis=0).astype(BF)
    gate_col = jnp.concatenate(gates, axis=0)
    rows_ref[span], gso_ref[span] = rows, jnp.concatenate(gso_all, axis=0).astype(BF)
    for start in range(0, w_in_ref.shape[2], FF_STEP):
        cols = slice(start, start + FF_STEP)
        u = dot_nn(rows, w_in_ref[0, :, cols])
        square = u * u
        t = jnp.tanh(GELU_A * (u + GELU_B * (u * square)))
        half = 0.5 * (1.0 + t)
        hidden = u * half
        slope = half + hidden * (1.0 - t) * (GELU_A * (1.0 + 3.0 * GELU_B * square))
        hidden_ref[span, cols] = hidden.astype(BF)
        pre_ref[span, cols] = (through_ref[:, cols] * (gate_col * slope)).astype(BF)
    grad_in = dot_nt(pre_ref[span], w_in_ref[0])
    result = dot_nt(hidden_ref[span], w_out_ref[0])
    lane = iota((ROWS, 8), 1)
    for g in range(2):
        part = slice(g * ROWS, (g + 1) * ROWS)
        out = (gates[g] * result[part]).astype(BF)
        out_ref[g] = out
        inner = jnp.sum(out.astype(F32) * cot_ref[g].astype(F32), axis=1, keepdims=True)
        high, mid, low = (piece.astype(F32) for piece in split3(inner))
        pieces = jnp.where(lane == 0, high, jnp.where(lane == 1, mid, jnp.where(lane == 2, low, 0.0)))
        side = side_row(dot_tn(pieces.astype(BF), eye), out.shape[1])
        back_ref[g] = jnp.where(row == CAPACITY, side, grad_in[part]).astype(BF)


def experts_body(where_ref, *refs):
    expert_rows(*refs[:7], slice(None), refs[7:])


def experts(where, n2, cot, through, w_in, w_out):
    groups, _, width = n2.shape
    hidden_n = w_in.shape[2]
    total = groups * ROWS
    weight = pl.BlockSpec((1, width, hidden_n), lambda i, w: (w[0], 0, 0))
    payload = pl.BlockSpec((2, ROWS, width), lambda i, w: (i, 0, 0))
    narrow = pl.BlockSpec((2 * ROWS, width), lambda i, w: (i, 0))
    wide = pl.BlockSpec((2 * ROWS, hidden_n), lambda i, w: (i, 0))
    return pl.pallas_call(
        experts_body,
        out_shape=(
            [pltpu.HBM((groups, ROWS, width), BF)] * 2
            + [pltpu.HBM((total, hidden_n), BF)] * 2
            + [pltpu.HBM((total, width), BF)] * 2
        ),
        grid_spec=pltpu.PrefetchScalarGridSpec(
            num_scalar_prefetch=1,
            grid=(groups // 2,),
            in_specs=[payload, payload, wide, weight, weight],
            out_specs=[payload, payload, wide, wide, narrow, narrow],
        ),
        compiler_params=params(44),
        cost_estimate=SMALL,
        name="experts",
    )(where, n2, cot, through, far(w_in), far(w_out))


def expert_grads_body(split, where_ref, hidden_ref, pre_ref, rows_ref, gso_ref, *refs):
    grad_refs, sum_ref = refs[:-1], refs[-1]
    step, steps = pl.program_id(0), pl.num_programs(0)
    for half, (left, right) in enumerate(((rows_ref, pre_ref), (gso_ref, hidden_ref))):
        grad = dot_tn(left[...], right[...]).astype(BF)
        if not split:
            grad_refs[0][half] = grad
            continue
        sum_ref[half] = grad
    if not split:
        return
    depth = sum_ref.shape[1] // 4
    for late in range(2):

        @pl.when((step < steps // 2) if late == 0 else (step >= steps // 2))
        def _(late=late):
            for half in range(2):
                for k in range(4):
                    start = pl.multiple_of((where_ref[1] ^ k) * depth, depth)
                    goes = k == 3 or k == 1 + late
                    ref = grad_refs[2 * late + (0 if goes else 1)]
                    ref[int(k == 3 or k == 2 - late), half] = sum_ref[half, pl.ds(start, depth), :]


def expert_grads(where, split, hidden, pre, rows, gso):
    total, width = rows.shape
    hidden_n = hidden.shape[1]
    steps = hidden_n // FF_STEP
    narrow = pl.BlockSpec((total, width), lambda i, w: (0, 0))
    wide = pl.BlockSpec((total, FF_STEP), lambda i, w: (0, i))
    if split:
        part = (2, 2, width // 4, FF_STEP)
        first = pl.BlockSpec(part, lambda i, w: (0, 0, 0, jnp.minimum(i, steps // 2 - 1)))
        second = pl.BlockSpec(part, lambda i, w: (0, 0, 0, jnp.maximum(i - steps // 2, 0)))
        grad_specs = [first, first, second, second]
        grad_shapes = [jax.ShapeDtypeStruct((2, 2, width // 4, hidden_n // 2), BF)] * 4
    else:
        grad_specs = [pl.BlockSpec((2, width, FF_STEP), lambda i, w: (0, 0, i))]
        grad_shapes = [pltpu.HBM((2, width, hidden_n), BF)]
    return pl.pallas_call(
        lambda *refs: expert_grads_body(split, *refs),
        out_shape=grad_shapes,
        grid_spec=pltpu.PrefetchScalarGridSpec(
            num_scalar_prefetch=1,
            grid=(steps,),
            in_specs=[wide, wide, narrow, narrow],
            out_specs=grad_specs,
            scratch_shapes=[pltpu.VMEM((2, width, FF_STEP), BF)],
        ),
        compiler_params=params(30),
        cost_estimate=SMALL,
        name="expert_grads",
    )(where, far(hidden), far(pre), far(rows), far(gso))


def place_grads(fast, reps, shards_n, pack_ref, which, grad):
    if not fast:
        pack_ref[which] = grad.astype(BF)
        return
    width = grad.shape[0]
    depth = width // shards_n
    rows = depth // reps
    grad = grad.astype(BF)
    for z in range(shards_n):
        for r in range(reps):
            start = z * depth + r * rows
            spot = ((r // 2) * 4 + which) * rows
            pack_ref[r % 2, z, spot : spot + rows, :] = grad[start : start + rows]


def tokens_back_body(back_ref, cot_ref, index_ref, small_ref, gate_ref, *refs):
    full_far, mixed_far, resid_far, grad_resid_ref, grad_mixed_ref, grad_out_ref, sums_ref = refs[:7]
    out_weight_ref, mixed_ref, resid_ref, sem = refs[7:]
    fetch = [
        pltpu.make_async_copy(source, target, sem.at[i])
        for i, (source, target) in enumerate(
            ((resid_far, resid_ref), (full_far.at[3], out_weight_ref), (mixed_far, mixed_ref))
        )
    ]
    for copy in fetch:
        copy.start()
    count, width = resid_ref.shape
    small = small_ref[...].astype(F32)
    index = index_ref[...]
    gates = gate_ref[...]
    grad_n2 = jnp.zeros((count, width), F32)
    rows_h = []
    for e in range(EXPERTS):
        row = iota((ROWS, count), 0) + e * ROWS
        pick = (row == index[0:1, :]) | (row == index[1:2, :])
        pick = jnp.where(pick, 1.0, 0.0).astype(BF)
        back = back_ref[e]
        side = side_parts(back.astype(F32)[CAPACITY : CAPACITY + 1]).astype(BF)
        rows_h.append(jnp.sum(dot_nn(side, pick), axis=0, keepdims=True))
        grad_n2 = grad_n2 + dot_tn(pick, back)
    inner = jnp.concatenate(rows_h, axis=0)
    grad_logits = (inner - gates * jnp.sum(inner, axis=0, keepdims=True)).astype(BF)
    wide_logits = jnp.concatenate(
        [grad_logits.astype(F32), jnp.zeros((8, count), F32)], axis=0
    ).astype(BF)
    grad_n2 = grad_n2 + dot_tn(wide_logits, small_ref[...])
    fetch[0].wait()
    unit2, inv2 = unit_of(resid_ref[...])
    n2 = (unit2 * small[9:10, :]).astype(BF)
    grad_router = dot_nn(wide_logits, n2)[0:EXPERTS]
    grad_gain2 = jnp.sum(grad_n2 * unit2, axis=0, keepdims=True)
    sums_ref[...] = jnp.concatenate(
        [grad_router, jnp.zeros((1, width), F32), grad_gain2, jnp.zeros((6, width), F32)], axis=0
    )
    a = grad_n2 * small[9:10, :]
    grad_resid = cot_ref[0].astype(F32) + inv2 * (
        a
        - jnp.mean(a, axis=-1, keepdims=True)
        - unit2 * jnp.mean(a * unit2, axis=-1, keepdims=True)
    )
    grad_resid_ref[...] = grad_resid
    branch = grad_resid.astype(BF)
    fetch[1].wait()
    grad_mixed_ref[...] = dot_nt(branch, out_weight_ref[...]).astype(BF)
    fetch[2].wait()
    grad_out_ref[...] = dot_tn(mixed_ref[...], branch).astype(BF)


def tokens_back(back, cot, index, small, gates, full, mixed, resid):
    count, width = resid.shape
    held = pl.BlockSpec(memory_space=pltpu.HBM)
    outs = (
        ((count, width), F32),
        ((count, width), BF),
        ((width, width), BF),
        ((16, width), F32),
    )
    return pl.pallas_call(
        tokens_back_body,
        out_shape=tuple(pltpu.HBM(*o) for o in outs),
        in_specs=vmem(5) + [held] * 3,
        out_specs=tuple(vmem(4)),
        scratch_shapes=[
            pltpu.VMEM((width, width), BF),
            pltpu.VMEM((count, width), BF),
            pltpu.VMEM((count, width), F32),
            pltpu.SemaphoreType.DMA((3,)),
        ],
        compiler_params=params(24),
        cost_estimate=SMALL,
        name="tokens_back",
    )(back, far(cot), index, small, gates, far(full), far(mixed), far(resid))


def backward_body(fast, reps, shards_n, where_ref, *refs):
    core = where_ref[0]
    grad_mixed_ref, small_ref, early_ref = refs[:3]
    sources = refs[3:8]
    if fast:
        gp_far, mine_ref, twin_ref, pack_ref = refs[8:12]
        refs = refs[12:]
    else:
        gp_far, pack_ref, sums_ref = refs[8:11]
        refs = refs[11:]
    gp_ref, proj_ref, weights_ref, full_ref, x_ref, grad_out_ref = refs[:-1]
    held, sem = refs[1:-1], refs[-1]
    pairs = HEADS // 2
    copies = {
        i: pltpu.make_async_copy(sources[i], held[i], sem.at[i]) for i in range(5) if i != 1
    }
    for pair in range(pairs):
        heads = pl.ds(2 * pair, 2)
        copies[1, pair] = pltpu.make_async_copy(
            sources[1].at[heads], weights_ref.at[heads], sem.at[5 + pair]
        )
    for which in (0, *((1, pair) for pair in range(pairs)), 3, 2, 4):
        copies[which].start()
    count, width = grad_mixed_ref.shape
    small = small_ref[...].astype(F32)
    masks = head_masks(count)
    factor = HEAD_DIM**-0.5
    copies[0].wait()
    for pair in range(pairs):
        lanes = slice(pair * 2 * HEAD_DIM, (pair + 1) * 2 * HEAD_DIM)
        q, k, v = proj_ref[0, :, lanes], proj_ref[1, :, lanes], proj_ref[2, :, lanes]
        gm = grad_mixed_ref[:, lanes]
        copies[1, pair].wait()
        parts = []
        for half in range(2):
            weights = weights_ref[2 * pair + half]
            probs = weights.astype(F32)
            grad_probs = dot_nt(v, jnp.where(masks[half], gm, BF(0)))
            total = jnp.sum(probs * grad_probs, axis=0, keepdims=True)
            grad_scores = (probs * (grad_probs - total)).astype(BF)
            parts.append(
                (dot_tn(grad_scores, k), dot_nn(grad_scores, q), dot_nn(weights, gm))
            )
        for s in range(3):
            both = jnp.where(masks[0], parts[0][s], parts[1][s])
            gp_ref[s, :, lanes] = (both * factor if s < 2 else both).astype(BF)
    gp_send = pltpu.make_async_copy(gp_ref, gp_far, sem.at[5 + pairs])
    gp_send.start()
    copies[3].wait()
    unit1, _ = unit_of(x_ref[0].astype(F32))
    n1 = (unit1 * small[8:9, :]).astype(BF)
    copies[2].wait()
    product = jnp.zeros((width, width), F32)
    for s in range(3):
        grad = dot_tn(n1, gp_ref[s])
        place_grads(fast, reps, shards_n, pack_ref, s, grad)
        product = product + full_ref[s].astype(F32) * grad
    copies[4].wait()
    place_grads(fast, reps, shards_n, pack_ref, 3, grad_out_ref[...])
    ones = jnp.ones((8, width), BF)
    high = product.astype(BF)
    low = (product - high.astype(F32)).astype(BF)
    grad_gain1 = (dot_nt(ones, high) + dot_nt(ones, low))[0:1] / small[8:9, :]
    sums = jnp.where(iota((16, width), 0) == 8, grad_gain1, early_ref[...])
    sends = [gp_send]
    if fast:
        depth = width // shards_n
        rows = depth // reps
        for z in range(shards_n):
            for half in range(2):
                eight = sums[8 * half : 8 * half + 8, z * depth : (z + 1) * depth]
                eight = jnp.concatenate([eight, jnp.zeros((8, width - depth), F32)], axis=1)
                pack_ref[half, z, 2 * reps * rows :, :] = eight.astype(BF)
        for i in range(2):
            send = pltpu.make_async_copy(pack_ref.at[core ^ i], (mine_ref, twin_ref)[i], sem.at[i])
            send.start()
            sends.append(send)
    else:
        sums_ref[...] = sums
    for send in sends:
        send.wait()


def backward(fast, reps, shards_n, where, grad_mixed, small, early, proj, weights, full, x, grad_out):
    _, count, width = x.shape
    sources = (proj, weights, full, x, grad_out)
    held = pl.BlockSpec(memory_space=pltpu.HBM)
    outs = [pltpu.HBM((3, count, width), BF)]
    scratch = [pltpu.VMEM((3, count, width), BF)]
    if fast:
        part = (shards_n, 2 * reps * (width // shards_n // reps) + 8, width)
        outs += [pltpu.VMEM(part, BF), pltpu.HBM(part, BF)]
        out_specs = [held, *vmem(1), held]
        scratch = [pltpu.VMEM((2, *part), BF)] + scratch
    else:
        outs += [
            jax.ShapeDtypeStruct((4, width, width), BF),
            jax.ShapeDtypeStruct((16, width), F32),
        ]
        out_specs = [held] + vmem(2)
    return pl.pallas_call(
        lambda *refs: backward_body(fast, reps, shards_n, *refs),
        out_shape=tuple(outs),
        in_specs=[pl.BlockSpec(memory_space=pltpu.SMEM)] + vmem(3) + [held] * 5,
        out_specs=tuple(out_specs),
        scratch_shapes=[
            *scratch,
            *(pltpu.VMEM(v.shape, v.dtype) for v in sources),
            pltpu.SemaphoreType.DMA((6 + HEADS // 2,)),
        ],
        compiler_params=params(40),
        cost_estimate=SMALL,
        name="backward",
    )(where, grad_mixed, small, early, *(far(v) for v in sources))


def input_back_body(gp_ref, full_ref, x_ref, grad_resid_ref, small_ref, grad_x_ref):
    small = small_ref[...].astype(F32)
    grad_n1 = dot_nt(gp_ref[0], full_ref[0])
    for s in range(1, 3):
        grad_n1 = grad_n1 + dot_nt(gp_ref[s], full_ref[s])
    unit1, inv1 = unit_of(x_ref[0].astype(F32))
    b = grad_n1 * small[8:9, :]
    grad_x = grad_resid_ref[...] + inv1 * (
        b
        - jnp.mean(b, axis=-1, keepdims=True)
        - unit1 * jnp.mean(b * unit1, axis=-1, keepdims=True)
    )
    grad_x_ref[0] = grad_x.astype(BF)


def input_back(gp, full, x, grad_resid, small):
    _, width = grad_resid.shape
    return pl.pallas_call(
        input_back_body,
        out_shape=pltpu.HBM(x.shape, BF),
        in_specs=vmem(5),
        out_specs=vmem(1)[0],
        compiler_params=params(20),
        cost_estimate=SMALL,
        name="input_back",
    )(far(gp), far(full), far(x), far(grad_resid), small)


def result_body(out_ref, index_ref, resid_ref, result_ref):
    total = resid_ref[...]
    count = total.shape[0]
    index = index_ref[...]
    for e in range(EXPERTS):
        row = iota((ROWS, count), 0) + e * ROWS
        pick = (row == index[0:1, :]) | (row == index[1:2, :])
        total = total + dot_tn(jnp.where(pick, 1.0, 0.0).astype(BF), out_ref[e])
    result_ref[0] = total.astype(BF)


def combine(out, index, resid):
    count, width = resid.shape
    return pl.pallas_call(
        result_body,
        out_shape=jax.ShapeDtypeStruct((1, count, width), BF),
        in_specs=vmem(3),
        out_specs=vmem(1)[0],
        compiler_params=params(8),
        cost_estimate=SMALL,
        name="combine",
    )(far(out), index, far(resid))


def plain(body, outs, *operands):
    return pl.pallas_call(
        body,
        out_shape=tuple(outs) if len(outs) > 1 else outs[0],
        in_specs=vmem(len(operands)),
        out_specs=tuple(vmem(len(outs))) if len(outs) > 1 else vmem(1)[0],
        compiler_params=params(16),
        cost_estimate=SMALL,
        name=body.__name__,
    )(*operands)


def first_sums(stay0_ref, come0_ref, stay1_ref, come1_ref, keep_ref, go0_ref, go1_ref):
    for half, (stay, come, go) in enumerate(
        ((stay0_ref, come0_ref, go0_ref), (stay1_ref, come1_ref, go1_ref))
    ):
        keep_ref[half] = (stay[0].astype(F32) + come[0].astype(F32)).astype(BF)
        go[...] = (stay[1].astype(F32) + come[1].astype(F32)).astype(BF)


def second_sums(keep_ref, come0_ref, come1_ref, sum_ref):
    for half, come in enumerate((come0_ref, come1_ref)):
        sum_ref[half] = (keep_ref[half].astype(F32) + come[...].astype(F32)).astype(BF)


def pair_sum(a_ref, b_ref, sum_ref):
    sum_ref[...] = (a_ref[...].astype(F32) + b_ref[...].astype(F32)).astype(BF)


def line_sum(parts_ref, tall_ref, small_ref):
    total = parts_ref[0].astype(F32)
    for i in range(1, parts_ref.shape[0]):
        total = total + parts_ref[i].astype(F32)
    rows = tall_ref.shape[0] * tall_ref.shape[1]
    for p in range(tall_ref.shape[0]):
        short = tall_ref.shape[1]
        tall_ref[p] = total[p * short : (p + 1) * short].astype(BF)
    small_ref[...] = total[rows:].astype(BF)


def plane_sum(parts_ref, small_ref, shares_ref):
    total = parts_ref[0].astype(F32)
    for i in range(1, parts_ref.shape[0]):
        total = total + parts_ref[i].astype(F32)
    short = total.shape[0]
    for r in range(shares_ref.shape[0]):
        shares_ref[r, 0:short, :] = total.astype(BF)
        shares_ref[r, short:, :] = small_ref[...]


def widen_body(places, aliased, where_ref, *refs):
    n = len(places)
    taken, wide, sem_in, sem_out = refs[-4:]
    outs = refs[-6:-4]
    srcs = refs[: len(refs) - 6 - 2 * aliased]
    _, depth, cols = srcs[0].shape[-3:]
    pieces = [ref.at[half] for ref in srcs for half in range(2)] if len(srcs) < n else srcs
    fetch = [pltpu.make_async_copy(pieces[i], taken.at[i], sem_in.at[i]) for i in range(n)]
    for copy in fetch:
        copy.start()
    sent = []
    for i, (other, k, half) in enumerate(places):
        fetch[i].wait()
        row = pl.multiple_of((where_ref[1] ^ k) * depth, depth)
        for which in range(2):
            wide[i, which] = taken[i, which].astype(F32)
            spot = outs[which].at[
                where_ref[0] ^ other, pl.ds(row, depth), half * cols : (half + 1) * cols
            ]
            copy = pltpu.make_async_copy(wide.at[i, which], spot, sem_out.at[i, which])
            copy.start()
            sent.append(copy)
    for copy in sent:
        copy.wait()


def widen(where, places, sources, shape, so_far=None):
    n = len(places)
    part = sources[0].shape[-3:]
    aliased = so_far is not None
    held = pl.BlockSpec(memory_space=pltpu.HBM)
    operands = [far(source) for source in sources] + (list(so_far) if aliased else [])
    return pl.pallas_call(
        lambda *refs: widen_body(places, aliased, *refs),
        out_shape=(pltpu.HBM(shape, F32), pltpu.HBM(shape, F32)),
        in_specs=[pl.BlockSpec(memory_space=pltpu.SMEM)] + [held] * len(operands),
        out_specs=(held, held),
        scratch_shapes=[
            pltpu.VMEM((n, *part), BF),
            pltpu.VMEM((n, *part), F32),
            pltpu.SemaphoreType.DMA((n,)),
            pltpu.SemaphoreType.DMA((n, 2)),
        ],
        input_output_aliases={len(sources) + 1: 0, len(sources) + 2: 1} if aliased else {},
        compiler_params=params(24),
        cost_estimate=SMALL,
        name="widen",
    )(where, *operands)


def finish_body(rows, parts_ref, qkv_ref, out_ref, router_ref, gains_ref):
    reps = parts_ref.shape[0]
    depth = out_ref.shape[0]
    for r in range(reps):
        for s in range(3):
            qkv_ref[s, r * rows : (r + 1) * rows, :] = parts_ref[
                r, s * rows : (s + 1) * rows, :
            ].astype(F32)
        out_ref[r * rows : (r + 1) * rows, :] = parts_ref[r, 3 * rows : 4 * rows, :].astype(F32)
    smalls = []
    for half in range(2):
        total = jnp.zeros((8, depth), F32)
        for peer in range(reps // 2):
            total = total + parts_ref[2 * peer + half].astype(F32)[4 * rows :, 0:depth]
        smalls.append(total)
    router_ref[...] = smalls[0]
    gains_ref[...] = smalls[1][0:2]


def finish(parts, rows):
    reps, _, width = parts.shape
    depth = rows * reps
    return pl.pallas_call(
        lambda *refs: finish_body(rows, *refs),
        out_shape=(
            jax.ShapeDtypeStruct((3, depth, width), F32),
            jax.ShapeDtypeStruct((depth, width), F32),
            jax.ShapeDtypeStruct((EXPERTS, depth), F32),
            jax.ShapeDtypeStruct((2, depth), F32),
        ),
        in_specs=vmem(1),
        out_specs=tuple(vmem(4)),
        compiler_params=params(4),
        name="finish",
    )(parts)


def shards(reps, shards_n, *args):
    tokens, segments, choices, priority, cotangent = args[:5]
    qkv_weights, out_weight, router_weight, gains, w_in, w_out = args[5:]
    rep, shard = lax.axis_index("rep"), lax.axis_index("shard")
    width, hidden = w_in.shape[1:]
    owned = w_in.shape[0]
    peers = reps // owned
    depth = width // shards_n
    fast = depth % (16 * reps) == 0 and depth == 128 and owned == 2 and peers == 4
    if not fast and owned != 1:
        raise NotImplementedError("mesh")
    column = [
        [(c * owned + e % owned) * shards_n + e // owned for e in range(EXPERTS)]
        for c in range(peers)
    ]

    def to_experts(rows):
        return lax.all_to_all(rows, AXES, 0, 0, axis_index_groups=column, tiled=True)

    where = jnp.stack([rep % owned, rep // owned]).astype(jnp.int32)
    index, cot_sent = route(choices[0].T, priority, cotangent)
    if fast:
        smalls, pieces, lines = gather_weights(
            rep, shard, reps, shards_n, qkv_weights, out_weight, router_weight.T, gains
        )
        place = jnp.stack([rep, shard]).astype(jnp.int32)
        weights_in = (qkv_weights, out_weight, smalls)
    else:
        place, pieces, lines = None, [], []
        weights_in = (
            lax.all_gather(qkv_weights, "shard", axis=1, tiled=True),
            lax.all_gather(out_weight, "shard", axis=0, tiled=True),
            lax.all_gather(router_weight, "shard", axis=0, tiled=True).T,
            lax.all_gather(gains, "shard", axis=1, tiled=True),
        )
    cot_in = to_experts(after(cot_sent, *lines))
    sent, small, gates, *kept = forward(
        fast, place, tokens, segments, index, weights_in, pieces
    )
    n2_in = to_experts(sent)

    def peer(value, k):
        return lax.ppermute(value, "rep", [(i, i ^ k) for i in range(reps)])

    through = cot_hidden(where, cot_in, w_out)
    back, out, *parts_in = experts(where, n2_in, cot_in, through, w_in, w_out)
    grads = expert_grads(where, fast, *parts_in)
    back_in = to_experts(back)
    out_in = to_experts(after(out, back_in))
    if fast:
        axes = ((owned, 2 * owned), (2 * owned, owned))
        halves = [peer(grads[2 * half], axes[half][0]) for half in range(2)]
        back_in = after(back_in, *grads)
    full, weights, proj, mixed, resid = kept
    grad_resid, grad_mixed, grad_out_w, early_sums = tokens_back(
        back_in, cotangent, index, small, gates, full, mixed, resid
    )
    if fast:
        grad_mixed, *halves = lax.optimization_barrier((grad_mixed, *halves))
        part = halves[0].shape[1:]
        small_part = jax.ShapeDtypeStruct(part, BF)
        keep, *leaves = plain(
            first_sums,
            [jax.ShapeDtypeStruct((2, *part), BF), small_part, small_part],
            grads[1],
            halves[0],
            grads[3],
            halves[1],
        )
        arrived = [peer(leaves[half], axes[half][1]) for half in range(2)]
        grad_mixed = after(grad_mixed, keep)
    grad_proj, *packs = backward(
        fast,
        reps,
        shards_n,
        where,
        grad_mixed,
        small,
        early_sums,
        proj,
        weights,
        full,
        tokens,
        grad_out_w,
    )
    grad_tokens = input_back(grad_proj, full, tokens, grad_resid, small)
    result = combine(out_in, index, kept[4])
    if fast:
        mine, twin, *arrived = lax.optimization_barrier((*packs, *arrived))
        total = plain(second_sums, [jax.ShapeDtypeStruct(keep.shape, BF)], keep, *arrived)
        twin = after(twin, total)
        chip = plain(pair_sum, [jax.ShapeDtypeStruct(mine.shape, BF)], mine, peer(twin, 1))
        line = lax.all_to_all(after(chip, out_in), "shard", 0, 0, tiled=True)
        short = 2 * depth // peers
        line, own_small = plain(
            line_sum,
            [
                jax.ShapeDtypeStruct((peers, short, width), BF),
                jax.ShapeDtypeStruct((8, width), BF),
            ],
            line,
        )
        early = [total] + [peer(total, k * owned) for k in (1, 2)]
        grad_tokens, *early = lax.optimization_barrier((grad_tokens, *early))
        late = [
            peer(early[axes[half][0] // owned][half], 3 * owned - axes[half][0]) for half in range(2)
        ]
        early += [peer(value, 1) for value in early]
        shape = (owned, width, hidden)
        places = [(other, k, half) for other in range(2) for k in range(3) for half in range(2)]
        so_far = widen(where, places, early, shape)
        plane_groups = [[p * owned + c for p in range(peers)] for c in range(owned)]
        plane = lax.all_to_all(line, "rep", 0, 0, axis_index_groups=plane_groups, tiled=True)
        plane, *so_far = lax.optimization_barrier((plane, *so_far))
        share = plain(
            plane_sum, [jax.ShapeDtypeStruct((reps, short + 8, width), BF)], plane, own_small
        )
        share, *late = lax.optimization_barrier((share, *late))
        late += [peer(value, 1) for value in late]
        parts = lax.all_to_all(share, "rep", 0, 0, tiled=True)
        places = [(other, 3, half) for other in range(2) for half in range(2)]
        grad_w_in, grad_w_out = widen(where, places, late, shape, so_far)
        parts = after(parts, grad_w_in, result)
        grad_qkv, grad_out, grad_router, grad_gains = finish(parts, depth // reps)
        grad_router = grad_router.T
    else:
        share = lax.psum_scatter(grads[0], "rep", scatter_dimension=1, tiled=True)
        every = lax.all_gather(share, "rep", axis=1, tiled=True).astype(F32)
        grad_w_in, grad_w_out = every[0:1], every[1:2]
        pack, sums = packs
        owned_rows = lax.psum_scatter(pack, "shard", scatter_dimension=1, tiled=True)
        owned_rows = lax.psum(owned_rows, "rep").astype(F32)
        grad_qkv, grad_out = owned_rows[0:3], owned_rows[3]
        sums = lax.psum(sums, AXES)
        mine = lax.dynamic_slice_in_dim(sums, shard * depth, depth, axis=1)
        grad_router, grad_gains = mine[0:EXPERTS].T, mine[EXPERTS : EXPERTS + 2]
    return (
        result,
        grad_tokens,
        grad_qkv,
        grad_out,
        grad_router,
        grad_gains,
        grad_w_in,
        grad_w_out,
    )


def solution(mesh):
    reps, shards_n = mesh.shape["rep"], mesh.shape["shard"]
    rows = P(("rep", "shard"), None, None)
    flat = P(("rep", "shard"), None)
    first = P("shard", None)
    stack = P("shard", None, None)
    second = P(None, "shard", None)
    return jax.shard_map(
        lambda *args: shards(reps, shards_n, *args),
        mesh=mesh,
        in_specs=(
            rows, flat, rows, flat, rows, second, first, first, P(None, "shard"), stack, stack,
        ),
        out_specs=(rows, rows, second, first, first, P(None, "shard"), stack, stack),
        check_vma=False,
    )
```

```python
import jax
import jax.numpy as jnp
from jax import lax
from jax.experimental import pallas as pl
from jax.experimental.pallas import tpu as pltpu
from jax.sharding import PartitionSpec as P

HEADS = 8
HEAD_DIM = 64
EXPERTS = 8
CAPACITY = 135
ROWS = 136
EPS = 1e-06
F32 = jnp.float32
BF = jnp.bfloat16
AXES = ("rep", "shard")
FF_STEP = 512
KEPT = 5
SMALL = pl.CostEstimate(flops=1000, bytes_accessed=1000, transcendentals=0)
GELU_A = 0.7978845608028654
GELU_B = 0.044715


def dot_nn(a, b):
    return lax.dot_general(a, b, (((1,), (0,)), ((), ())), preferred_element_type=F32)


def dot_nt(a, b):
    return lax.dot_general(a, b, (((1,), (1,)), ((), ())), preferred_element_type=F32)


def dot_tn(a, b):
    return lax.dot_general(a, b, (((0,), (0,)), ((), ())), preferred_element_type=F32)


def after(value, *others):
    return lax.optimization_barrier((value, *others))[0]


def iota(shape, dim):
    return lax.broadcasted_iota(jnp.int32, shape, dim)


def unit_of(values):
    mean = jnp.mean(values, axis=-1, keepdims=True)
    centered = values - mean
    inv = lax.rsqrt(jnp.mean(centered * centered, axis=-1, keepdims=True) + EPS)
    return centered * inv, inv


def split3(values):
    high = values.astype(BF)
    rest = values - high.astype(F32)
    mid = rest.astype(BF)
    low = (rest - mid.astype(F32)).astype(BF)
    return high, mid, low


def piece_rows(values):
    high, mid, low = split3(values)
    shape = (8, values.shape[1])
    row = iota(shape, 0)
    parts = [jnp.broadcast_to(part.astype(F32), shape) for part in (high, mid, low)]
    return jnp.where(
        row == 0, parts[0], jnp.where(row == 1, parts[1], jnp.where(row == 2, parts[2], 0.0))
    )


def side_row(pieces, width):
    wide = jnp.concatenate([pieces, jnp.zeros((8, width - ROWS), F32)], axis=1)
    row = iota((8, width), 0)
    moved = jnp.where(
        row == 0,
        wide,
        jnp.where(row == 1, pltpu.roll(wide, ROWS, 1), pltpu.roll(wide, 2 * ROWS, 1)),
    )
    return jnp.sum(jnp.where(row < 3, moved, 0.0), axis=0, keepdims=True)


def side_parts(side):
    width = side.shape[1]
    wide = jnp.broadcast_to(side, (8, width))
    row = iota((8, width), 0)
    back = jnp.where(
        row == 0,
        wide,
        jnp.where(row == 1, pltpu.roll(wide, width - ROWS, 1), pltpu.roll(wide, width - 2 * ROWS, 1)),
    )
    return jnp.where(row < 3, back, 0.0)[:, 0:ROWS]


def far(value):
    return pltpu.with_memory_space_constraint(value, pltpu.HBM)


def near(value):
    return pltpu.with_memory_space_constraint(value, pltpu.VMEM)


def vmem(n):
    return [pl.BlockSpec(memory_space=pltpu.VMEM)] * n


def params(mib):
    return pltpu.CompilerParams(vmem_limit_bytes=mib << 20)


def route_body(choice_ref, prio_ref, cot_ref, index_ref, sent_ref):
    count = cot_ref.shape[-2]
    choice = choice_ref[...]
    experts = iota((EXPERTS, count), 0)
    first = jnp.where(choice[0:1, :] == experts, 1.0, 0.0)
    second = jnp.where(choice[1:2, :] == experts, 1.0, 0.0)
    order = jnp.where(iota((count, count), 0) == prio_ref[...], 1.0, 0.0).astype(BF)
    earlier = jnp.where(iota((count, count), 0) < iota((count, count), 1), 1.0, 0.0).astype(BF)
    both = jnp.concatenate([first, second], axis=0).astype(BF)
    before = dot_nn(dot_nt(both, order).astype(BF), earlier)
    held = jnp.sum(first, axis=1, keepdims=True)
    before = jnp.concatenate([before[0:EXPERTS], before[EXPERTS:] + held], axis=0)
    before = dot_nn(jnp.minimum(before, 255.0).astype(BF), order)
    slot0 = jnp.sum(first * before[0:EXPERTS], axis=0, keepdims=True)
    slot1 = jnp.sum(second * before[EXPERTS:], axis=0, keepdims=True)
    slot = jnp.concatenate([slot0, slot1], axis=0).astype(jnp.int32)
    index = jnp.where(slot < CAPACITY, choice * ROWS + slot, -1)
    index_ref[...] = index
    cot = cot_ref[0]
    for e in range(EXPERTS):
        row = iota((ROWS, count), 0) + e * ROWS
        pick = (row == index[0:1, :]) | (row == index[1:2, :])
        sent_ref[e] = dot_nn(jnp.where(pick, 1.0, 0.0).astype(BF), cot).astype(BF)


def route(choice_t, prio, cot):
    _, count, width = cot.shape
    return pl.pallas_call(
        route_body,
        out_shape=(
            jax.ShapeDtypeStruct((2, count), jnp.int32),
            pltpu.HBM((EXPERTS, ROWS, width), BF),
        ),
        in_specs=vmem(3),
        out_specs=tuple(vmem(2)),
        compiler_params=params(12),
        cost_estimate=SMALL,
        name="route",
    )(far(choice_t), far(prio), far(cot))


def pack_body(where_ref, qkv_ref, out_ref, router_ref, gains_ref, pack_ref):
    rows = pack_ref.shape[1]
    start = pl.multiple_of(where_ref[0] * rows, rows)
    for s in range(3):
        pack_ref[s] = qkv_ref[s, pl.ds(start, rows), :]
    pack_ref[3] = out_ref[pl.ds(start, rows), :]
    depth = router_ref.shape[1]
    small = jnp.concatenate(
        [router_ref[...].astype(F32), gains_ref[...].astype(F32), jnp.zeros((6, depth), F32)],
        axis=0,
    )
    pack_ref[4, :, 0:depth] = small.astype(BF)
    pack_ref[4, :, depth:] = jnp.zeros((rows, pack_ref.shape[2] - depth), BF)


def pack_weights(rep, qkv, out, router, gains, rows):
    width = out.shape[1]
    return pl.pallas_call(
        pack_body,
        out_shape=jax.ShapeDtypeStruct((5, rows, width), BF),
        in_specs=[pl.BlockSpec(memory_space=pltpu.SMEM)] + vmem(4),
        out_specs=vmem(1)[0],
        compiler_params=params(4),
        name="pack_weights",
    )(rep.reshape(1), far(qkv), far(out), far(router), far(gains))


def gather_weights(rep, shard, reps, shards_n, qkv, out, router, gains):
    rows = qkv.shape[1] // reps
    pack = pack_weights(rep, qkv, out, router, gains, rows)
    lines = [
        lax.ppermute(pack, "shard", [(i, i ^ dz) for i in range(shards_n)])
        for dz in range(1, shards_n)
    ]
    block = jnp.stack([piece[0:4] for piece in lines])
    smalls = jnp.stack([piece[4] for piece in [pack] + lines])
    spread = [block] + [
        lax.ppermute(block, "rep", [(i, i ^ k) for i in range(reps)]) for k in range(2, reps, 2)
    ]
    twin = [lax.ppermute(piece, "rep", [(i, i ^ 1) for i in range(reps)]) for piece in spread]
    pieces = []
    for own, other in zip(spread, twin, strict=True):
        pieces += [own, other]
    return smalls, pieces, lines


def fill_weights(rep, shard, qkv_ref, out_ref, smalls_ref, piece_refs, full_ref, small_ref):
    depth = out_ref.shape[0]
    own = pl.multiple_of(shard * depth, depth)
    for s in range(3):
        full_ref[s, pl.ds(own, depth), :] = qkv_ref[s]
    full_ref[3, pl.ds(own, depth), :] = out_ref[...]
    small_ref[:, pl.ds(own, depth)] = smalls_ref[0, :, 0:depth]
    for far in range(1, smalls_ref.shape[0]):
        base = pl.multiple_of((shard ^ far) * depth, depth)
        small_ref[:, pl.ds(base, depth)] = smalls_ref[far, :, 0:depth]
        for k, piece in enumerate(piece_refs):
            rows = piece.shape[2]
            start = pl.multiple_of(base + (rep ^ k) * rows, rows)
            for s in range(4):
                full_ref[s, pl.ds(start, rows), :] = piece[far - 1, s]


def head_masks(count):
    lane = iota((count, 2 * HEAD_DIM), 1)
    return [lane < HEAD_DIM, lane >= HEAD_DIM]


def kept_shapes(count, width):
    return (
        ((4, width, width), BF),
        ((HEADS, count, count), BF),
        ((3, count, width), BF),
        ((count, width), BF),
        ((count, width), F32),
    )


def kept_copies(sources, targets, sem):
    copies = {
        i: pltpu.make_async_copy(sources[i], targets[i], sem.at[i]) for i in range(KEPT) if i != 1
    }
    for pair in range(HEADS // 2):
        heads = pl.ds(2 * pair, 2)
        copies[1, pair] = pltpu.make_async_copy(
            sources[1].at[heads], targets[1].at[heads], sem.at[KEPT + pair]
        )
    return copies


def forward_body(fast, n_pieces, *refs):
    if fast:
        where_ref, x_ref, seg_ref, index_ref, qkv_ref, out_ref, smalls_ref = refs[:7]
        piece_refs = refs[7 : 7 + n_pieces]
        refs = refs[7 + n_pieces :]
    else:
        x_ref, seg_ref, index_ref, qkv_ref, out_ref, router_ref, gains_ref = refs[:7]
        refs = refs[7:]
    sent_ref, small_ref, gate_ref, *kept = refs[: 3 + KEPT]
    full_ref, weights_ref, proj_ref, mixed_ref, resid_ref = held = refs[3 + KEPT : -1]
    copies = kept_copies(held, kept, refs[-1])
    if fast:
        fill_weights(
            where_ref[0], where_ref[1], qkv_ref, out_ref, smalls_ref, piece_refs, full_ref, small_ref
        )
    else:
        full_ref[0:3] = qkv_ref[...]
        full_ref[3] = out_ref[...]
        small_ref[...] = jnp.concatenate(
            [
                router_ref[...].astype(F32),
                gains_ref[...].astype(F32),
                jnp.zeros((6, out_ref.shape[1]), F32),
            ],
            axis=0,
        ).astype(BF)
    copies[0].start()
    x = x_ref[0].astype(F32)
    count, width = x.shape
    small = small_ref[...].astype(F32)
    unit1, _ = unit_of(x)
    n1 = (unit1 * small[8:9, :]).astype(BF)
    for s in range(3):
        proj_ref[s] = dot_nn(n1, full_ref[s]).astype(BF)
    copies[2].start()
    document = jnp.where(iota((8, count), 0) == seg_ref[...], 1.0, 0.0).astype(BF)
    bias = jnp.where(dot_tn(document, document) > 0.5, 0.0, -1e30)
    masks = head_masks(count)
    for pair in range(HEADS // 2):
        lanes = slice(pair * 2 * HEAD_DIM, (pair + 1) * 2 * HEAD_DIM)
        q, k, v = proj_ref[0, :, lanes], proj_ref[1, :, lanes], proj_ref[2, :, lanes]
        q = q * BF(HEAD_DIM**-0.5)
        halves = []
        for half in range(2):
            scores = dot_nt(k, jnp.where(masks[half], q, BF(0))) + bias
            top = jnp.max(scores, axis=0, keepdims=True)
            terms = jnp.exp(scores - top)
            total = jnp.sum(terms, axis=0, keepdims=True)
            weights = (terms * (1.0 / total)).astype(BF)
            weights_ref[2 * pair + half] = weights
            halves.append(dot_tn(weights, v))
        copies[1, pair].start()
        mixed_ref[:, lanes] = jnp.where(masks[0], halves[0], halves[1]).astype(BF)
    copies[3].start()
    resid = x + dot_nn(mixed_ref[...], full_ref[3])
    resid_ref[...] = resid
    copies[4].start()
    unit2, _ = unit_of(resid)
    n2 = (unit2 * small[9:10, :]).astype(BF)
    logits = dot_nt(small_ref[...], n2)[0:EXPERTS]
    terms = jnp.exp(logits - jnp.max(logits, axis=0, keepdims=True))
    gates = terms / jnp.sum(terms, axis=0, keepdims=True)
    gate_ref[...] = gates
    index = index_ref[...]
    for e in range(EXPERTS):
        row = iota((ROWS, count), 0) + e * ROWS
        pick = (row == index[0:1, :]) | (row == index[1:2, :])
        pick = jnp.where(pick, 1.0, 0.0).astype(BF)
        rows = dot_nn(pick, n2)
        side = side_row(dot_nt(piece_rows(gates[e : e + 1, :]).astype(BF), pick), width)
        last = iota((ROWS, 1), 0) == CAPACITY
        sent_ref[e] = jnp.where(last, side, rows).astype(BF)
    for copy in copies.values():
        copy.wait()


def forward(fast, where, x, seg, index, weights_in, pieces):
    _, count, width = x.shape
    body = lambda *refs: forward_body(fast, len(pieces), *refs)
    operands = [far(x), far(seg), index, *(far(w) for w in weights_in[:2]), *weights_in[2:], *pieces]
    specs = vmem(len(operands))
    if fast:
        operands = [where] + operands
        specs = [pl.BlockSpec(memory_space=pltpu.SMEM)] + specs
    shown = (
        pltpu.HBM((EXPERTS, ROWS, width), BF),
        jax.ShapeDtypeStruct((16, width), BF),
        jax.ShapeDtypeStruct((EXPERTS, count), F32),
    )
    kept = kept_shapes(count, width)
    return pl.pallas_call(
        body,
        out_shape=(*shown, *(pltpu.HBM(*k) for k in kept)),
        in_specs=specs,
        out_specs=(*vmem(3), *([pl.BlockSpec(memory_space=pltpu.HBM)] * KEPT)),
        scratch_shapes=[
            *(pltpu.VMEM(*k) for k in kept),
            pltpu.SemaphoreType.DMA((KEPT + HEADS // 2,)),
        ],
        compiler_params=params(40),
        cost_estimate=SMALL,
        name="forward",
    )(*operands)


def cot_hidden_body(where_ref, cot_ref, w_out_ref, through_ref):
    rows = jnp.concatenate([cot_ref[g].astype(F32) for g in range(2)], axis=0).astype(BF)
    for start in range(0, w_out_ref.shape[2], FF_STEP):
        cols = slice(start, start + FF_STEP)
        through_ref[:, cols] = dot_nn(rows, w_out_ref[0, :, cols])


def cot_hidden(where, cot, w_out):
    groups, _, width = cot.shape
    hidden_n = w_out.shape[2]
    return pl.pallas_call(
        cot_hidden_body,
        out_shape=pltpu.HBM((groups * ROWS, hidden_n), F32),
        grid_spec=pltpu.PrefetchScalarGridSpec(
            num_scalar_prefetch=1,
            grid=(groups // 2,),
            in_specs=[
                pl.BlockSpec((2, ROWS, width), lambda i, w: (i, 0, 0)),
                pl.BlockSpec((1, width, hidden_n), lambda i, w: (w[0], 0, 0)),
            ],
            out_specs=pl.BlockSpec((2 * ROWS, hidden_n), lambda i, w: (i, 0)),
        ),
        compiler_params=params(24),
        cost_estimate=SMALL,
        name="cot_hidden",
    )(where, cot, far(w_out))


def experts_body(where_ref, *refs):
    n2_ref, cot_ref, through_ref, w_in_ref, w_out_ref = refs[:5]
    back_ref, out_ref, hidden_ref, pre_ref, gso_ref = refs[5:]
    eye = jnp.where(iota((ROWS, ROWS), 0) == iota((ROWS, ROWS), 1), 1.0, 0.0).astype(BF)
    lane = iota((ROWS, 8), 1)
    gates = []
    for g in range(2):
        last = (g + 1) * ROWS - 1
        start = last // 16 * 16
        eight = n2_ref[start : start + 16, :].astype(F32)
        parts = side_parts(eight[last - start : last - start + 1]).astype(BF)
        gates.append(jnp.sum(dot_nt(eye, parts), axis=1, keepdims=True))
    gate_col = jnp.concatenate(gates, axis=0)
    rows = n2_ref[...]
    gso_ref[...] = (gate_col * cot_ref[...].astype(F32)).astype(BF)
    for start in range(0, w_in_ref.shape[2], FF_STEP):
        cols = slice(start, start + FF_STEP)
        u = dot_nn(rows, w_in_ref[0, :, cols])
        square = u * u
        t = jnp.tanh(GELU_A * (u + GELU_B * (u * square)))
        half = 0.5 * (1.0 + t)
        hidden = u * half
        slope = half + hidden * (1.0 - t) * (GELU_A * (1.0 + 3.0 * GELU_B * square))
        hidden_ref[:, cols] = hidden.astype(BF)
        pre_ref[:, cols] = (through_ref[:, cols] * (gate_col * slope)).astype(BF)
    grad_in = dot_nt(pre_ref[...], w_in_ref[0])
    result = dot_nt(hidden_ref[...], w_out_ref[0])
    out = (gate_col * result).astype(BF)
    out_ref[...] = out
    inner_all = jnp.sum(out.astype(F32) * cot_ref[...].astype(F32), axis=1, keepdims=True)
    row = iota((2 * ROWS, 1), 0)
    back = grad_in
    for g in range(2):
        inner = inner_all[g * ROWS : (g + 1) * ROWS]
        high, mid, low = (piece.astype(F32) for piece in split3(inner))
        pieces = jnp.where(lane == 0, high, jnp.where(lane == 1, mid, jnp.where(lane == 2, low, 0.0)))
        side = side_row(dot_tn(pieces.astype(BF), eye), out.shape[1])
        back = jnp.where(row == (g + 1) * ROWS - 1, side, back)
    back_ref[...] = back.astype(BF)


def experts(where, n2, cot, through, w_in, w_out):
    groups, _, width = n2.shape
    hidden_n = w_in.shape[2]
    total = groups * ROWS
    weight = pl.BlockSpec((1, width, hidden_n), lambda i, w: (w[0], 0, 0))
    narrow = pl.BlockSpec((2 * ROWS, width), lambda i, w: (i, 0))
    wide = pl.BlockSpec((2 * ROWS, hidden_n), lambda i, w: (i, 0))
    n2, cot = n2.reshape(total, width), cot.reshape(total, width)
    back, out, hidden, pre, gso = pl.pallas_call(
        experts_body,
        out_shape=[
            pltpu.HBM((total, width), BF),
            pltpu.HBM((total, width), BF),
            pltpu.HBM((total, hidden_n), BF),
            pltpu.HBM((total, hidden_n), BF),
            pltpu.HBM((total, width), BF),
        ],
        grid_spec=pltpu.PrefetchScalarGridSpec(
            num_scalar_prefetch=1,
            grid=(groups // 2,),
            in_specs=[narrow, narrow, wide, weight, weight],
            out_specs=[narrow, narrow, wide, wide, narrow],
        ),
        compiler_params=params(44),
        cost_estimate=SMALL,
        name="experts",
    )(where, n2, cot, through, far(w_in), far(w_out))
    shape = (groups, ROWS, width)
    return back.reshape(shape), out.reshape(shape), hidden, pre, n2, gso


def expert_grads_body(split, where_ref, hidden_ref, pre_ref, rows_ref, gso_ref, *refs):
    grad_refs, sum_ref = refs[:-1], refs[-1]
    step, steps = pl.program_id(0), pl.num_programs(0)
    for half, (left, right) in enumerate(((rows_ref, pre_ref), (gso_ref, hidden_ref))):
        grad = dot_tn(left[...], right[...]).astype(BF)
        if not split:
            grad_refs[0][half] = grad
            continue
        sum_ref[half] = grad
    if not split:
        return
    depth = sum_ref.shape[1] // 4
    for late in range(2):

        @pl.when((step < steps // 2) if late == 0 else (step >= steps // 2))
        def _(late=late):
            for half in range(2):
                for k in range(4):
                    start = pl.multiple_of((where_ref[1] ^ k) * depth, depth)
                    goes = k == 3 or k == 1 + late
                    ref = grad_refs[2 * late + (0 if goes else 1)]
                    ref[int(k == 3 or k == 2 - late), half] = sum_ref[half, pl.ds(start, depth), :]


def expert_grads(where, split, hidden, pre, rows, gso):
    total, width = rows.shape
    hidden_n = hidden.shape[1]
    steps = hidden_n // FF_STEP
    narrow = pl.BlockSpec((total, width), lambda i, w: (0, 0))
    wide = pl.BlockSpec((total, FF_STEP), lambda i, w: (0, i))
    if split:
        part = (2, 2, width // 4, FF_STEP)
        first = pl.BlockSpec(part, lambda i, w: (0, 0, 0, jnp.minimum(i, steps // 2 - 1)))
        second = pl.BlockSpec(part, lambda i, w: (0, 0, 0, jnp.maximum(i - steps // 2, 0)))
        grad_specs = [first, first, second, second]
        grad_shapes = [jax.ShapeDtypeStruct((2, 2, width // 4, hidden_n // 2), BF)] * 4
    else:
        grad_specs = [pl.BlockSpec((2, width, FF_STEP), lambda i, w: (0, 0, i))]
        grad_shapes = [pltpu.HBM((2, width, hidden_n), BF)]
    return pl.pallas_call(
        lambda *refs: expert_grads_body(split, *refs),
        out_shape=grad_shapes,
        grid_spec=pltpu.PrefetchScalarGridSpec(
            num_scalar_prefetch=1,
            grid=(steps,),
            in_specs=[wide, wide, narrow, narrow],
            out_specs=grad_specs,
            scratch_shapes=[pltpu.VMEM((2, width, FF_STEP), BF)],
        ),
        compiler_params=params(30),
        cost_estimate=SMALL,
        name="expert_grads",
    )(where, far(hidden), far(pre), far(rows), far(gso))


def place_grads(fast, reps, shards_n, pack_ref, which, grad):
    if not fast:
        pack_ref[which] = grad.astype(BF)
        return
    width = grad.shape[0]
    depth = width // shards_n
    rows = depth // reps
    grad = grad.astype(BF)
    for z in range(shards_n):
        for r in range(reps):
            start = z * depth + r * rows
            spot = ((r // 2) * 4 + which) * rows
            pack_ref[r % 2, z, spot : spot + rows, :] = grad[start : start + rows]


def tokens_back_body(back_ref, cot_ref, index_ref, small_ref, gate_ref, *refs):
    full_far, mixed_far, resid_far, grad_resid_ref, grad_mixed_ref, grad_out_ref, sums_ref = refs[:7]
    out_weight_ref, mixed_ref, resid_ref, sem = refs[7:]
    fetch = [
        pltpu.make_async_copy(source, target, sem.at[i])
        for i, (source, target) in enumerate(
            ((resid_far, resid_ref), (full_far.at[3], out_weight_ref), (mixed_far, mixed_ref))
        )
    ]
    for copy in fetch:
        copy.start()
    count, width = resid_ref.shape
    small = small_ref[...].astype(F32)
    index = index_ref[...]
    gates = gate_ref[...]
    grad_n2 = jnp.zeros((count, width), F32)
    rows_h = []
    for e in range(EXPERTS):
        row = iota((ROWS, count), 0) + e * ROWS
        pick = (row == index[0:1, :]) | (row == index[1:2, :])
        pick = jnp.where(pick, 1.0, 0.0).astype(BF)
        back = back_ref[e]
        side = side_parts(back.astype(F32)[CAPACITY : CAPACITY + 1]).astype(BF)
        rows_h.append(jnp.sum(dot_nn(side, pick), axis=0, keepdims=True))
        grad_n2 = grad_n2 + dot_tn(pick, back)
    inner = jnp.concatenate(rows_h, axis=0)
    grad_logits = (inner - gates * jnp.sum(inner, axis=0, keepdims=True)).astype(BF)
    wide_logits = jnp.concatenate(
        [grad_logits.astype(F32), jnp.zeros((8, count), F32)], axis=0
    ).astype(BF)
    grad_n2 = grad_n2 + dot_tn(wide_logits, small_ref[...])
    fetch[0].wait()
    unit2, inv2 = unit_of(resid_ref[...])
    n2 = (unit2 * small[9:10, :]).astype(BF)
    grad_router = dot_nn(wide_logits, n2)[0:EXPERTS]
    grad_gain2 = jnp.sum(grad_n2 * unit2, axis=0, keepdims=True)
    sums_ref[...] = jnp.concatenate(
        [grad_router, jnp.zeros((1, width), F32), grad_gain2, jnp.zeros((6, width), F32)], axis=0
    )
    a = grad_n2 * small[9:10, :]
    grad_resid = cot_ref[0].astype(F32) + inv2 * (
        a
        - jnp.mean(a, axis=-1, keepdims=True)
        - unit2 * jnp.mean(a * unit2, axis=-1, keepdims=True)
    )
    grad_resid_ref[...] = grad_resid
    branch = grad_resid.astype(BF)
    fetch[1].wait()
    grad_mixed_ref[...] = dot_nt(branch, out_weight_ref[...]).astype(BF)
    fetch[2].wait()
    grad_out_ref[...] = dot_tn(mixed_ref[...], branch).astype(BF)


def tokens_back(back, cot, index, small, gates, full, mixed, resid):
    count, width = resid.shape
    held = pl.BlockSpec(memory_space=pltpu.HBM)
    outs = (
        ((count, width), F32),
        ((count, width), BF),
        ((width, width), BF),
        ((16, width), F32),
    )
    return pl.pallas_call(
        tokens_back_body,
        out_shape=tuple(pltpu.HBM(*o) for o in outs),
        in_specs=vmem(5) + [held] * 3,
        out_specs=tuple(vmem(4)),
        scratch_shapes=[
            pltpu.VMEM((width, width), BF),
            pltpu.VMEM((count, width), BF),
            pltpu.VMEM((count, width), F32),
            pltpu.SemaphoreType.DMA((3,)),
        ],
        compiler_params=params(24),
        cost_estimate=SMALL,
        name="tokens_back",
    )(back, far(cot), index, small, gates, far(full), far(mixed), far(resid))


def backward_body(fast, reps, shards_n, where_ref, *refs):
    core = where_ref[0]
    grad_mixed_ref, small_ref, early_ref = refs[:3]
    sources = refs[3:8]
    if fast:
        gp_far, mine_ref, twin_ref, pack_ref = refs[8:12]
        refs = refs[12:]
    else:
        gp_far, pack_ref, sums_ref = refs[8:11]
        refs = refs[11:]
    gp_ref, proj_ref, weights_ref, full_ref, x_ref, grad_out_ref = refs[:-1]
    held, sem = refs[1:-1], refs[-1]
    pairs = HEADS // 2
    copies = {
        i: pltpu.make_async_copy(sources[i], held[i], sem.at[i]) for i in range(5) if i != 1
    }
    for pair in range(pairs):
        heads = pl.ds(2 * pair, 2)
        copies[1, pair] = pltpu.make_async_copy(
            sources[1].at[heads], weights_ref.at[heads], sem.at[5 + pair]
        )
    for which in (0, *((1, pair) for pair in range(pairs)), 3, 2, 4):
        copies[which].start()
    count, width = grad_mixed_ref.shape
    small = small_ref[...].astype(F32)
    masks = head_masks(count)
    factor = HEAD_DIM**-0.5
    copies[0].wait()
    for pair in range(pairs):
        lanes = slice(pair * 2 * HEAD_DIM, (pair + 1) * 2 * HEAD_DIM)
        q, k, v = proj_ref[0, :, lanes], proj_ref[1, :, lanes], proj_ref[2, :, lanes]
        gm = grad_mixed_ref[:, lanes]
        copies[1, pair].wait()
        parts = []
        for half in range(2):
            weights = weights_ref[2 * pair + half]
            probs = weights.astype(F32)
            grad_probs = dot_nt(v, jnp.where(masks[half], gm, BF(0)))
            total = jnp.sum(probs * grad_probs, axis=0, keepdims=True)
            grad_scores = (probs * (grad_probs - total)).astype(BF)
            parts.append(
                (dot_tn(grad_scores, k), dot_nn(grad_scores, q), dot_nn(weights, gm))
            )
        for s in range(3):
            both = jnp.where(masks[0], parts[0][s], parts[1][s])
            gp_ref[s, :, lanes] = (both * factor if s < 2 else both).astype(BF)
    gp_send = pltpu.make_async_copy(gp_ref, gp_far, sem.at[5 + pairs])
    gp_send.start()
    copies[3].wait()
    unit1, _ = unit_of(x_ref[0].astype(F32))
    n1 = (unit1 * small[8:9, :]).astype(BF)
    copies[2].wait()
    product = jnp.zeros((width, width), F32)
    for s in range(3):
        grad = dot_tn(n1, gp_ref[s])
        place_grads(fast, reps, shards_n, pack_ref, s, grad)
        product = product + full_ref[s].astype(F32) * grad
    copies[4].wait()
    place_grads(fast, reps, shards_n, pack_ref, 3, grad_out_ref[...])
    ones = jnp.ones((8, width), BF)
    high = product.astype(BF)
    low = (product - high.astype(F32)).astype(BF)
    grad_gain1 = (dot_nt(ones, high) + dot_nt(ones, low))[0:1] / small[8:9, :]
    sums = jnp.where(iota((16, width), 0) == 8, grad_gain1, early_ref[...])
    sends = [gp_send]
    if fast:
        depth = width // shards_n
        rows = depth // reps
        for z in range(shards_n):
            for half in range(2):
                eight = sums[8 * half : 8 * half + 8, z * depth : (z + 1) * depth]
                eight = jnp.concatenate([eight, jnp.zeros((8, width - depth), F32)], axis=1)
                pack_ref[half, z, 2 * reps * rows :, :] = eight.astype(BF)
        for i in range(2):
            send = pltpu.make_async_copy(pack_ref.at[core ^ i], (mine_ref, twin_ref)[i], sem.at[i])
            send.start()
            sends.append(send)
    else:
        sums_ref[...] = sums
    for send in sends:
        send.wait()


def backward(fast, reps, shards_n, where, grad_mixed, small, early, proj, weights, full, x, grad_out):
    _, count, width = x.shape
    sources = (proj, weights, full, x, grad_out)
    held = pl.BlockSpec(memory_space=pltpu.HBM)
    outs = [pltpu.HBM((3, count, width), BF)]
    scratch = [pltpu.VMEM((3, count, width), BF)]
    if fast:
        part = (shards_n, 2 * reps * (width // shards_n // reps) + 8, width)
        outs += [pltpu.VMEM(part, BF), pltpu.HBM(part, BF)]
        out_specs = [held, *vmem(1), held]
        scratch = [pltpu.VMEM((2, *part), BF)] + scratch
    else:
        outs += [
            jax.ShapeDtypeStruct((4, width, width), BF),
            jax.ShapeDtypeStruct((16, width), F32),
        ]
        out_specs = [held] + vmem(2)
    return pl.pallas_call(
        lambda *refs: backward_body(fast, reps, shards_n, *refs),
        out_shape=tuple(outs),
        in_specs=[pl.BlockSpec(memory_space=pltpu.SMEM)] + vmem(3) + [held] * 5,
        out_specs=tuple(out_specs),
        scratch_shapes=[
            *scratch,
            *(pltpu.VMEM(v.shape, v.dtype) for v in sources),
            pltpu.SemaphoreType.DMA((6 + HEADS // 2,)),
        ],
        compiler_params=params(40),
        cost_estimate=SMALL,
        name="backward",
    )(where, grad_mixed, small, early, *(far(v) for v in sources))


def input_back_body(gp_ref, full_ref, x_ref, grad_resid_ref, small_ref, grad_x_ref):
    small = small_ref[...].astype(F32)
    grad_n1 = dot_nt(gp_ref[0], full_ref[0])
    for s in range(1, 3):
        grad_n1 = grad_n1 + dot_nt(gp_ref[s], full_ref[s])
    unit1, inv1 = unit_of(x_ref[0].astype(F32))
    b = grad_n1 * small[8:9, :]
    grad_x = grad_resid_ref[...] + inv1 * (
        b
        - jnp.mean(b, axis=-1, keepdims=True)
        - unit1 * jnp.mean(b * unit1, axis=-1, keepdims=True)
    )
    grad_x_ref[0] = grad_x.astype(BF)


def input_back(gp, full, x, grad_resid, small):
    _, width = grad_resid.shape
    return pl.pallas_call(
        input_back_body,
        out_shape=pltpu.HBM(x.shape, BF),
        in_specs=vmem(5),
        out_specs=vmem(1)[0],
        compiler_params=params(20),
        cost_estimate=SMALL,
        name="input_back",
    )(far(gp), far(full), far(x), far(grad_resid), small)


def result_body(out_ref, index_ref, resid_ref, result_ref):
    total = resid_ref[...]
    count = total.shape[0]
    index = index_ref[...]
    for e in range(EXPERTS):
        row = iota((ROWS, count), 0) + e * ROWS
        pick = (row == index[0:1, :]) | (row == index[1:2, :])
        total = total + dot_tn(jnp.where(pick, 1.0, 0.0).astype(BF), out_ref[e])
    result_ref[0] = total.astype(BF)


def combine(out, index, resid):
    count, width = resid.shape
    return pl.pallas_call(
        result_body,
        out_shape=jax.ShapeDtypeStruct((1, count, width), BF),
        in_specs=vmem(3),
        out_specs=vmem(1)[0],
        compiler_params=params(8),
        cost_estimate=SMALL,
        name="combine",
    )(far(out), index, far(resid))


def plain(body, outs, *operands):
    return pl.pallas_call(
        body,
        out_shape=tuple(outs) if len(outs) > 1 else outs[0],
        in_specs=vmem(len(operands)),
        out_specs=tuple(vmem(len(outs))) if len(outs) > 1 else vmem(1)[0],
        compiler_params=params(16),
        cost_estimate=SMALL,
        name=body.__name__,
    )(*operands)


def first_sums(stay0_ref, come0_ref, stay1_ref, come1_ref, keep_ref, go0_ref, go1_ref):
    for half, (stay, come, go) in enumerate(
        ((stay0_ref, come0_ref, go0_ref), (stay1_ref, come1_ref, go1_ref))
    ):
        keep_ref[half] = (stay[0].astype(F32) + come[0].astype(F32)).astype(BF)
        go[...] = (stay[1].astype(F32) + come[1].astype(F32)).astype(BF)


def second_sums(keep_ref, come0_ref, come1_ref, sum_ref):
    for half, come in enumerate((come0_ref, come1_ref)):
        sum_ref[half] = (keep_ref[half].astype(F32) + come[...].astype(F32)).astype(BF)


def pair_sum(a_ref, b_ref, sum_ref):
    sum_ref[...] = (a_ref[...].astype(F32) + b_ref[...].astype(F32)).astype(BF)


def line_sum(parts_ref, tall_ref, small_ref):
    total = parts_ref[0].astype(F32)
    for i in range(1, parts_ref.shape[0]):
        total = total + parts_ref[i].astype(F32)
    rows = tall_ref.shape[0] * tall_ref.shape[1]
    for p in range(tall_ref.shape[0]):
        short = tall_ref.shape[1]
        tall_ref[p] = total[p * short : (p + 1) * short].astype(BF)
    small_ref[...] = total[rows:].astype(BF)


def plane_sum(parts_ref, small_ref, shares_ref):
    total = parts_ref[0].astype(F32)
    for i in range(1, parts_ref.shape[0]):
        total = total + parts_ref[i].astype(F32)
    short = total.shape[0]
    for r in range(shares_ref.shape[0]):
        shares_ref[r, 0:short, :] = total.astype(BF)
        shares_ref[r, short:, :] = small_ref[...]


def widen_body(places, aliased, where_ref, *refs):
    n = len(places)
    taken, wide, sem_in, sem_out = refs[-4:]
    outs = refs[-6:-4]
    srcs = refs[: len(refs) - 6 - 2 * aliased]
    _, depth, cols = srcs[0].shape[-3:]
    pieces = [ref.at[half] for ref in srcs for half in range(2)] if len(srcs) < n else srcs
    fetch = [pltpu.make_async_copy(pieces[i], taken.at[i], sem_in.at[i]) for i in range(n)]
    for copy in fetch:
        copy.start()
    sent = []
    for i, (other, k, half) in enumerate(places):
        fetch[i].wait()
        row = pl.multiple_of((where_ref[1] ^ k) * depth, depth)
        for which in range(2):
            wide[i, which] = taken[i, which].astype(F32)
            spot = outs[which].at[
                where_ref[0] ^ other, pl.ds(row, depth), half * cols : (half + 1) * cols
            ]
            copy = pltpu.make_async_copy(wide.at[i, which], spot, sem_out.at[i, which])
            copy.start()
            sent.append(copy)
    for copy in sent:
        copy.wait()


def widen(where, places, sources, shape, so_far=None):
    n = len(places)
    part = sources[0].shape[-3:]
    aliased = so_far is not None
    held = pl.BlockSpec(memory_space=pltpu.HBM)
    operands = [far(source) for source in sources] + (list(so_far) if aliased else [])
    return pl.pallas_call(
        lambda *refs: widen_body(places, aliased, *refs),
        out_shape=(pltpu.HBM(shape, F32), pltpu.HBM(shape, F32)),
        in_specs=[pl.BlockSpec(memory_space=pltpu.SMEM)] + [held] * len(operands),
        out_specs=(held, held),
        scratch_shapes=[
            pltpu.VMEM((n, *part), BF),
            pltpu.VMEM((n, *part), F32),
            pltpu.SemaphoreType.DMA((n,)),
            pltpu.SemaphoreType.DMA((n, 2)),
        ],
        input_output_aliases={len(sources) + 1: 0, len(sources) + 2: 1} if aliased else {},
        compiler_params=params(24),
        cost_estimate=SMALL,
        name="widen",
    )(where, *operands)


def finish_body(rows, parts_ref, qkv_ref, out_ref, router_ref, gains_ref):
    reps = parts_ref.shape[0]
    depth = out_ref.shape[0]
    for r in range(reps):
        for s in range(3):
            qkv_ref[s, r * rows : (r + 1) * rows, :] = parts_ref[
                r, s * rows : (s + 1) * rows, :
            ].astype(F32)
        out_ref[r * rows : (r + 1) * rows, :] = parts_ref[r, 3 * rows : 4 * rows, :].astype(F32)
    smalls = []
    for half in range(2):
        total = jnp.zeros((8, depth), F32)
        for peer in range(reps // 2):
            total = total + parts_ref[2 * peer + half].astype(F32)[4 * rows :, 0:depth]
        smalls.append(total)
    router_ref[...] = smalls[0]
    gains_ref[...] = smalls[1][0:2]


def finish(parts, rows):
    reps, _, width = parts.shape
    depth = rows * reps
    return pl.pallas_call(
        lambda *refs: finish_body(rows, *refs),
        out_shape=(
            jax.ShapeDtypeStruct((3, depth, width), F32),
            jax.ShapeDtypeStruct((depth, width), F32),
            jax.ShapeDtypeStruct((EXPERTS, depth), F32),
            jax.ShapeDtypeStruct((2, depth), F32),
        ),
        in_specs=vmem(1),
        out_specs=tuple(vmem(4)),
        compiler_params=params(4),
        name="finish",
    )(parts)


def shards(reps, shards_n, *args):
    tokens, segments, choices, priority, cotangent = args[:5]
    qkv_weights, out_weight, router_weight, gains, w_in, w_out = args[5:]
    rep, shard = lax.axis_index("rep"), lax.axis_index("shard")
    width, hidden = w_in.shape[1:]
    owned = w_in.shape[0]
    peers = reps // owned
    depth = width // shards_n
    fast = depth % (16 * reps) == 0 and depth == 128 and owned == 2 and peers == 4
    if not fast and owned != 1:
        raise NotImplementedError("mesh")
    column = [
        [(c * owned + e % owned) * shards_n + e // owned for e in range(EXPERTS)]
        for c in range(peers)
    ]

    def to_experts(rows):
        return lax.all_to_all(rows, AXES, 0, 0, axis_index_groups=column, tiled=True)

    where = jnp.stack([rep % owned, rep // owned]).astype(jnp.int32)
    index, cot_sent = route(choices[0].T, priority, cotangent)
    if fast:
        smalls, pieces, lines = gather_weights(
            rep, shard, reps, shards_n, qkv_weights, out_weight, router_weight.T, gains
        )
        place = jnp.stack([rep, shard]).astype(jnp.int32)
        weights_in = (qkv_weights, out_weight, smalls)
    else:
        place, pieces, lines = None, [], []
        weights_in = (
            lax.all_gather(qkv_weights, "shard", axis=1, tiled=True),
            lax.all_gather(out_weight, "shard", axis=0, tiled=True),
            lax.all_gather(router_weight, "shard", axis=0, tiled=True).T,
            lax.all_gather(gains, "shard", axis=1, tiled=True),
        )
    cot_in = to_experts(after(cot_sent, *lines))
    sent, small, gates, *kept = forward(
        fast, place, tokens, segments, index, weights_in, pieces
    )
    n2_in = to_experts(sent)

    def peer(value, k):
        return lax.ppermute(value, "rep", [(i, i ^ k) for i in range(reps)])

    through = cot_hidden(where, cot_in, w_out)
    back, out, *parts_in = experts(where, n2_in, cot_in, through, w_in, w_out)
    grads = expert_grads(where, fast, *parts_in)
    back_in = to_experts(back)
    out_in = to_experts(after(out, back_in))
    if fast:
        axes = ((owned, 2 * owned), (2 * owned, owned))
        halves = [peer(grads[2 * half], axes[half][0]) for half in range(2)]
        back_in = after(back_in, *grads)
    full, weights, proj, mixed, resid = kept
    grad_resid, grad_mixed, grad_out_w, early_sums = tokens_back(
        back_in, cotangent, index, small, gates, full, mixed, resid
    )
    if fast:
        grad_mixed, *halves = lax.optimization_barrier((grad_mixed, *halves))
        part = halves[0].shape[1:]
        small_part = jax.ShapeDtypeStruct(part, BF)
        keep, *leaves = plain(
            first_sums,
            [jax.ShapeDtypeStruct((2, *part), BF), small_part, small_part],
            grads[1],
            halves[0],
            grads[3],
            halves[1],
        )
        arrived = [peer(leaves[half], axes[half][1]) for half in range(2)]
        grad_mixed = after(grad_mixed, keep)
    grad_proj, *packs = backward(
        fast,
        reps,
        shards_n,
        where,
        grad_mixed,
        small,
        early_sums,
        proj,
        weights,
        full,
        tokens,
        grad_out_w,
    )
    grad_tokens = input_back(grad_proj, full, tokens, grad_resid, small)
    result = combine(out_in, index, kept[4])
    if fast:
        mine, twin, *arrived = lax.optimization_barrier((*packs, *arrived))
        total = plain(second_sums, [jax.ShapeDtypeStruct(keep.shape, BF)], keep, *arrived)
        twin = after(twin, total)
        chip = plain(pair_sum, [jax.ShapeDtypeStruct(mine.shape, BF)], mine, peer(twin, 1))
        line = lax.all_to_all(after(chip, out_in), "shard", 0, 0, tiled=True)
        short = 2 * depth // peers
        line, own_small = plain(
            line_sum,
            [
                jax.ShapeDtypeStruct((peers, short, width), BF),
                jax.ShapeDtypeStruct((8, width), BF),
            ],
            line,
        )
        early = [total] + [peer(total, k * owned) for k in (1, 2)]
        grad_tokens, *early = lax.optimization_barrier((grad_tokens, *early))
        late = [
            peer(early[axes[half][0] // owned][half], 3 * owned - axes[half][0]) for half in range(2)
        ]
        early += [peer(value, 1) for value in early]
        shape = (owned, width, hidden)
        places = [(other, k, half) for other in range(2) for k in range(3) for half in range(2)]
        so_far = widen(where, places, early, shape)
        plane_groups = [[p * owned + c for p in range(peers)] for c in range(owned)]
        plane = lax.all_to_all(line, "rep", 0, 0, axis_index_groups=plane_groups, tiled=True)
        plane, *so_far = lax.optimization_barrier((plane, *so_far))
        share = plain(
            plane_sum, [jax.ShapeDtypeStruct((reps, short + 8, width), BF)], plane, own_small
        )
        share, *late = lax.optimization_barrier((share, *late))
        late += [peer(value, 1) for value in late]
        parts = lax.all_to_all(share, "rep", 0, 0, tiled=True)
        places = [(other, 3, half) for other in range(2) for half in range(2)]
        grad_w_in, grad_w_out = widen(where, places, late, shape, so_far)
        parts = after(parts, grad_w_in, result)
        grad_qkv, grad_out, grad_router, grad_gains = finish(parts, depth // reps)
        grad_router = grad_router.T
    else:
        share = lax.psum_scatter(grads[0], "rep", scatter_dimension=1, tiled=True)
        every = lax.all_gather(share, "rep", axis=1, tiled=True).astype(F32)
        grad_w_in, grad_w_out = every[0:1], every[1:2]
        pack, sums = packs
        owned_rows = lax.psum_scatter(pack, "shard", scatter_dimension=1, tiled=True)
        owned_rows = lax.psum(owned_rows, "rep").astype(F32)
        grad_qkv, grad_out = owned_rows[0:3], owned_rows[3]
        sums = lax.psum(sums, AXES)
        mine = lax.dynamic_slice_in_dim(sums, shard * depth, depth, axis=1)
        grad_router, grad_gains = mine[0:EXPERTS].T, mine[EXPERTS : EXPERTS + 2]
    return (
        result,
        grad_tokens,
        grad_qkv,
        grad_out,
        grad_router,
        grad_gains,
        grad_w_in,
        grad_w_out,
    )


def solution(mesh):
    reps, shards_n = mesh.shape["rep"], mesh.shape["shard"]
    rows = P(("rep", "shard"), None, None)
    flat = P(("rep", "shard"), None)
    first = P("shard", None)
    stack = P("shard", None, None)
    second = P(None, "shard", None)
    return jax.shard_map(
        lambda *args: shards(reps, shards_n, *args),
        mesh=mesh,
        in_specs=(
            rows, flat, rows, flat, rows, second, first, first, P(None, "shard"), stack, stack,
        ),
        out_specs=(rows, rows, second, first, first, P(None, "shard"), stack, stack),
        check_vma=False,
    )
```

```python
import jax
import jax.numpy as jnp
from jax import lax
from jax.experimental import pallas as pl
from jax.experimental.pallas import tpu as pltpu
from jax.sharding import PartitionSpec as P

HEADS = 8
HEAD_DIM = 64
EXPERTS = 8
CAPACITY = 135
ROWS = 136
EPS = 1e-06
F32 = jnp.float32
BF = jnp.bfloat16
AXES = ("rep", "shard")
FF_STEP = 512
KEPT = 5
SMALL = pl.CostEstimate(flops=1000, bytes_accessed=1000, transcendentals=0)
GELU_A = 0.7978845608028654
GELU_B = 0.044715


def dot_nn(a, b):
    return lax.dot_general(a, b, (((1,), (0,)), ((), ())), preferred_element_type=F32)


def dot_nt(a, b):
    return lax.dot_general(a, b, (((1,), (1,)), ((), ())), preferred_element_type=F32)


def dot_tn(a, b):
    return lax.dot_general(a, b, (((0,), (0,)), ((), ())), preferred_element_type=F32)


def after(value, *others):
    return lax.optimization_barrier((value, *others))[0]


def iota(shape, dim):
    return lax.broadcasted_iota(jnp.int32, shape, dim)


def unit_of(values):
    mean = jnp.mean(values, axis=-1, keepdims=True)
    centered = values - mean
    inv = lax.rsqrt(jnp.mean(centered * centered, axis=-1, keepdims=True) + EPS)
    return centered * inv, inv


def split3(values):
    high = values.astype(BF)
    rest = values - high.astype(F32)
    mid = rest.astype(BF)
    low = (rest - mid.astype(F32)).astype(BF)
    return high, mid, low


def piece_rows(values):
    high, mid, low = split3(values)
    shape = (8, values.shape[1])
    row = iota(shape, 0)
    parts = [jnp.broadcast_to(part.astype(F32), shape) for part in (high, mid, low)]
    return jnp.where(
        row == 0, parts[0], jnp.where(row == 1, parts[1], jnp.where(row == 2, parts[2], 0.0))
    )


def side_row(pieces, width):
    wide = jnp.concatenate([pieces, jnp.zeros((8, width - ROWS), F32)], axis=1)
    row = iota((8, width), 0)
    moved = jnp.where(
        row == 0,
        wide,
        jnp.where(row == 1, pltpu.roll(wide, ROWS, 1), pltpu.roll(wide, 2 * ROWS, 1)),
    )
    return jnp.sum(jnp.where(row < 3, moved, 0.0), axis=0, keepdims=True)


def side_parts(side):
    width = side.shape[1]
    wide = jnp.broadcast_to(side, (8, width))
    row = iota((8, width), 0)
    back = jnp.where(
        row == 0,
        wide,
        jnp.where(row == 1, pltpu.roll(wide, width - ROWS, 1), pltpu.roll(wide, width - 2 * ROWS, 1)),
    )
    return jnp.where(row < 3, back, 0.0)[:, 0:ROWS]


def far(value):
    return pltpu.with_memory_space_constraint(value, pltpu.HBM)


def near(value):
    return pltpu.with_memory_space_constraint(value, pltpu.VMEM)


def vmem(n):
    return [pl.BlockSpec(memory_space=pltpu.VMEM)] * n


def params(mib):
    return pltpu.CompilerParams(vmem_limit_bytes=mib << 20)


def route_body(choice_ref, prio_ref, cot_ref, index_ref, sent_ref):
    count = cot_ref.shape[-2]
    choice = choice_ref[...]
    experts = iota((EXPERTS, count), 0)
    first = jnp.where(choice[0:1, :] == experts, 1.0, 0.0)
    second = jnp.where(choice[1:2, :] == experts, 1.0, 0.0)
    order = jnp.where(iota((count, count), 0) == prio_ref[...], 1.0, 0.0).astype(BF)
    earlier = jnp.where(iota((count, count), 0) < iota((count, count), 1), 1.0, 0.0).astype(BF)
    both = jnp.concatenate([first, second], axis=0).astype(BF)
    before = dot_nn(dot_nt(both, order).astype(BF), earlier)
    held = jnp.sum(first, axis=1, keepdims=True)
    before = jnp.concatenate([before[0:EXPERTS], before[EXPERTS:] + held], axis=0)
    before = dot_nn(jnp.minimum(before, 255.0).astype(BF), order)
    slot0 = jnp.sum(first * before[0:EXPERTS], axis=0, keepdims=True)
    slot1 = jnp.sum(second * before[EXPERTS:], axis=0, keepdims=True)
    slot = jnp.concatenate([slot0, slot1], axis=0).astype(jnp.int32)
    index = jnp.where(slot < CAPACITY, choice * ROWS + slot, -1)
    index_ref[...] = index
    cot = cot_ref[0]
    for e in range(EXPERTS):
        row = iota((ROWS, count), 0) + e * ROWS
        pick = (row == index[0:1, :]) | (row == index[1:2, :])
        sent_ref[e] = dot_nn(jnp.where(pick, 1.0, 0.0).astype(BF), cot).astype(BF)


def route(choice_t, prio, cot):
    _, count, width = cot.shape
    return pl.pallas_call(
        route_body,
        out_shape=(
            jax.ShapeDtypeStruct((2, count), jnp.int32),
            pltpu.HBM((EXPERTS, ROWS, width), BF),
        ),
        in_specs=vmem(3),
        out_specs=tuple(vmem(2)),
        compiler_params=params(12),
        cost_estimate=SMALL,
        name="route",
    )(far(choice_t), far(prio), far(cot))


def pack_body(where_ref, qkv_ref, out_ref, router_ref, gains_ref, pack_ref):
    rows = pack_ref.shape[1]
    start = pl.multiple_of(where_ref[0] * rows, rows)
    for s in range(3):
        pack_ref[s] = qkv_ref[s, pl.ds(start, rows), :]
    pack_ref[3] = out_ref[pl.ds(start, rows), :]
    depth = router_ref.shape[1]
    small = jnp.concatenate(
        [router_ref[...].astype(F32), gains_ref[...].astype(F32), jnp.zeros((6, depth), F32)],
        axis=0,
    )
    pack_ref[4, :, 0:depth] = small.astype(BF)
    pack_ref[4, :, depth:] = jnp.zeros((rows, pack_ref.shape[2] - depth), BF)


def pack_weights(rep, qkv, out, router, gains, rows):
    width = out.shape[1]
    return pl.pallas_call(
        pack_body,
        out_shape=jax.ShapeDtypeStruct((5, rows, width), BF),
        in_specs=[pl.BlockSpec(memory_space=pltpu.SMEM)] + vmem(4),
        out_specs=vmem(1)[0],
        compiler_params=params(4),
        name="pack_weights",
    )(rep.reshape(1), far(qkv), far(out), far(router), far(gains))


def gather_weights(rep, shard, reps, shards_n, qkv, out, router, gains):
    rows = qkv.shape[1] // reps
    pack = pack_weights(rep, qkv, out, router, gains, rows)
    lines = [
        lax.ppermute(pack, "shard", [(i, i ^ dz) for i in range(shards_n)])
        for dz in range(1, shards_n)
    ]
    block = jnp.stack([piece[0:4] for piece in lines])
    smalls = jnp.stack([piece[4] for piece in [pack] + lines])
    spread = [block] + [
        lax.ppermute(block, "rep", [(i, i ^ k) for i in range(reps)]) for k in range(2, reps, 2)
    ]
    twin = [lax.ppermute(piece, "rep", [(i, i ^ 1) for i in range(reps)]) for piece in spread]
    pieces = []
    for own, other in zip(spread, twin, strict=True):
        pieces += [own, other]
    return smalls, pieces, lines


def fill_weights(rep, shard, qkv_ref, out_ref, smalls_ref, piece_refs, full_ref, small_ref):
    depth = out_ref.shape[0]
    own = pl.multiple_of(shard * depth, depth)
    for s in range(3):
        full_ref[s, pl.ds(own, depth), :] = qkv_ref[s]
    full_ref[3, pl.ds(own, depth), :] = out_ref[...]
    small_ref[:, pl.ds(own, depth)] = smalls_ref[0, :, 0:depth]
    for far in range(1, smalls_ref.shape[0]):
        base = pl.multiple_of((shard ^ far) * depth, depth)
        small_ref[:, pl.ds(base, depth)] = smalls_ref[far, :, 0:depth]
        for k, piece in enumerate(piece_refs):
            rows = piece.shape[2]
            start = pl.multiple_of(base + (rep ^ k) * rows, rows)
            for s in range(4):
                full_ref[s, pl.ds(start, rows), :] = piece[far - 1, s]


def head_masks(count):
    lane = iota((count, 2 * HEAD_DIM), 1)
    return [lane < HEAD_DIM, lane >= HEAD_DIM]


def kept_shapes(count, width):
    return (
        ((4, width, width), BF),
        ((HEADS, count, count), BF),
        ((3, count, width), BF),
        ((count, width), BF),
        ((count, width), F32),
    )


def kept_copies(sources, targets, sem):
    copies = {
        i: pltpu.make_async_copy(sources[i], targets[i], sem.at[i]) for i in range(KEPT) if i != 1
    }
    for pair in range(HEADS // 2):
        heads = pl.ds(2 * pair, 2)
        copies[1, pair] = pltpu.make_async_copy(
            sources[1].at[heads], targets[1].at[heads], sem.at[KEPT + pair]
        )
    return copies


def forward_body(fast, n_pieces, *refs):
    if fast:
        where_ref, x_ref, seg_ref, index_ref, qkv_ref, out_ref, smalls_ref = refs[:7]
        piece_refs = refs[7 : 7 + n_pieces]
        refs = refs[7 + n_pieces :]
    else:
        x_ref, seg_ref, index_ref, qkv_ref, out_ref, router_ref, gains_ref = refs[:7]
        refs = refs[7:]
    sent_ref, small_ref, gate_ref, *kept = refs[: 3 + KEPT]
    full_ref, weights_ref, proj_ref, mixed_ref, resid_ref = held = refs[3 + KEPT : -1]
    copies = kept_copies(held, kept, refs[-1])
    if fast:
        fill_weights(
            where_ref[0], where_ref[1], qkv_ref, out_ref, smalls_ref, piece_refs, full_ref, small_ref
        )
    else:
        full_ref[0:3] = qkv_ref[...]
        full_ref[3] = out_ref[...]
        small_ref[...] = jnp.concatenate(
            [
                router_ref[...].astype(F32),
                gains_ref[...].astype(F32),
                jnp.zeros((6, out_ref.shape[1]), F32),
            ],
            axis=0,
        ).astype(BF)
    copies[0].start()
    x = x_ref[0].astype(F32)
    count, width = x.shape
    small = small_ref[...].astype(F32)
    unit1, _ = unit_of(x)
    n1 = (unit1 * small[8:9, :]).astype(BF)
    for s in range(3):
        proj_ref[s] = dot_nn(n1, full_ref[s]).astype(BF)
    copies[2].start()
    document = jnp.where(iota((8, count), 0) == seg_ref[...], 1.0, 0.0).astype(BF)
    bias = jnp.where(dot_tn(document, document) > 0.5, 0.0, -1e30)
    masks = head_masks(count)
    for pair in range(HEADS // 2):
        lanes = slice(pair * 2 * HEAD_DIM, (pair + 1) * 2 * HEAD_DIM)
        q, k, v = proj_ref[0, :, lanes], proj_ref[1, :, lanes], proj_ref[2, :, lanes]
        q = q * BF(HEAD_DIM**-0.5)
        halves = []
        for half in range(2):
            scores = dot_nt(k, jnp.where(masks[half], q, BF(0))) + bias
            top = jnp.max(scores, axis=0, keepdims=True)
            terms = jnp.exp(scores - top)
            total = jnp.sum(terms, axis=0, keepdims=True)
            weights = (terms * (1.0 / total)).astype(BF)
            weights_ref[2 * pair + half] = weights
            halves.append(dot_tn(weights, v))
        copies[1, pair].start()
        mixed_ref[:, lanes] = jnp.where(masks[0], halves[0], halves[1]).astype(BF)
    copies[3].start()
    resid = x + dot_nn(mixed_ref[...], full_ref[3])
    resid_ref[...] = resid
    copies[4].start()
    unit2, _ = unit_of(resid)
    n2 = (unit2 * small[9:10, :]).astype(BF)
    logits = dot_nt(small_ref[...], n2)[0:EXPERTS]
    terms = jnp.exp(logits - jnp.max(logits, axis=0, keepdims=True))
    gates = terms / jnp.sum(terms, axis=0, keepdims=True)
    gate_ref[...] = gates
    index = index_ref[...]
    for e in range(EXPERTS):
        row = iota((ROWS, count), 0) + e * ROWS
        pick = (row == index[0:1, :]) | (row == index[1:2, :])
        pick = jnp.where(pick, 1.0, 0.0).astype(BF)
        rows = dot_nn(pick, n2)
        side = side_row(dot_nt(piece_rows(gates[e : e + 1, :]).astype(BF), pick), width)
        last = iota((ROWS, 1), 0) == CAPACITY
        sent_ref[e] = jnp.where(last, side, rows).astype(BF)
    for copy in copies.values():
        copy.wait()


def forward(fast, where, x, seg, index, weights_in, pieces):
    _, count, width = x.shape
    body = lambda *refs: forward_body(fast, len(pieces), *refs)
    operands = [far(x), far(seg), index, *(far(w) for w in weights_in[:2]), *weights_in[2:], *pieces]
    specs = vmem(len(operands))
    if fast:
        operands = [where] + operands
        specs = [pl.BlockSpec(memory_space=pltpu.SMEM)] + specs
    shown = (
        pltpu.HBM((EXPERTS, ROWS, width), BF),
        jax.ShapeDtypeStruct((16, width), BF),
        jax.ShapeDtypeStruct((EXPERTS, count), F32),
    )
    kept = kept_shapes(count, width)
    return pl.pallas_call(
        body,
        out_shape=(*shown, *(pltpu.HBM(*k) for k in kept)),
        in_specs=specs,
        out_specs=(*vmem(3), *([pl.BlockSpec(memory_space=pltpu.HBM)] * KEPT)),
        scratch_shapes=[
            *(pltpu.VMEM(*k) for k in kept),
            pltpu.SemaphoreType.DMA((KEPT + HEADS // 2,)),
        ],
        compiler_params=params(40),
        cost_estimate=SMALL,
        name="forward",
    )(*operands)


def cot_hidden_body(where_ref, cot_ref, w_out_ref, through_ref):
    rows = jnp.concatenate([cot_ref[g].astype(F32) for g in range(2)], axis=0).astype(BF)
    for start in range(0, w_out_ref.shape[2], FF_STEP):
        cols = slice(start, start + FF_STEP)
        through_ref[:, cols] = dot_nn(rows, w_out_ref[0, :, cols])


def cot_hidden(where, cot, w_out):
    groups, _, width = cot.shape
    hidden_n = w_out.shape[2]
    return pl.pallas_call(
        cot_hidden_body,
        out_shape=pltpu.HBM((groups * ROWS, hidden_n), F32),
        grid_spec=pltpu.PrefetchScalarGridSpec(
            num_scalar_prefetch=1,
            grid=(groups // 2,),
            in_specs=[
                pl.BlockSpec((2, ROWS, width), lambda i, w: (i, 0, 0)),
                pl.BlockSpec((1, width, hidden_n), lambda i, w: (w[0], 0, 0)),
            ],
            out_specs=pl.BlockSpec((2 * ROWS, hidden_n), lambda i, w: (i, 0)),
        ),
        compiler_params=params(24),
        cost_estimate=SMALL,
        name="cot_hidden",
    )(where, cot, far(w_out))


def experts_body(where_ref, *refs):
    n2_ref, cot_ref, through_ref, w_in_ref, w_out_ref = refs[:5]
    back_ref, out_ref, hidden_ref, pre_ref, gso_ref = refs[5:]
    eye = jnp.where(iota((ROWS, ROWS), 0) == iota((ROWS, ROWS), 1), 1.0, 0.0).astype(BF)
    lane = iota((ROWS, 8), 1)
    gates = []
    for g in range(2):
        last = (g + 1) * ROWS - 1
        start = last // 16 * 16
        eight = n2_ref[start : start + 16, :].astype(F32)
        parts = side_parts(eight[last - start : last - start + 1]).astype(BF)
        gates.append(jnp.sum(dot_nt(eye, parts), axis=1, keepdims=True))
    gate_col = jnp.concatenate(gates, axis=0)
    rows = n2_ref[...]
    gso_ref[...] = (gate_col * cot_ref[...].astype(F32)).astype(BF)
    for start in range(0, w_in_ref.shape[2], FF_STEP):
        cols = slice(start, start + FF_STEP)
        u = dot_nn(rows, w_in_ref[0, :, cols])
        square = u * u
        t = jnp.tanh(u * (GELU_A + (GELU_A * GELU_B) * square))
        half = 0.5 + 0.5 * t
        hidden = u * half
        slope = half + hidden * ((1.0 - t) * (GELU_A + (3.0 * GELU_A * GELU_B) * square))
        hidden_ref[:, cols] = hidden.astype(BF)
        pre_ref[:, cols] = (through_ref[:, cols] * (gate_col * slope)).astype(BF)
    grad_in = dot_nt(pre_ref[...], w_in_ref[0])
    result = dot_nt(hidden_ref[...], w_out_ref[0])
    out = (gate_col * result).astype(BF)
    out_ref[...] = out
    inner_all = jnp.sum(out.astype(F32) * cot_ref[...].astype(F32), axis=1, keepdims=True)
    row = iota((2 * ROWS, 1), 0)
    back = grad_in
    for g in range(2):
        inner = inner_all[g * ROWS : (g + 1) * ROWS]
        high, mid, low = (piece.astype(F32) for piece in split3(inner))
        pieces = jnp.where(lane == 0, high, jnp.where(lane == 1, mid, jnp.where(lane == 2, low, 0.0)))
        side = side_row(dot_tn(pieces.astype(BF), eye), out.shape[1])
        back = jnp.where(row == (g + 1) * ROWS - 1, side, back)
    back_ref[...] = back.astype(BF)


def experts(where, n2, cot, through, w_in, w_out):
    groups, _, width = n2.shape
    hidden_n = w_in.shape[2]
    total = groups * ROWS
    weight = pl.BlockSpec((1, width, hidden_n), lambda i, w: (w[0], 0, 0))
    narrow = pl.BlockSpec((2 * ROWS, width), lambda i, w: (i, 0))
    wide = pl.BlockSpec((2 * ROWS, hidden_n), lambda i, w: (i, 0))
    n2, cot = n2.reshape(total, width), cot.reshape(total, width)
    back, out, hidden, pre, gso = pl.pallas_call(
        experts_body,
        out_shape=[
            pltpu.HBM((total, width), BF),
            pltpu.HBM((total, width), BF),
            pltpu.HBM((total, hidden_n), BF),
            pltpu.HBM((total, hidden_n), BF),
            pltpu.HBM((total, width), BF),
        ],
        grid_spec=pltpu.PrefetchScalarGridSpec(
            num_scalar_prefetch=1,
            grid=(groups // 2,),
            in_specs=[narrow, narrow, wide, weight, weight],
            out_specs=[narrow, narrow, wide, wide, narrow],
        ),
        compiler_params=params(44),
        cost_estimate=SMALL,
        name="experts",
    )(where, n2, cot, through, far(w_in), far(w_out))
    shape = (groups, ROWS, width)
    return back.reshape(shape), out.reshape(shape), hidden, pre, n2, gso


def expert_grads_body(split, where_ref, hidden_ref, pre_ref, rows_ref, gso_ref, *refs):
    grad_refs, sum_ref = refs[:-1], refs[-1]
    step, steps = pl.program_id(0), pl.num_programs(0)
    for half, (left, right) in enumerate(((rows_ref, pre_ref), (gso_ref, hidden_ref))):
        grad = dot_tn(left[...], right[...]).astype(BF)
        if not split:
            grad_refs[0][half] = grad
            continue
        sum_ref[half] = grad
    if not split:
        return
    depth = sum_ref.shape[1] // 4
    for late in range(2):

        @pl.when((step < steps // 2) if late == 0 else (step >= steps // 2))
        def _(late=late):
            for half in range(2):
                for k in range(4):
                    start = pl.multiple_of((where_ref[1] ^ k) * depth, depth)
                    goes = k == 3 or k == 1 + late
                    ref = grad_refs[2 * late + (0 if goes else 1)]
                    ref[int(k == 3 or k == 2 - late), half] = sum_ref[half, pl.ds(start, depth), :]


def expert_grads(where, split, hidden, pre, rows, gso):
    total, width = rows.shape
    hidden_n = hidden.shape[1]
    steps = hidden_n // FF_STEP
    narrow = pl.BlockSpec((total, width), lambda i, w: (0, 0))
    wide = pl.BlockSpec((total, FF_STEP), lambda i, w: (0, i))
    if split:
        part = (2, 2, width // 4, FF_STEP)
        first = pl.BlockSpec(part, lambda i, w: (0, 0, 0, jnp.minimum(i, steps // 2 - 1)))
        second = pl.BlockSpec(part, lambda i, w: (0, 0, 0, jnp.maximum(i - steps // 2, 0)))
        grad_specs = [first, first, second, second]
        grad_shapes = [jax.ShapeDtypeStruct((2, 2, width // 4, hidden_n // 2), BF)] * 4
    else:
        grad_specs = [pl.BlockSpec((2, width, FF_STEP), lambda i, w: (0, 0, i))]
        grad_shapes = [pltpu.HBM((2, width, hidden_n), BF)]
    return pl.pallas_call(
        lambda *refs: expert_grads_body(split, *refs),
        out_shape=grad_shapes,
        grid_spec=pltpu.PrefetchScalarGridSpec(
            num_scalar_prefetch=1,
            grid=(steps,),
            in_specs=[wide, wide, narrow, narrow],
            out_specs=grad_specs,
            scratch_shapes=[pltpu.VMEM((2, width, FF_STEP), BF)],
        ),
        compiler_params=params(30),
        cost_estimate=SMALL,
        name="expert_grads",
    )(where, far(hidden), far(pre), far(rows), far(gso))


def place_grads(fast, reps, shards_n, pack_ref, which, grad):
    if not fast:
        pack_ref[which] = grad.astype(BF)
        return
    width = grad.shape[0]
    depth = width // shards_n
    rows = depth // reps
    grad = grad.astype(BF)
    for z in range(shards_n):
        for r in range(reps):
            start = z * depth + r * rows
            spot = ((r // 2) * 4 + which) * rows
            pack_ref[r % 2, z, spot : spot + rows, :] = grad[start : start + rows]


def tokens_back_body(back_ref, cot_ref, index_ref, small_ref, gate_ref, *refs):
    full_far, mixed_far, resid_far, grad_resid_ref, grad_mixed_ref, grad_out_ref, sums_ref = refs[:7]
    out_weight_ref, mixed_ref, resid_ref, sem = refs[7:]
    fetch = [
        pltpu.make_async_copy(source, target, sem.at[i])
        for i, (source, target) in enumerate(
            ((resid_far, resid_ref), (full_far.at[3], out_weight_ref), (mixed_far, mixed_ref))
        )
    ]
    for copy in fetch:
        copy.start()
    count, width = resid_ref.shape
    small = small_ref[...].astype(F32)
    index = index_ref[...]
    gates = gate_ref[...]
    grad_n2 = jnp.zeros((count, width), F32)
    rows_h = []
    for e in range(EXPERTS):
        row = iota((ROWS, count), 0) + e * ROWS
        pick = (row == index[0:1, :]) | (row == index[1:2, :])
        pick = jnp.where(pick, 1.0, 0.0).astype(BF)
        back = back_ref[e]
        side = side_parts(back.astype(F32)[CAPACITY : CAPACITY + 1]).astype(BF)
        rows_h.append(jnp.sum(dot_nn(side, pick), axis=0, keepdims=True))
        grad_n2 = grad_n2 + dot_tn(pick, back)
    inner = jnp.concatenate(rows_h, axis=0)
    grad_logits = (inner - gates * jnp.sum(inner, axis=0, keepdims=True)).astype(BF)
    wide_logits = jnp.concatenate(
        [grad_logits.astype(F32), jnp.zeros((8, count), F32)], axis=0
    ).astype(BF)
    grad_n2 = grad_n2 + dot_tn(wide_logits, small_ref[...])
    fetch[0].wait()
    unit2, inv2 = unit_of(resid_ref[...])
    n2 = (unit2 * small[9:10, :]).astype(BF)
    grad_router = dot_nn(wide_logits, n2)[0:EXPERTS]
    grad_gain2 = jnp.sum(grad_n2 * unit2, axis=0, keepdims=True)
    sums_ref[...] = jnp.concatenate(
        [grad_router, jnp.zeros((1, width), F32), grad_gain2, jnp.zeros((6, width), F32)], axis=0
    )
    a = grad_n2 * small[9:10, :]
    grad_resid = cot_ref[0].astype(F32) + inv2 * (
        a
        - jnp.mean(a, axis=-1, keepdims=True)
        - unit2 * jnp.mean(a * unit2, axis=-1, keepdims=True)
    )
    grad_resid_ref[...] = grad_resid
    branch = grad_resid.astype(BF)
    fetch[1].wait()
    grad_mixed_ref[...] = dot_nt(branch, out_weight_ref[...]).astype(BF)
    fetch[2].wait()
    grad_out_ref[...] = dot_tn(mixed_ref[...], branch).astype(BF)


def tokens_back(back, cot, index, small, gates, full, mixed, resid):
    count, width = resid.shape
    held = pl.BlockSpec(memory_space=pltpu.HBM)
    outs = (
        ((count, width), F32),
        ((count, width), BF),
        ((width, width), BF),
        ((16, width), F32),
    )
    return pl.pallas_call(
        tokens_back_body,
        out_shape=tuple(pltpu.HBM(*o) for o in outs),
        in_specs=vmem(5) + [held] * 3,
        out_specs=tuple(vmem(4)),
        scratch_shapes=[
            pltpu.VMEM((width, width), BF),
            pltpu.VMEM((count, width), BF),
            pltpu.VMEM((count, width), F32),
            pltpu.SemaphoreType.DMA((3,)),
        ],
        compiler_params=params(24),
        cost_estimate=SMALL,
        name="tokens_back",
    )(back, far(cot), index, small, gates, far(full), far(mixed), far(resid))


def backward_body(fast, reps, shards_n, where_ref, *refs):
    core = where_ref[0]
    grad_mixed_ref, small_ref, early_ref = refs[:3]
    sources = refs[3:8]
    if fast:
        gp_far, mine_ref, twin_ref, pack_ref = refs[8:12]
        refs = refs[12:]
    else:
        gp_far, pack_ref, sums_ref = refs[8:11]
        refs = refs[11:]
    gp_ref, proj_ref, weights_ref, full_ref, x_ref, grad_out_ref = refs[:-1]
    held, sem = refs[1:-1], refs[-1]
    pairs = HEADS // 2
    copies = {
        i: pltpu.make_async_copy(sources[i], held[i], sem.at[i]) for i in range(5) if i != 1
    }
    for pair in range(pairs):
        heads = pl.ds(2 * pair, 2)
        copies[1, pair] = pltpu.make_async_copy(
            sources[1].at[heads], weights_ref.at[heads], sem.at[5 + pair]
        )
    for which in (0, *((1, pair) for pair in range(pairs)), 3, 2, 4):
        copies[which].start()
    count, width = grad_mixed_ref.shape
    small = small_ref[...].astype(F32)
    masks = head_masks(count)
    factor = HEAD_DIM**-0.5
    copies[0].wait()
    for pair in range(pairs):
        lanes = slice(pair * 2 * HEAD_DIM, (pair + 1) * 2 * HEAD_DIM)
        q, k, v = proj_ref[0, :, lanes], proj_ref[1, :, lanes], proj_ref[2, :, lanes]
        gm = grad_mixed_ref[:, lanes]
        copies[1, pair].wait()
        parts = []
        for half in range(2):
            weights = weights_ref[2 * pair + half]
            probs = weights.astype(F32)
            grad_probs = dot_nt(v, jnp.where(masks[half], gm, BF(0)))
            total = jnp.sum(probs * grad_probs, axis=0, keepdims=True)
            grad_scores = (probs * (grad_probs - total)).astype(BF)
            parts.append(
                (dot_tn(grad_scores, k), dot_nn(grad_scores, q), dot_nn(weights, gm))
            )
        for s in range(3):
            both = jnp.where(masks[0], parts[0][s], parts[1][s])
            gp_ref[s, :, lanes] = (both * factor if s < 2 else both).astype(BF)
    gp_send = pltpu.make_async_copy(gp_ref, gp_far, sem.at[5 + pairs])
    gp_send.start()
    copies[3].wait()
    unit1, _ = unit_of(x_ref[0].astype(F32))
    n1 = (unit1 * small[8:9, :]).astype(BF)
    copies[2].wait()
    product = jnp.zeros((width, width), F32)
    for s in range(3):
        grad = dot_tn(n1, gp_ref[s])
        place_grads(fast, reps, shards_n, pack_ref, s, grad)
        product = product + full_ref[s].astype(F32) * grad
    copies[4].wait()
    place_grads(fast, reps, shards_n, pack_ref, 3, grad_out_ref[...])
    ones = jnp.ones((8, width), BF)
    high = product.astype(BF)
    low = (product - high.astype(F32)).astype(BF)
    grad_gain1 = (dot_nt(ones, high) + dot_nt(ones, low))[0:1] / small[8:9, :]
    sums = jnp.where(iota((16, width), 0) == 8, grad_gain1, early_ref[...])
    sends = [gp_send]
    if fast:
        depth = width // shards_n
        rows = depth // reps
        for z in range(shards_n):
            for half in range(2):
                eight = sums[8 * half : 8 * half + 8, z * depth : (z + 1) * depth]
                eight = jnp.concatenate([eight, jnp.zeros((8, width - depth), F32)], axis=1)
                pack_ref[half, z, 2 * reps * rows :, :] = eight.astype(BF)
        for i in range(2):
            send = pltpu.make_async_copy(pack_ref.at[core ^ i], (mine_ref, twin_ref)[i], sem.at[i])
            send.start()
            sends.append(send)
    else:
        sums_ref[...] = sums
    for send in sends:
        send.wait()


def backward(fast, reps, shards_n, where, grad_mixed, small, early, proj, weights, full, x, grad_out):
    _, count, width = x.shape
    sources = (proj, weights, full, x, grad_out)
    held = pl.BlockSpec(memory_space=pltpu.HBM)
    outs = [pltpu.HBM((3, count, width), BF)]
    scratch = [pltpu.VMEM((3, count, width), BF)]
    if fast:
        part = (shards_n, 2 * reps * (width // shards_n // reps) + 8, width)
        outs += [pltpu.VMEM(part, BF), pltpu.HBM(part, BF)]
        out_specs = [held, *vmem(1), held]
        scratch = [pltpu.VMEM((2, *part), BF)] + scratch
    else:
        outs += [
            jax.ShapeDtypeStruct((4, width, width), BF),
            jax.ShapeDtypeStruct((16, width), F32),
        ]
        out_specs = [held] + vmem(2)
    return pl.pallas_call(
        lambda *refs: backward_body(fast, reps, shards_n, *refs),
        out_shape=tuple(outs),
        in_specs=[pl.BlockSpec(memory_space=pltpu.SMEM)] + vmem(3) + [held] * 5,
        out_specs=tuple(out_specs),
        scratch_shapes=[
            *scratch,
            *(pltpu.VMEM(v.shape, v.dtype) for v in sources),
            pltpu.SemaphoreType.DMA((6 + HEADS // 2,)),
        ],
        compiler_params=params(40),
        cost_estimate=SMALL,
        name="backward",
    )(where, grad_mixed, small, early, *(far(v) for v in sources))


def input_back_body(gp_ref, full_ref, x_ref, grad_resid_ref, small_ref, grad_x_ref):
    small = small_ref[...].astype(F32)
    grad_n1 = dot_nt(gp_ref[0], full_ref[0])
    for s in range(1, 3):
        grad_n1 = grad_n1 + dot_nt(gp_ref[s], full_ref[s])
    unit1, inv1 = unit_of(x_ref[0].astype(F32))
    b = grad_n1 * small[8:9, :]
    grad_x = grad_resid_ref[...] + inv1 * (
        b
        - jnp.mean(b, axis=-1, keepdims=True)
        - unit1 * jnp.mean(b * unit1, axis=-1, keepdims=True)
    )
    grad_x_ref[0] = grad_x.astype(BF)


def input_back(gp, full, x, grad_resid, small):
    _, width = grad_resid.shape
    return pl.pallas_call(
        input_back_body,
        out_shape=pltpu.HBM(x.shape, BF),
        in_specs=vmem(5),
        out_specs=vmem(1)[0],
        compiler_params=params(20),
        cost_estimate=SMALL,
        name="input_back",
    )(far(gp), far(full), far(x), far(grad_resid), small)


def result_body(out_ref, index_ref, resid_ref, result_ref):
    total = resid_ref[...]
    count = total.shape[0]
    index = index_ref[...]
    for e in range(EXPERTS):
        row = iota((ROWS, count), 0) + e * ROWS
        pick = (row == index[0:1, :]) | (row == index[1:2, :])
        total = total + dot_tn(jnp.where(pick, 1.0, 0.0).astype(BF), out_ref[e])
    result_ref[0] = total.astype(BF)


def combine(out, index, resid):
    count, width = resid.shape
    return pl.pallas_call(
        result_body,
        out_shape=jax.ShapeDtypeStruct((1, count, width), BF),
        in_specs=vmem(3),
        out_specs=vmem(1)[0],
        compiler_params=params(8),
        cost_estimate=SMALL,
        name="combine",
    )(far(out), index, far(resid))


def plain(body, outs, *operands):
    return pl.pallas_call(
        body,
        out_shape=tuple(outs) if len(outs) > 1 else outs[0],
        in_specs=vmem(len(operands)),
        out_specs=tuple(vmem(len(outs))) if len(outs) > 1 else vmem(1)[0],
        compiler_params=params(16),
        cost_estimate=SMALL,
        name=body.__name__,
    )(*operands)


def first_sums(stay0_ref, come0_ref, stay1_ref, come1_ref, keep_ref, go0_ref, go1_ref):
    for half, (stay, come, go) in enumerate(
        ((stay0_ref, come0_ref, go0_ref), (stay1_ref, come1_ref, go1_ref))
    ):
        keep_ref[half] = (stay[0].astype(F32) + come[0].astype(F32)).astype(BF)
        go[...] = (stay[1].astype(F32) + come[1].astype(F32)).astype(BF)


def second_sums(keep_ref, come0_ref, come1_ref, sum_ref):
    for half, come in enumerate((come0_ref, come1_ref)):
        sum_ref[half] = (keep_ref[half].astype(F32) + come[...].astype(F32)).astype(BF)


def pair_sum(a_ref, b_ref, sum_ref):
    sum_ref[...] = (a_ref[...].astype(F32) + b_ref[...].astype(F32)).astype(BF)


def line_sum(parts_ref, tall_ref, small_ref):
    total = parts_ref[0].astype(F32)
    for i in range(1, parts_ref.shape[0]):
        total = total + parts_ref[i].astype(F32)
    rows = tall_ref.shape[0] * tall_ref.shape[1]
    for p in range(tall_ref.shape[0]):
        short = tall_ref.shape[1]
        tall_ref[p] = total[p * short : (p + 1) * short].astype(BF)
    small_ref[...] = total[rows:].astype(BF)


def plane_sum(parts_ref, small_ref, shares_ref):
    total = parts_ref[0].astype(F32)
    for i in range(1, parts_ref.shape[0]):
        total = total + parts_ref[i].astype(F32)
    short = total.shape[0]
    for r in range(shares_ref.shape[0]):
        shares_ref[r, 0:short, :] = total.astype(BF)
        shares_ref[r, short:, :] = small_ref[...]


def widen_body(places, aliased, where_ref, *refs):
    n = len(places)
    taken, wide, sem_in, sem_out = refs[-4:]
    outs = refs[-6:-4]
    srcs = refs[: len(refs) - 6 - 2 * aliased]
    _, depth, cols = srcs[0].shape[-3:]
    pieces = [ref.at[half] for ref in srcs for half in range(2)] if len(srcs) < n else srcs
    fetch = [pltpu.make_async_copy(pieces[i], taken.at[i], sem_in.at[i]) for i in range(n)]
    for copy in fetch:
        copy.start()
    sent = []
    for i, (other, k, half) in enumerate(places):
        fetch[i].wait()
        row = pl.multiple_of((where_ref[1] ^ k) * depth, depth)
        for which in range(2):
            wide[i, which] = taken[i, which].astype(F32)
            spot = outs[which].at[
                where_ref[0] ^ other, pl.ds(row, depth), half * cols : (half + 1) * cols
            ]
            copy = pltpu.make_async_copy(wide.at[i, which], spot, sem_out.at[i, which])
            copy.start()
            sent.append(copy)
    for copy in sent:
        copy.wait()


def widen(where, places, sources, shape, so_far=None):
    n = len(places)
    part = sources[0].shape[-3:]
    aliased = so_far is not None
    held = pl.BlockSpec(memory_space=pltpu.HBM)
    operands = [far(source) for source in sources] + (list(so_far) if aliased else [])
    return pl.pallas_call(
        lambda *refs: widen_body(places, aliased, *refs),
        out_shape=(pltpu.HBM(shape, F32), pltpu.HBM(shape, F32)),
        in_specs=[pl.BlockSpec(memory_space=pltpu.SMEM)] + [held] * len(operands),
        out_specs=(held, held),
        scratch_shapes=[
            pltpu.VMEM((n, *part), BF),
            pltpu.VMEM((n, *part), F32),
            pltpu.SemaphoreType.DMA((n,)),
            pltpu.SemaphoreType.DMA((n, 2)),
        ],
        input_output_aliases={len(sources) + 1: 0, len(sources) + 2: 1} if aliased else {},
        compiler_params=params(24),
        cost_estimate=SMALL,
        name="widen",
    )(where, *operands)


def finish_body(rows, parts_ref, qkv_ref, out_ref, router_ref, gains_ref):
    reps = parts_ref.shape[0]
    depth = out_ref.shape[0]
    for r in range(reps):
        for s in range(3):
            qkv_ref[s, r * rows : (r + 1) * rows, :] = parts_ref[
                r, s * rows : (s + 1) * rows, :
            ].astype(F32)
        out_ref[r * rows : (r + 1) * rows, :] = parts_ref[r, 3 * rows : 4 * rows, :].astype(F32)
    smalls = []
    for half in range(2):
        total = jnp.zeros((8, depth), F32)
        for peer in range(reps // 2):
            total = total + parts_ref[2 * peer + half].astype(F32)[4 * rows :, 0:depth]
        smalls.append(total)
    router_ref[...] = smalls[0]
    gains_ref[...] = smalls[1][0:2]


def finish(parts, rows):
    reps, _, width = parts.shape
    depth = rows * reps
    return pl.pallas_call(
        lambda *refs: finish_body(rows, *refs),
        out_shape=(
            jax.ShapeDtypeStruct((3, depth, width), F32),
            jax.ShapeDtypeStruct((depth, width), F32),
            jax.ShapeDtypeStruct((EXPERTS, depth), F32),
            jax.ShapeDtypeStruct((2, depth), F32),
        ),
        in_specs=vmem(1),
        out_specs=tuple(vmem(4)),
        compiler_params=params(4),
        name="finish",
    )(parts)


def shards(reps, shards_n, *args):
    tokens, segments, choices, priority, cotangent = args[:5]
    qkv_weights, out_weight, router_weight, gains, w_in, w_out = args[5:]
    rep, shard = lax.axis_index("rep"), lax.axis_index("shard")
    width, hidden = w_in.shape[1:]
    owned = w_in.shape[0]
    peers = reps // owned
    depth = width // shards_n
    fast = depth % (16 * reps) == 0 and depth == 128 and owned == 2 and peers == 4
    if not fast and owned != 1:
        raise NotImplementedError("mesh")
    column = [
        [(c * owned + e % owned) * shards_n + e // owned for e in range(EXPERTS)]
        for c in range(peers)
    ]

    def to_experts(rows):
        return lax.all_to_all(rows, AXES, 0, 0, axis_index_groups=column, tiled=True)

    where = jnp.stack([rep % owned, rep // owned]).astype(jnp.int32)
    index, cot_sent = route(choices[0].T, priority, cotangent)
    if fast:
        smalls, pieces, lines = gather_weights(
            rep, shard, reps, shards_n, qkv_weights, out_weight, router_weight.T, gains
        )
        place = jnp.stack([rep, shard]).astype(jnp.int32)
        weights_in = (qkv_weights, out_weight, smalls)
    else:
        place, pieces, lines = None, [], []
        weights_in = (
            lax.all_gather(qkv_weights, "shard", axis=1, tiled=True),
            lax.all_gather(out_weight, "shard", axis=0, tiled=True),
            lax.all_gather(router_weight, "shard", axis=0, tiled=True).T,
            lax.all_gather(gains, "shard", axis=1, tiled=True),
        )
    cot_in = to_experts(after(cot_sent, *lines))
    sent, small, gates, *kept = forward(
        fast, place, tokens, segments, index, weights_in, pieces
    )
    n2_in = to_experts(sent)

    def peer(value, k):
        return lax.ppermute(value, "rep", [(i, i ^ k) for i in range(reps)])

    through = cot_hidden(where, cot_in, w_out)
    back, out, *parts_in = experts(where, n2_in, cot_in, through, w_in, w_out)
    grads = expert_grads(where, fast, *parts_in)
    back_in = to_experts(back)
    out_in = to_experts(after(out, back_in))
    if fast:
        axes = ((owned, 2 * owned), (2 * owned, owned))
        halves = [peer(grads[2 * half], axes[half][0]) for half in range(2)]
        back_in = after(back_in, *grads)
    full, weights, proj, mixed, resid = kept
    grad_resid, grad_mixed, grad_out_w, early_sums = tokens_back(
        back_in, cotangent, index, small, gates, full, mixed, resid
    )
    if fast:
        grad_mixed, *halves = lax.optimization_barrier((grad_mixed, *halves))
        part = halves[0].shape[1:]
        small_part = jax.ShapeDtypeStruct(part, BF)
        keep, *leaves = plain(
            first_sums,
            [jax.ShapeDtypeStruct((2, *part), BF), small_part, small_part],
            grads[1],
            halves[0],
            grads[3],
            halves[1],
        )
        arrived = [peer(leaves[half], axes[half][1]) for half in range(2)]
        grad_mixed = after(grad_mixed, keep)
    grad_proj, *packs = backward(
        fast,
        reps,
        shards_n,
        where,
        grad_mixed,
        small,
        early_sums,
        proj,
        weights,
        full,
        tokens,
        grad_out_w,
    )
    grad_tokens = input_back(grad_proj, full, tokens, grad_resid, small)
    result = combine(out_in, index, kept[4])
    if fast:
        mine, twin, *arrived = lax.optimization_barrier((*packs, *arrived))
        total = plain(second_sums, [jax.ShapeDtypeStruct(keep.shape, BF)], keep, *arrived)
        twin = after(twin, total)
        chip = plain(pair_sum, [jax.ShapeDtypeStruct(mine.shape, BF)], mine, peer(twin, 1))
        line = lax.all_to_all(after(chip, out_in), "shard", 0, 0, tiled=True)
        short = 2 * depth // peers
        line, own_small = plain(
            line_sum,
            [
                jax.ShapeDtypeStruct((peers, short, width), BF),
                jax.ShapeDtypeStruct((8, width), BF),
            ],
            line,
        )
        early = [total] + [peer(total, k * owned) for k in (1, 2)]
        grad_tokens, *early = lax.optimization_barrier((grad_tokens, *early))
        late = [
            peer(early[axes[half][0] // owned][half], 3 * owned - axes[half][0]) for half in range(2)
        ]
        early += [peer(value, 1) for value in early]
        shape = (owned, width, hidden)
        places = [(other, k, half) for other in range(2) for k in range(3) for half in range(2)]
        so_far = widen(where, places, early, shape)
        plane_groups = [[p * owned + c for p in range(peers)] for c in range(owned)]
        plane = lax.all_to_all(line, "rep", 0, 0, axis_index_groups=plane_groups, tiled=True)
        plane, *so_far = lax.optimization_barrier((plane, *so_far))
        share = plain(
            plane_sum, [jax.ShapeDtypeStruct((reps, short + 8, width), BF)], plane, own_small
        )
        share, *late = lax.optimization_barrier((share, *late))
        late += [peer(value, 1) for value in late]
        parts = lax.all_to_all(share, "rep", 0, 0, tiled=True)
        places = [(other, 3, half) for other in range(2) for half in range(2)]
        grad_w_in, grad_w_out = widen(where, places, late, shape, so_far)
        parts = after(parts, grad_w_in, result)
        grad_qkv, grad_out, grad_router, grad_gains = finish(parts, depth // reps)
        grad_router = grad_router.T
    else:
        share = lax.psum_scatter(grads[0], "rep", scatter_dimension=1, tiled=True)
        every = lax.all_gather(share, "rep", axis=1, tiled=True).astype(F32)
        grad_w_in, grad_w_out = every[0:1], every[1:2]
        pack, sums = packs
        owned_rows = lax.psum_scatter(pack, "shard", scatter_dimension=1, tiled=True)
        owned_rows = lax.psum(owned_rows, "rep").astype(F32)
        grad_qkv, grad_out = owned_rows[0:3], owned_rows[3]
        sums = lax.psum(sums, AXES)
        mine = lax.dynamic_slice_in_dim(sums, shard * depth, depth, axis=1)
        grad_router, grad_gains = mine[0:EXPERTS].T, mine[EXPERTS : EXPERTS + 2]
    return (
        result,
        grad_tokens,
        grad_qkv,
        grad_out,
        grad_router,
        grad_gains,
        grad_w_in,
        grad_w_out,
    )


def solution(mesh):
    reps, shards_n = mesh.shape["rep"], mesh.shape["shard"]
    rows = P(("rep", "shard"), None, None)
    flat = P(("rep", "shard"), None)
    first = P("shard", None)
    stack = P("shard", None, None)
    second = P(None, "shard", None)
    return jax.shard_map(
        lambda *args: shards(reps, shards_n, *args),
        mesh=mesh,
        in_specs=(
            rows, flat, rows, flat, rows, second, first, first, P(None, "shard"), stack, stack,
        ),
        out_specs=(rows, rows, second, first, first, P(None, "shard"), stack, stack),
        check_vma=False,
    )
```
